256 devices in a mesh: wide: 128 (over x, y, z_lo, core), head: 2 (over z_hi).
Axes of the slice: x: 4, y: 4, z: 8 (z_hi: 2, z_lo: 4; z = z_hi * 4 + z_lo), core: 2. Of those that a mesh axis runs over, the one named last changes fastest.
Arguments:
- branch_query: bfloat16 [512, 8192], P('wide', 'head'), may hold values from -6 to 6
- key_new: bfloat16 [512, 1024], P('wide', 'head'), may hold values from -6 to 6
- value_new: bfloat16 [512, 1024], P('wide', 'head'), may hold values from -6 to 6
- pool_pages: bfloat16 [2, 8192, 16, 1024], P(None, 'wide', None, 'head'), may hold values from -6 to 6
- page_table: int32 [512, 16], P('wide'), may hold values from 0 to 63, as said below
- tail_length: int32 [512], P('wide'), may hold values from 1 to 256
- parent_row: int32 [512], P('wide'), may hold values from 0 to 511, as said below
- residual: bfloat16 [512, 8192], P(('wide', 'head')), may hold values from -6 to 6
- norm_gain: float32 [8192], replicated, may hold values from 0.5 to 1.5
- gate_blocks: bfloat16 [128, 32, 128, 128], P('wide'), may hold values from -0.09375 to 0.09375
- up_blocks: bfloat16 [128, 32, 128, 128], P('wide'), may hold values from -0.09375 to 0.09375
- gate_up_keep: int32 [128, 32], P('wide'), may hold values from 0 to 63, as said below
- gate_scale: float32 [128, 32], P('wide'), may hold values from 0.5 to 2
- up_scale: float32 [128, 32], P('wide'), may hold values from 0.5 to 2
- down_blocks: bfloat16 [128, 32, 128, 128], P('wide'), may hold values from -0.0625 to 0.0625
- down_keep: int32 [128, 32], P('wide'), may hold values from 0 to 63, as said below
- down_scale: float32 [128, 32], P('wide'), may hold values from 0.5 to 2
Outputs:
- layer_out: bfloat16 [512, 8192], P(('wide', 'head'))
The draws below stay inside these ranges and needn't reach their ends.
Inputs may be any that keep to these rules, and one draw needn't show every extreme that they name: parent_row never falls with the branch index, and parent_row[b] <= b and parent_row[b] > b - 4. `page_table`: the entries of the 4 rows held by one index of wide name each of that index's 64 pages once. `gate_up_keep`: each row names 32 different blocks. `down_keep`: each row names 32 different blocks.
All inputs are finite; a program needn't handle non-finite values.
Results may differ from the reference program's by a relative error of at most 0.017.
Values may be sent and summed in bfloat16 or wider, within the bound.
A program may use at most 64 MiB of HBM per device.

```python
import math
import jax
import jax.numpy as jnp
from jax import lax

D = 8192
QH = 64
KVH = 8
HD = 128
FF = 16384
BLK = 128
KEEP = 32
PAGE = 16
TPAGES = 16
ROW_DEV = 4
ROWS = 512
TAIL = 256
POOL_DEV = 64
POOL = 8192
NBD = 64
NCB = 128


def base_normal(key, shape):
    return jnp.clip(jax.random.normal(key, shape, jnp.float32), -6.0, 6.0)


def draw_branch_query(key, part):
    sub_key = jax.random.fold_in(key, 31)
    base = base_normal(sub_key, (ROWS, QH, HD))
    return base.reshape(ROWS, QH * HD).astype(jnp.bfloat16)


def draw_key_new(key, part):
    sub_key = jax.random.fold_in(key, 32)
    base = base_normal(sub_key, (ROWS, KVH, HD))
    return base.reshape(ROWS, KVH * HD).astype(jnp.bfloat16)


def draw_pool_pages(key, part):
    sub_key = jax.random.fold_in(key, 33)
    base = base_normal(sub_key, (2, POOL, PAGE, KVH, HD))
    return base.reshape(2, POOL, PAGE, KVH * HD).astype(jnp.bfloat16)


def draw_residual(key, part):
    sub_key = jax.random.fold_in(key, 34)
    base = base_normal(sub_key, (ROWS, D))
    row_scale = jnp.exp(jax.random.uniform(jax.random.fold_in(key, 35), (ROWS, 1), jnp.float32, math.log(0.03), math.log(0.3)))
    col_scale = jnp.exp(jax.random.uniform(jax.random.fold_in(key, 36), (1, D), jnp.float32, math.log(0.3), math.log(3.0)))
    return (base * row_scale * col_scale).astype(jnp.bfloat16)


def draw_page_table(key, part):
    keys_all = jax.random.split(jax.random.fold_in(key, 13), ROWS // ROW_DEV)
    perms = jax.vmap(lambda one_key: jax.random.permutation(one_key, POOL_DEV))(keys_all)
    return perms.reshape(ROWS, TPAGES).astype(jnp.int32)


def draw_tail_length(key, part):
    lengths = jax.random.randint(jax.random.fold_in(key, 14), (ROWS,), 1, TAIL + 1, jnp.int32)
    lengths = lengths.at[::ROW_DEV].set(TAIL)
    lengths = lengths.at[1].set(1)
    return lengths


def draw_parent_row(key, part):
    delta = jax.random.randint(jax.random.fold_in(key, 15), (ROWS,), 0, ROW_DEV, jnp.int32)
    row_ids = jnp.arange(ROWS, dtype=jnp.int32)
    first_rows = (row_ids % ROW_DEV == 0) & (row_ids > 0)
    delta = jnp.where(first_rows, jnp.maximum(delta, 1), delta)
    candidate = jnp.maximum(row_ids - delta, 0)
    candidate = candidate.at[ROWS - 1].set(ROWS - 1)
    return lax.cummax(candidate, axis=0).astype(jnp.int32)


def keep_lists(key):
    keys_all = jax.random.split(key, NCB)
    perms = jax.vmap(lambda one_key: jax.random.permutation(one_key, NBD))(keys_all)
    return perms[:, :KEEP].astype(jnp.int32)


def draw_gate_up_keep(key, part):
    return keep_lists(jax.random.fold_in(key, 11))


def draw_down_keep(key, part):
    return keep_lists(jax.random.fold_in(key, 12))


def block_scale(stream_key, extent, cuts, smallest, high):
    factor_of, own = 1.0, jax.random.fold_in(stream_key, 6)
    for dim, shards_of in cuts:
        heights = jnp.exp(jax.random.uniform(jax.random.fold_in(own, dim), (shards_of,), jnp.float32, smallest / len(cuts), high / len(cuts)))
        factor_of = factor_of * jnp.repeat(heights, extent[dim] // shards_of).reshape([-1 if axis == dim else 1 for axis in range(len(extent))])
    return factor_of


def centred(key, shape, scale, reach, shards=(), kind=jnp.bfloat16):
    values = scale * jax.random.normal(key, shape, jnp.float32)
    if shards:
        values = values * block_scale(key, shape, shards, -0.22, 0.18)
    return jnp.clip(values, -reach, reach).astype(kind)


def setup_inputs(seed: int = 0) -> dict:
    seeds = jax.random.split(jax.random.key(seed), 18)
    return {
        "branch_query": draw_branch_query(jax.random.fold_in(seeds[17], 71), 0),
        "key_new": draw_key_new(jax.random.fold_in(seeds[17], 71), 0),
        "value_new": centred(seeds[2], (ROWS, KVH * HD), 1.0, 6.0, ((0, 128), (1, 2))),
        "pool_pages": draw_pool_pages(jax.random.fold_in(seeds[17], 71), 0),
        "page_table": draw_page_table(jax.random.fold_in(seeds[17], 71), 0),
        "tail_length": draw_tail_length(jax.random.fold_in(seeds[17], 71), 0),
        "parent_row": draw_parent_row(jax.random.fold_in(seeds[17], 71), 0),
        "residual": draw_residual(jax.random.fold_in(seeds[17], 71), 0),
        "norm_gain": jnp.clip(1.0 + 0.1 * jax.random.normal(seeds[8], (D,), jnp.float32), 0.5, 1.5),
        "gate_blocks": centred(seeds[9], (NCB, KEEP, BLK, BLK), (KEEP * BLK) ** -0.5, 0.09375, ((0, 128),)),
        "up_blocks": centred(seeds[10], (NCB, KEEP, BLK, BLK), (KEEP * BLK) ** -0.5, 0.09375, ((0, 128),)),
        "gate_up_keep": draw_gate_up_keep(jax.random.fold_in(seeds[17], 71), 0),
        "gate_scale": jnp.clip(jnp.exp(math.log(2.0) - 1.3862944 * jax.random.uniform(seeds[12], (NCB, KEEP), jnp.float32) ** block_scale(seeds[12], (NCB, KEEP), ((0, 128),), -0.2, 0.2)), 0.5, 2.0),
        "up_scale": jnp.clip(jnp.exp(math.log(2.0) - 1.3862944 * jax.random.uniform(seeds[13], (NCB, KEEP), jnp.float32) ** block_scale(seeds[13], (NCB, KEEP), ((0, 128),), -0.2, 0.2)), 0.5, 2.0),
        "down_blocks": centred(seeds[14], (NCB, KEEP, BLK, BLK), (FF // 2) ** -0.5, 0.0625, ((0, 128),)),
        "down_keep": draw_down_keep(jax.random.fold_in(seeds[17], 71), 0),
        "down_scale": jnp.clip(jnp.exp(math.log(2.0) - 1.3862944 * jax.random.uniform(seeds[16], (NCB, KEEP), jnp.float32) ** block_scale(seeds[16], (NCB, KEEP), ((0, 128),), -0.2, 0.2)), 0.5, 2.0),
    }


def reference(branch_query, key_new, value_new, pool_pages, page_table, tail_length, parent_row, residual, norm_gain, gate_blocks, up_blocks, gate_up_keep, gate_scale, up_scale, down_blocks, down_keep, down_scale):
    per_group = QH // KVH
    factor = 1.0 / math.sqrt(HD)
    pool_keys = pool_pages[0]
    pool_values = pool_pages[1]
    highest_prec = lax.Precision.HIGHEST

    def one_branch(branch):
        parent_index = parent_row[branch]
        owner = parent_index // ROW_DEV
        pages = (owner * POOL_DEV + page_table[parent_index]).astype(jnp.int32)
        tail_keys = pool_keys[pages].reshape(TAIL, KVH, HD)
        tail_values = pool_values[pages].reshape(TAIL, KVH, HD)
        keys_all = jnp.concatenate([tail_keys, key_new[branch].reshape(1, KVH, HD)], axis=0).astype(jnp.float32)
        values_all = jnp.concatenate([tail_values, value_new[branch].reshape(1, KVH, HD)], axis=0).astype(jnp.float32)
        queries = branch_query[branch].reshape(KVH, per_group, HD).astype(jnp.float32)
        scores = jnp.einsum('gjd,tgd->gjt', queries, keys_all, precision=highest_prec) * factor
        length = tail_length[parent_index]
        live_mask = jnp.concatenate([jnp.arange(TAIL, dtype=jnp.int32) < length, jnp.ones((1,), dtype=bool)])
        top_score = lax.optimization_barrier(jnp.max(jnp.where(live_mask, scores, -1e+30), axis=-1))
        expo = jnp.where(live_mask, jnp.exp(scores - top_score[..., None]), 0.0)
        weights_all = (expo / lax.optimization_barrier(jnp.sum(expo, axis=-1))[..., None]).astype(jnp.bfloat16)
        mixture = jnp.einsum('gjt,tgd->gjd', weights_all.astype(jnp.float32), values_all, precision=highest_prec)
        return mixture.reshape(QH * HD).astype(jnp.bfloat16)
    attention = lax.map(one_branch, jnp.arange(ROWS, dtype=jnp.int32))
    middle = residual.astype(jnp.float32) + attention.astype(jnp.float32)
    normed = (middle * lax.rsqrt(lax.optimization_barrier(jnp.mean(middle * middle, axis=-1, keepdims=True)) + 1e-05) * norm_gain).astype(jnp.bfloat16)
    blocks = normed.reshape(ROWS, NBD, BLK)

    def column_step(accum, pieces):
        gate_w, up_w, keep_rows, gate_s, up_s, down_w, keep_cols, down_s = pieces
        picked = blocks[:, keep_rows].astype(jnp.float32)
        gate_sum = lax.optimization_barrier(jnp.sum(jnp.einsum('rkd,kdf->rkf', picked, gate_w.astype(jnp.float32), precision=highest_prec) * gate_s[None, :, None], axis=1))
        up_sum = lax.optimization_barrier(jnp.sum(jnp.einsum('rkd,kdf->rkf', picked, up_w.astype(jnp.float32), precision=highest_prec) * up_s[None, :, None], axis=1))
        hidden = (jax.nn.silu(gate_sum) * up_sum).astype(jnp.bfloat16)
        contrib = jnp.einsum('rf,kfe->rke', hidden.astype(jnp.float32), down_w.astype(jnp.float32), precision=highest_prec) * down_s[None, :, None]
        return (accum.at[:, keep_cols].add(contrib), None)
    start_acc = jnp.zeros((ROWS, NBD, BLK), jnp.float32)
    ffn_acc, _ = lax.scan(column_step, start_acc, (gate_blocks, up_blocks, gate_up_keep, gate_scale, up_scale, down_blocks, down_keep, down_scale))
    ffn_sum = ffn_acc.reshape(ROWS, D)
    return (middle + ffn_sum).astype(jnp.bfloat16)
```

```python
import math

import jax
import jax.numpy as jnp
from jax import lax
from jax.sharding import PartitionSpec as P

HD = 128
BLK = 128


def shifted(block, axis, distance):
    devices = range(lax.axis_size(axis))
    route = [(i - distance, i) for i in devices if i - distance in devices]
    return lax.ppermute(block, axis, route)


def attend(branch_query, key_new, value_new, child_tails, child_length):
    row_count = branch_query.shape[0]
    groups = key_new.shape[1] // HD
    per_group = branch_query.shape[1] // (groups * HD)
    tail_size = child_tails.shape[2]
    queries = branch_query.reshape(row_count, groups, per_group, HD)
    tail_keys = child_tails[0].reshape(row_count, tail_size, groups, HD)
    tail_values = child_tails[1].reshape(row_count, tail_size, groups, HD)
    own_keys = key_new.reshape(row_count, groups, HD)
    own_values = value_new.reshape(row_count, groups, HD)
    factor = 1.0 / math.sqrt(HD)
    tail_scores = (
        jnp.einsum("rgjd,rtgd->rgjt", queries, tail_keys, preferred_element_type=jnp.float32)
        * factor
    )
    own_scores = (
        jnp.einsum("rgjd,rgd->rgj", queries, own_keys, preferred_element_type=jnp.float32) * factor
    )
    live_mask = (jnp.arange(tail_size, dtype=jnp.float32)[None, :] < child_length[:, None])[
        :, None, None, :
    ]
    top_score = jnp.maximum(jnp.max(jnp.where(live_mask, tail_scores, -1e30), axis=-1), own_scores)
    tail_exp = jnp.where(live_mask, jnp.exp(tail_scores - top_score[..., None]), 0.0)
    own_exp = jnp.exp(own_scores - top_score)
    totals = jnp.sum(tail_exp, axis=-1) + own_exp
    tail_weights = (tail_exp / totals[..., None]).astype(jnp.bfloat16)
    own_weights = (own_exp / totals).astype(jnp.bfloat16)
    mixture = jnp.einsum(
        "rgjt,rtgd->rgjd", tail_weights, tail_values, preferred_element_type=jnp.float32
    )
    mixture = mixture + own_weights[..., None].astype(jnp.float32) * own_values[
        :, :, None, :
    ].astype(jnp.float32)
    return mixture.reshape(row_count, -1).astype(jnp.bfloat16)


def ffn_terms(picked, gate_blocks, up_blocks, gate_scale, up_scale, down_blocks, down_scale):
    gate_part = jnp.einsum(
        "rkd,kdf->rkf", picked, gate_blocks[0], preferred_element_type=jnp.float32
    )
    up_part = jnp.einsum("rkd,kdf->rkf", picked, up_blocks[0], preferred_element_type=jnp.float32)
    gate_sum = jnp.sum(gate_part * gate_scale[0][None, :, None], axis=1)
    up_sum = jnp.sum(up_part * up_scale[0][None, :, None], axis=1)
    hidden = (jax.nn.silu(gate_sum) * up_sum).astype(jnp.bfloat16)
    return (
        jnp.einsum("rf,kfe->rke", hidden, down_blocks[0], preferred_element_type=jnp.float32)
        * down_scale[0][None, :, None]
    )


def per_device(
    branch_query,
    key_new,
    value_new,
    pool_pages,
    page_table,
    tail_length,
    parent_row,
    residual,
    norm_gain,
    gate_blocks,
    up_blocks,
    gate_up_keep,
    gate_scale,
    up_scale,
    down_blocks,
    down_keep,
    down_scale,
):
    row_count = branch_query.shape[0]
    tail_size = page_table.shape[1] * pool_pages.shape[2]
    own_tails = pool_pages[:, page_table].reshape(2, row_count, tail_size, pool_pages.shape[3])
    own_length = tail_length.astype(jnp.bfloat16)
    prior_tails, prior_length = shifted((own_tails, own_length), "wide", 1)
    both_tails = jnp.concatenate([prior_tails, own_tails], axis=1)
    both_length = jnp.concatenate([prior_length, own_length]).astype(jnp.float32)
    local_parent = parent_row - (lax.axis_index("wide") - 1) * row_count
    child_tails = both_tails[:, local_parent]
    child_length = both_length[local_parent]
    attention = attend(branch_query, key_new, value_new, child_tails, child_length)
    head_rows = lax.all_to_all(attention, "head", split_axis=0, concat_axis=1, tiled=True)
    middle = residual.astype(jnp.float32) + head_rows.astype(jnp.float32)
    normed = (
        middle * lax.rsqrt(jnp.mean(middle * middle, axis=-1, keepdims=True) + 1e-05) * norm_gain
    ).astype(jnp.bfloat16)
    keep_lists = lax.all_gather(
        jnp.concatenate([gate_up_keep, down_keep], axis=1), "wide", axis=0, tiled=True
    )
    keep = gate_up_keep.shape[1]
    in_keep, out_keep = keep_lists[:, :keep], keep_lists[:, keep:]
    feature_blocks = normed.shape[1] // BLK
    normed_blocks = normed.reshape(normed.shape[0], feature_blocks, BLK)
    outgoing = jnp.swapaxes(normed_blocks[:, in_keep], 0, 1)
    picked = lax.all_to_all(outgoing, "wide", split_axis=0, concat_axis=0, tiled=True)
    picked = picked.reshape(-1, keep, BLK)
    contrib = ffn_terms(
        picked, gate_blocks, up_blocks, gate_scale, up_scale, down_blocks, down_scale
    ).astype(jnp.bfloat16)
    contrib = contrib.reshape(-1, normed.shape[0], keep, BLK)
    arrived = lax.all_to_all(contrib, "wide", split_axis=0, concat_axis=0, tiled=True)
    senders = arrived.shape[0]
    placement = (
        out_keep.reshape(senders * keep, 1) == jnp.arange(feature_blocks, dtype=jnp.int32)[None, :]
    ).astype(jnp.bfloat16)
    flat = jnp.swapaxes(arrived, 0, 1).reshape(normed.shape[0], senders * keep, BLK)
    ffn_share = jnp.einsum(
        "rsd,sb->rbd", flat, placement, preferred_element_type=jnp.float32
    ).reshape(normed.shape[0], -1)
    return (middle + ffn_share).astype(jnp.bfloat16)


def solution(mesh):
    placed = (
        P("wide", "head"),
        P("wide", "head"),
        P("wide", "head"),
        P(None, "wide", None, "head"),
        P("wide", None),
        P("wide"),
        P("wide"),
        P(("wide", "head"), None),
        P(),
        P("wide", None, None, None),
        P("wide", None, None, None),
        P("wide", None),
        P("wide", None),
        P("wide", None),
        P("wide", None, None, None),
        P("wide", None),
        P("wide", None),
    )
    return jax.shard_map(
        per_device, mesh=mesh, in_specs=placed, out_specs=P(("wide", "head"), None), check_vma=False
    )
```

```python
import math

import jax
import jax.numpy as jnp
from jax import lax
from jax.sharding import PartitionSpec as P

HD = 128
BLK = 128


def shifted(block, axis, distance):
    devices = range(lax.axis_size(axis))
    route = [(i - distance, i) for i in devices if i - distance in devices]
    return lax.ppermute(block, axis, route)


def attend(branch_query, key_new, value_new, child_tails, child_length):
    row_count = branch_query.shape[0]
    groups = key_new.shape[1] // HD
    per_group = branch_query.shape[1] // (groups * HD)
    tail_size = child_tails.shape[2]
    queries = branch_query.reshape(row_count, groups, per_group, HD)
    tail_keys = child_tails[0].reshape(row_count, tail_size, groups, HD)
    tail_values = child_tails[1].reshape(row_count, tail_size, groups, HD)
    own_keys = key_new.reshape(row_count, groups, HD)
    own_values = value_new.reshape(row_count, groups, HD)
    factor = 1.0 / math.sqrt(HD)
    tail_scores = (
        jnp.einsum("rgjd,rtgd->rgjt", queries, tail_keys, preferred_element_type=jnp.float32)
        * factor
    )
    own_scores = (
        jnp.einsum("rgjd,rgd->rgj", queries, own_keys, preferred_element_type=jnp.float32) * factor
    )
    live_mask = (jnp.arange(tail_size, dtype=jnp.float32)[None, :] < child_length[:, None])[
        :, None, None, :
    ]
    top_score = jnp.maximum(jnp.max(jnp.where(live_mask, tail_scores, -1e30), axis=-1), own_scores)
    tail_exp = jnp.where(live_mask, jnp.exp(tail_scores - top_score[..., None]), 0.0)
    own_exp = jnp.exp(own_scores - top_score)
    totals = jnp.sum(tail_exp, axis=-1) + own_exp
    tail_weights = (tail_exp / totals[..., None]).astype(jnp.bfloat16)
    own_weights = (own_exp / totals).astype(jnp.bfloat16)
    mixture = jnp.einsum(
        "rgjt,rtgd->rgjd", tail_weights, tail_values, preferred_element_type=jnp.float32
    )
    mixture = mixture + own_weights[..., None].astype(jnp.float32) * own_values[
        :, :, None, :
    ].astype(jnp.float32)
    return mixture.reshape(row_count, -1).astype(jnp.bfloat16)


def ffn_terms(picked, gate_blocks, up_blocks, gate_scale, up_scale, down_blocks, down_scale):
    gate_part = jnp.einsum(
        "rkd,kdf->rkf", picked, gate_blocks[0], preferred_element_type=jnp.float32
    )
    up_part = jnp.einsum("rkd,kdf->rkf", picked, up_blocks[0], preferred_element_type=jnp.float32)
    gate_sum = jnp.sum(gate_part * gate_scale[0][None, :, None], axis=1)
    up_sum = jnp.sum(up_part * up_scale[0][None, :, None], axis=1)
    hidden = (jax.nn.silu(gate_sum) * up_sum).astype(jnp.bfloat16)
    return (
        jnp.einsum("rf,kfe->rke", hidden, down_blocks[0], preferred_element_type=jnp.float32)
        * down_scale[0][None, :, None]
    )


def per_device(
    branch_query,
    key_new,
    value_new,
    pool_pages,
    page_table,
    tail_length,
    parent_row,
    residual,
    norm_gain,
    gate_blocks,
    up_blocks,
    gate_up_keep,
    gate_scale,
    up_scale,
    down_blocks,
    down_keep,
    down_scale,
):
    row_count = branch_query.shape[0]
    tail_size = page_table.shape[1] * pool_pages.shape[2]
    own_tails = pool_pages[:, page_table].reshape(2, row_count, tail_size, pool_pages.shape[3])
    own_length = tail_length.astype(jnp.bfloat16)
    prior_tails, prior_length = shifted((own_tails, own_length), "wide", 1)
    both_tails = jnp.concatenate([prior_tails, own_tails], axis=1)
    both_length = jnp.concatenate([prior_length, own_length]).astype(jnp.float32)
    local_parent = parent_row - (lax.axis_index("wide") - 1) * row_count
    child_tails = both_tails[:, local_parent]
    child_length = both_length[local_parent]
    attention = attend(branch_query, key_new, value_new, child_tails, child_length)
    head_rows = lax.all_to_all(attention, "head", split_axis=0, concat_axis=1, tiled=True)
    middle = residual.astype(jnp.float32) + head_rows.astype(jnp.float32)
    normed = (
        middle * lax.rsqrt(jnp.mean(middle * middle, axis=-1, keepdims=True) + 1e-05) * norm_gain
    ).astype(jnp.bfloat16)
    peers = lax.axis_size("wide")
    own_lists = jnp.concatenate([gate_up_keep, down_keep], axis=1)
    keep_lists = lax.all_to_all(
        jnp.broadcast_to(own_lists, (peers, own_lists.shape[1])),
        "wide",
        split_axis=0,
        concat_axis=0,
        tiled=True,
    )
    keep = gate_up_keep.shape[1]
    in_keep, out_keep = keep_lists[:, :keep], keep_lists[:, keep:]
    feature_blocks = normed.shape[1] // BLK
    blocks = jnp.arange(feature_blocks, dtype=jnp.int32)
    choose = (in_keep.reshape(peers * keep, 1) == blocks[None, :]).astype(jnp.bfloat16)
    normed_blocks = normed.reshape(normed.shape[0], feature_blocks, BLK)
    outgoing = jnp.einsum(
        "sb,rbd->srd", choose, normed_blocks, preferred_element_type=jnp.float32
    ).astype(jnp.bfloat16)
    outgoing = outgoing.reshape(peers, keep, normed.shape[0], BLK)
    picked = lax.all_to_all(outgoing, "wide", split_axis=0, concat_axis=0, tiled=True)
    picked = jnp.swapaxes(picked, 1, 2).reshape(-1, keep, BLK)
    contrib = ffn_terms(
        picked, gate_blocks, up_blocks, gate_scale, up_scale, down_blocks, down_scale
    ).astype(jnp.bfloat16)
    contrib = contrib.reshape(-1, normed.shape[0], keep, BLK)
    arrived = lax.all_to_all(contrib, "wide", split_axis=0, concat_axis=0, tiled=True)
    senders = arrived.shape[0]
    placement = (
        out_keep.reshape(senders * keep, 1) == jnp.arange(feature_blocks, dtype=jnp.int32)[None, :]
    ).astype(jnp.bfloat16)
    flat = jnp.swapaxes(arrived, 0, 1).reshape(normed.shape[0], senders * keep, BLK)
    ffn_share = jnp.einsum(
        "rsd,sb->rbd", flat, placement, preferred_element_type=jnp.float32
    ).reshape(normed.shape[0], -1)
    return (middle + ffn_share).astype(jnp.bfloat16)


def solution(mesh):
    placed = (
        P("wide", "head"),
        P("wide", "head"),
        P("wide", "head"),
        P(None, "wide", None, "head"),
        P("wide", None),
        P("wide"),
        P("wide"),
        P(("wide", "head"), None),
        P(),
        P("wide", None, None, None),
        P("wide", None, None, None),
        P("wide", None),
        P("wide", None),
        P("wide", None),
        P("wide", None, None, None),
        P("wide", None),
        P("wide", None),
    )
    return jax.shard_map(
        per_device, mesh=mesh, in_specs=placed, out_specs=P(("wide", "head"), None), check_vma=False
    )
```

```python
import functools
import math

import jax
import jax.numpy as jnp
from jax import lax
from jax.experimental import pallas as pl
from jax.experimental.pallas import tpu as pltpu
from jax.sharding import PartitionSpec as P

HD = 128
BLK = 128


def exchange_kernel(axis, x_ref, y_ref, send_sem, recv_sem, local_sem):
    me = lax.axis_index(axis)
    n = x_ref.shape[0]
    local = pltpu.make_async_copy(x_ref.at[me], y_ref.at[me], local_sem)
    local.start()

    def send(j, carry):
        peer = lax.rem(me + j, n)
        pltpu.make_async_remote_copy(
            src_ref=x_ref.at[peer],
            dst_ref=y_ref.at[me],
            send_sem=send_sem,
            recv_sem=recv_sem,
            device_id={axis: peer},
            device_id_type=pl.DeviceIdType.MESH,
        ).start()
        return carry

    lax.fori_loop(1, n, send, 0)
    every = pltpu.make_async_remote_copy(
        src_ref=x_ref.at[pl.ds(0, n - 1)],
        dst_ref=y_ref.at[pl.ds(0, n - 1)],
        send_sem=send_sem,
        recv_sem=recv_sem,
        device_id={axis: me},
        device_id_type=pl.DeviceIdType.MESH,
    )
    every.wait_send()
    every.wait_recv()
    local.wait()


def exchange(x, axis):
    return pl.pallas_call(
        functools.partial(exchange_kernel, axis),
        out_shape=jax.ShapeDtypeStruct(x.shape, x.dtype),
        in_specs=[pl.BlockSpec(memory_space=pl.ANY)],
        out_specs=pl.BlockSpec(memory_space=pl.ANY),
        scratch_shapes=[pltpu.SemaphoreType.DMA, pltpu.SemaphoreType.DMA, pltpu.SemaphoreType.DMA],
        compiler_params=pltpu.CompilerParams(has_side_effects=True),
    )(x)


def shifted(block, axis, distance):
    devices = range(lax.axis_size(axis))
    route = [(i - distance, i) for i in devices if i - distance in devices]
    return lax.ppermute(block, axis, route)


def attend(branch_query, key_new, value_new, child_tails, child_length):
    row_count = branch_query.shape[0]
    groups = key_new.shape[1] // HD
    per_group = branch_query.shape[1] // (groups * HD)
    tail_size = child_tails.shape[2]
    queries = branch_query.reshape(row_count, groups, per_group, HD)
    tail_keys = child_tails[0].reshape(row_count, tail_size, groups, HD)
    tail_values = child_tails[1].reshape(row_count, tail_size, groups, HD)
    own_keys = key_new.reshape(row_count, groups, HD)
    own_values = value_new.reshape(row_count, groups, HD)
    factor = 1.0 / math.sqrt(HD)
    tail_scores = (
        jnp.einsum("rgjd,rtgd->rgjt", queries, tail_keys, preferred_element_type=jnp.float32)
        * factor
    )
    own_scores = (
        jnp.einsum("rgjd,rgd->rgj", queries, own_keys, preferred_element_type=jnp.float32) * factor
    )
    live_mask = (jnp.arange(tail_size, dtype=jnp.float32)[None, :] < child_length[:, None])[
        :, None, None, :
    ]
    top_score = jnp.maximum(jnp.max(jnp.where(live_mask, tail_scores, -1e30), axis=-1), own_scores)
    tail_exp = jnp.where(live_mask, jnp.exp(tail_scores - top_score[..., None]), 0.0)
    own_exp = jnp.exp(own_scores - top_score)
    totals = jnp.sum(tail_exp, axis=-1) + own_exp
    tail_weights = (tail_exp / totals[..., None]).astype(jnp.bfloat16)
    own_weights = (own_exp / totals).astype(jnp.bfloat16)
    mixture = jnp.einsum(
        "rgjt,rtgd->rgjd", tail_weights, tail_values, preferred_element_type=jnp.float32
    )
    mixture = mixture + own_weights[..., None].astype(jnp.float32) * own_values[
        :, :, None, :
    ].astype(jnp.float32)
    return mixture.reshape(row_count, -1).astype(jnp.bfloat16)


def ffn_terms(picked, gate_blocks, up_blocks, gate_scale, up_scale, down_blocks, down_scale):
    gate_part = jnp.einsum(
        "rkd,kdf->rkf", picked, gate_blocks[0], preferred_element_type=jnp.float32
    )
    up_part = jnp.einsum("rkd,kdf->rkf", picked, up_blocks[0], preferred_element_type=jnp.float32)
    gate_sum = jnp.sum(gate_part * gate_scale[0][None, :, None], axis=1)
    up_sum = jnp.sum(up_part * up_scale[0][None, :, None], axis=1)
    hidden = (jax.nn.silu(gate_sum) * up_sum).astype(jnp.bfloat16)
    return (
        jnp.einsum("rf,kfe->rke", hidden, down_blocks[0], preferred_element_type=jnp.float32)
        * down_scale[0][None, :, None]
    )


def per_device(
    branch_query,
    key_new,
    value_new,
    pool_pages,
    page_table,
    tail_length,
    parent_row,
    residual,
    norm_gain,
    gate_blocks,
    up_blocks,
    gate_up_keep,
    gate_scale,
    up_scale,
    down_blocks,
    down_keep,
    down_scale,
):
    row_count = branch_query.shape[0]
    tail_size = page_table.shape[1] * pool_pages.shape[2]
    own_tails = pool_pages[:, page_table].reshape(2, row_count, tail_size, pool_pages.shape[3])
    own_length = tail_length.astype(jnp.bfloat16)
    prior_tails, prior_length = shifted((own_tails, own_length), "wide", 1)
    both_tails = jnp.concatenate([prior_tails, own_tails], axis=1)
    both_length = jnp.concatenate([prior_length, own_length]).astype(jnp.float32)
    local_parent = parent_row - (lax.axis_index("wide") - 1) * row_count
    child_tails = both_tails[:, local_parent]
    child_length = both_length[local_parent]
    attention = attend(branch_query, key_new, value_new, child_tails, child_length)
    head_rows = lax.all_to_all(attention, "head", split_axis=0, concat_axis=1, tiled=True)
    middle = residual.astype(jnp.float32) + head_rows.astype(jnp.float32)
    normed = (
        middle * lax.rsqrt(jnp.mean(middle * middle, axis=-1, keepdims=True) + 1e-05) * norm_gain
    ).astype(jnp.bfloat16)
    peers = lax.axis_size("wide")
    own_lists = jnp.concatenate([gate_up_keep, down_keep], axis=1)
    keep_lists = lax.all_to_all(
        jnp.broadcast_to(own_lists, (peers, own_lists.shape[1])),
        "wide",
        split_axis=0,
        concat_axis=0,
        tiled=True,
    )
    keep = gate_up_keep.shape[1]
    in_keep, out_keep = keep_lists[:, :keep], keep_lists[:, keep:]
    feature_blocks = normed.shape[1] // BLK
    blocks = jnp.arange(feature_blocks, dtype=jnp.int32)
    choose = (in_keep.reshape(peers * keep, 1) == blocks[None, :]).astype(jnp.bfloat16)
    normed_blocks = normed.reshape(normed.shape[0], feature_blocks, BLK)
    outgoing = jnp.einsum(
        "sb,rbd->srd", choose, normed_blocks, preferred_element_type=jnp.float32
    ).astype(jnp.bfloat16)
    outgoing = outgoing.reshape(peers, keep, normed.shape[0], BLK)
    picked = exchange(outgoing, "wide")
    picked = jnp.swapaxes(picked, 1, 2).reshape(-1, keep, BLK)
    contrib = ffn_terms(
        picked, gate_blocks, up_blocks, gate_scale, up_scale, down_blocks, down_scale
    ).astype(jnp.bfloat16)
    contrib = contrib.reshape(-1, normed.shape[0], keep, BLK)
    arrived = exchange(contrib, "wide")
    senders = arrived.shape[0]
    placement = (
        out_keep.reshape(senders * keep, 1) == jnp.arange(feature_blocks, dtype=jnp.int32)[None, :]
    ).astype(jnp.bfloat16)
    flat = jnp.swapaxes(arrived, 0, 1).reshape(normed.shape[0], senders * keep, BLK)
    ffn_share = jnp.einsum(
        "rsd,sb->rbd", flat, placement, preferred_element_type=jnp.float32
    ).reshape(normed.shape[0], -1)
    return (middle + ffn_share).astype(jnp.bfloat16)


def solution(mesh):
    placed = (
        P("wide", "head"),
        P("wide", "head"),
        P("wide", "head"),
        P(None, "wide", None, "head"),
        P("wide", None),
        P("wide"),
        P("wide"),
        P(("wide", "head"), None),
        P(),
        P("wide", None, None, None),
        P("wide", None, None, None),
        P("wide", None),
        P("wide", None),
        P("wide", None),
        P("wide", None, None, None),
        P("wide", None),
        P("wide", None),
    )
    return jax.shard_map(
        per_device, mesh=mesh, in_specs=placed, out_specs=P(("wide", "head"), None), check_vma=False
    )
```

```python
import functools
import math

import jax
import jax.numpy as jnp
from jax import lax
from jax.experimental import pallas as pl
from jax.experimental.pallas import tpu as pltpu
from jax.sharding import PartitionSpec as P

HD = 128
BLK = 128
Z_LANES = 4


def copy_head(source_z, target_lane, source_core, lanes):
    offset = (source_z - target_lane + 2 * lanes) % (2 * lanes)
    upper = ((offset + 1) % (2 * lanes)) // lanes
    tie = ((offset % lanes) // 2) * (1 - (offset % lanes) % 2)
    return upper + tie * source_core * (1 - 2 * upper)


def gather_route(me, here, peer, lanes):
    source_z = (me // 2) % lanes + lanes * here
    return copy_head(source_z, (peer // 2) % lanes, me % 2, lanes)


def return_route(me, here, peer, lanes):
    first = copy_head((peer // 2) % lanes, (me // 2) % lanes, peer % 2, lanes)
    return (first + here) % 2


def exchange_kernel(route, lanes, x_ref, y_ref, send_sem, recv_sem, local_sem):
    me = lax.axis_index("wide")
    here = lax.axis_index("head")
    n = x_ref.shape[0]
    local = pltpu.make_async_copy(x_ref.at[me], y_ref.at[me], local_sem)
    local.start()

    def send(j, carry):
        peer = lax.rem(me + j, n)
        pltpu.make_async_remote_copy(
            src_ref=x_ref.at[peer],
            dst_ref=y_ref.at[me],
            send_sem=send_sem,
            recv_sem=recv_sem,
            device_id=(peer, route(me, here, peer, lanes)),
            device_id_type=pl.DeviceIdType.MESH,
        ).start()
        return carry

    lax.fori_loop(1, n, send, 0)
    every = pltpu.make_async_remote_copy(
        src_ref=x_ref.at[pl.ds(0, n - 1)],
        dst_ref=y_ref.at[pl.ds(0, n - 1)],
        send_sem=send_sem,
        recv_sem=recv_sem,
        device_id=(me, here),
        device_id_type=pl.DeviceIdType.MESH,
    )
    every.wait_send()
    every.wait_recv()
    local.wait()


def exchange(x, route, lanes):
    return pl.pallas_call(
        functools.partial(exchange_kernel, route, lanes),
        out_shape=jax.ShapeDtypeStruct(x.shape, x.dtype),
        in_specs=[pl.BlockSpec(memory_space=pl.ANY)],
        out_specs=pl.BlockSpec(memory_space=pl.ANY),
        scratch_shapes=[pltpu.SemaphoreType.DMA, pltpu.SemaphoreType.DMA, pltpu.SemaphoreType.DMA],
        compiler_params=pltpu.CompilerParams(has_side_effects=True),
    )(x)


def shifted(block, axis, distance):
    devices = range(lax.axis_size(axis))
    route = [(i - distance, i) for i in devices if i - distance in devices]
    return lax.ppermute(block, axis, route)


def attend(branch_query, key_new, value_new, child_tails, child_length):
    row_count = branch_query.shape[0]
    groups = key_new.shape[1] // HD
    per_group = branch_query.shape[1] // (groups * HD)
    tail_size = child_tails.shape[2]
    queries = branch_query.reshape(row_count, groups, per_group, HD)
    tail_keys = child_tails[0].reshape(row_count, tail_size, groups, HD)
    tail_values = child_tails[1].reshape(row_count, tail_size, groups, HD)
    own_keys = key_new.reshape(row_count, groups, HD)
    own_values = value_new.reshape(row_count, groups, HD)
    factor = 1.0 / math.sqrt(HD)
    tail_scores = (
        jnp.einsum("rgjd,rtgd->rgjt", queries, tail_keys, preferred_element_type=jnp.float32)
        * factor
    )
    own_scores = (
        jnp.einsum("rgjd,rgd->rgj", queries, own_keys, preferred_element_type=jnp.float32) * factor
    )
    live_mask = (jnp.arange(tail_size, dtype=jnp.float32)[None, :] < child_length[:, None])[
        :, None, None, :
    ]
    top_score = jnp.maximum(jnp.max(jnp.where(live_mask, tail_scores, -1e30), axis=-1), own_scores)
    tail_exp = jnp.where(live_mask, jnp.exp(tail_scores - top_score[..., None]), 0.0)
    own_exp = jnp.exp(own_scores - top_score)
    totals = jnp.sum(tail_exp, axis=-1) + own_exp
    tail_weights = (tail_exp / totals[..., None]).astype(jnp.bfloat16)
    own_weights = (own_exp / totals).astype(jnp.bfloat16)
    mixture = jnp.einsum(
        "rgjt,rtgd->rgjd", tail_weights, tail_values, preferred_element_type=jnp.float32
    )
    mixture = mixture + own_weights[..., None].astype(jnp.float32) * own_values[
        :, :, None, :
    ].astype(jnp.float32)
    return mixture.reshape(row_count, -1).astype(jnp.bfloat16)


def ffn_terms(picked, gate_blocks, up_blocks, gate_scale, up_scale, down_blocks, down_scale):
    gate_part = jnp.einsum(
        "skd,kdf->skf", picked, gate_blocks[0], preferred_element_type=jnp.float32
    )
    up_part = jnp.einsum("skd,kdf->skf", picked, up_blocks[0], preferred_element_type=jnp.float32)
    gate_sum = jnp.sum(gate_part * gate_scale[0][None, :, None], axis=1)
    up_sum = jnp.sum(up_part * up_scale[0][None, :, None], axis=1)
    hidden = (jax.nn.silu(gate_sum) * up_sum).astype(jnp.bfloat16)
    return (
        jnp.einsum("sf,kfe->ske", hidden, down_blocks[0], preferred_element_type=jnp.float32)
        * down_scale[0][None, :, None]
    ).astype(jnp.bfloat16)


def per_device(
    branch_query,
    key_new,
    value_new,
    pool_pages,
    page_table,
    tail_length,
    parent_row,
    residual,
    norm_gain,
    gate_blocks,
    up_blocks,
    gate_up_keep,
    gate_scale,
    up_scale,
    down_blocks,
    down_keep,
    down_scale,
):
    row_count = branch_query.shape[0]
    tail_size = page_table.shape[1] * pool_pages.shape[2]
    own_tails = pool_pages[:, page_table].reshape(2, row_count, tail_size, pool_pages.shape[3])
    own_length = tail_length.astype(jnp.bfloat16)
    prior_tails, prior_length = shifted((own_tails, own_length), "wide", 1)
    both_tails = jnp.concatenate([prior_tails, own_tails], axis=1)
    both_length = jnp.concatenate([prior_length, own_length]).astype(jnp.float32)
    local_parent = parent_row - (lax.axis_index("wide") - 1) * row_count
    child_tails = both_tails[:, local_parent]
    child_length = both_length[local_parent]
    attention = attend(branch_query, key_new, value_new, child_tails, child_length)
    head_rows = lax.all_to_all(attention, "head", split_axis=0, concat_axis=1, tiled=True)
    middle = residual.astype(jnp.float32) + head_rows.astype(jnp.float32)
    normed = (
        middle * lax.rsqrt(jnp.mean(middle * middle, axis=-1, keepdims=True) + 1e-05) * norm_gain
    ).astype(jnp.bfloat16)
    peers = lax.axis_size("wide")
    own_lists = jnp.concatenate([gate_up_keep, down_keep], axis=1)
    keep_lists = lax.all_to_all(
        jnp.broadcast_to(own_lists, (peers, own_lists.shape[1])),
        "wide",
        split_axis=0,
        concat_axis=0,
        tiled=True,
    )
    keep = gate_up_keep.shape[1]
    in_keep, out_keep = keep_lists[:, :keep], keep_lists[:, keep:]
    feature_blocks = normed.shape[1] // BLK
    rows = normed.shape[0]
    blocks = jnp.arange(feature_blocks, dtype=jnp.int32)
    choose = (in_keep.reshape(peers * keep, 1) == blocks[None, :]).astype(jnp.bfloat16)
    by_block = jnp.swapaxes(normed.reshape(rows, feature_blocks, BLK), 0, 1)
    outgoing = jnp.dot(
        choose, by_block.reshape(feature_blocks, rows * BLK), preferred_element_type=jnp.float32
    ).astype(jnp.bfloat16)
    picked = exchange(outgoing.reshape(peers, keep, rows * BLK), gather_route, Z_LANES)
    terms = [
        ffn_terms(
            picked[:, :, r * BLK : (r + 1) * BLK],
            gate_blocks,
            up_blocks,
            gate_scale,
            up_scale,
            down_blocks,
            down_scale,
        )
        for r in range(rows)
    ]
    arrived = exchange(jnp.concatenate(terms, axis=2), return_route, Z_LANES)
    placement = (out_keep.reshape(peers * keep, 1) == blocks[None, :]).astype(jnp.bfloat16)
    summed = lax.dot_general(
        placement,
        arrived.reshape(peers * keep, rows * BLK),
        (((0,), (0,)), ((), ())),
        preferred_element_type=jnp.float32,
    )
    ffn_share = jnp.swapaxes(summed.reshape(feature_blocks, rows, BLK), 0, 1).reshape(rows, -1)
    return (middle + ffn_share).astype(jnp.bfloat16)


def solution(mesh):
    placed = (
        P("wide", "head"),
        P("wide", "head"),
        P("wide", "head"),
        P(None, "wide", None, "head"),
        P("wide", None),
        P("wide"),
        P("wide"),
        P(("wide", "head"), None),
        P(),
        P("wide", None, None, None),
        P("wide", None, None, None),
        P("wide", None),
        P("wide", None),
        P("wide", None),
        P("wide", None, None, None),
        P("wide", None),
        P("wide", None),
    )
    return jax.shard_map(
        per_device, mesh=mesh, in_specs=placed, out_specs=P(("wide", "head"), None), check_vma=False
    )
```

```python
import functools
import math

import jax
import jax.numpy as jnp
from jax import lax
from jax.experimental import pallas as pl
from jax.experimental.pallas import tpu as pltpu
from jax.sharding import PartitionSpec as P

HD = 128
BLK = 128
Z_LANES = 4


def copy_head(source_z, target_lane, source_core, lanes):
    offset = (source_z - target_lane + 2 * lanes) % (2 * lanes)
    upper = ((offset + 1) % (2 * lanes)) // lanes
    tie = ((offset % lanes) // 2) * (1 - (offset % lanes) % 2)
    return upper + tie * source_core * (1 - 2 * upper)


def gather_route(me, here, peer, lanes):
    source_z = (me // 2) % lanes + lanes * here
    return copy_head(source_z, (peer // 2) % lanes, me % 2, lanes)


def return_route(me, here, peer, lanes):
    first = copy_head((peer // 2) % lanes, (me // 2) % lanes, peer % 2, lanes)
    return (first + here) % 2


def exchange_kernel(route, lanes, x_ref, y_ref, send_sem, recv_sem, local_sem):
    me = lax.axis_index("wide")
    here = lax.axis_index("head")
    n = x_ref.shape[0]
    local = pltpu.make_async_copy(x_ref.at[me], y_ref.at[me], local_sem)
    local.start()

    def send(j, carry):
        peer = lax.rem(me + j, n)
        pltpu.make_async_remote_copy(
            src_ref=x_ref.at[peer],
            dst_ref=y_ref.at[me],
            send_sem=send_sem,
            recv_sem=recv_sem,
            device_id=(peer, route(me, here, peer, lanes)),
            device_id_type=pl.DeviceIdType.MESH,
        ).start()
        return carry

    lax.fori_loop(1, n, send, 0)
    every = pltpu.make_async_remote_copy(
        src_ref=x_ref.at[pl.ds(0, n - 1)],
        dst_ref=y_ref.at[pl.ds(0, n - 1)],
        send_sem=send_sem,
        recv_sem=recv_sem,
        device_id=(me, here),
        device_id_type=pl.DeviceIdType.MESH,
    )
    every.wait_send()
    every.wait_recv()
    local.wait()


def exchange(x, route, lanes):
    return pl.pallas_call(
        functools.partial(exchange_kernel, route, lanes),
        out_shape=jax.ShapeDtypeStruct(x.shape, x.dtype),
        in_specs=[pl.BlockSpec(memory_space=pl.ANY)],
        out_specs=pl.BlockSpec(memory_space=pl.ANY),
        scratch_shapes=[pltpu.SemaphoreType.DMA, pltpu.SemaphoreType.DMA, pltpu.SemaphoreType.DMA],
        compiler_params=pltpu.CompilerParams(has_side_effects=True),
    )(x)


def shifted(block, axis, distance):
    devices = range(lax.axis_size(axis))
    route = [(i - distance, i) for i in devices if i - distance in devices]
    return lax.ppermute(block, axis, route)


def attend(branch_query, key_new, value_new, child_tails, child_length):
    row_count = branch_query.shape[0]
    groups = key_new.shape[1] // HD
    per_group = branch_query.shape[1] // (groups * HD)
    tail_size = child_tails.shape[2]
    queries = branch_query.reshape(row_count, groups, per_group, HD)
    tail_keys = child_tails[0].reshape(row_count, tail_size, groups, HD)
    tail_values = child_tails[1].reshape(row_count, tail_size, groups, HD)
    own_keys = key_new.reshape(row_count, groups, HD)
    own_values = value_new.reshape(row_count, groups, HD)
    factor = 1.0 / math.sqrt(HD)
    tail_scores = (
        jnp.einsum("rgjd,rtgd->rgjt", queries, tail_keys, preferred_element_type=jnp.float32)
        * factor
    )
    own_scores = (
        jnp.einsum("rgjd,rgd->rgj", queries, own_keys, preferred_element_type=jnp.float32) * factor
    )
    live_mask = (jnp.arange(tail_size, dtype=jnp.float32)[None, :] < child_length[:, None])[
        :, None, None, :
    ]
    top_score = jnp.maximum(jnp.max(jnp.where(live_mask, tail_scores, -1e30), axis=-1), own_scores)
    tail_exp = jnp.where(live_mask, jnp.exp(tail_scores - top_score[..., None]), 0.0)
    own_exp = jnp.exp(own_scores - top_score)
    totals = jnp.sum(tail_exp, axis=-1) + own_exp
    tail_weights = (tail_exp / totals[..., None]).astype(jnp.bfloat16)
    own_weights = (own_exp / totals).astype(jnp.bfloat16)
    mixture = jnp.einsum(
        "rgjt,rtgd->rgjd", tail_weights, tail_values, preferred_element_type=jnp.float32
    )
    mixture = mixture + own_weights[..., None].astype(jnp.float32) * own_values[
        :, :, None, :
    ].astype(jnp.float32)
    return mixture.reshape(row_count, -1).astype(jnp.bfloat16)


def ffn_terms(picked, gate_blocks, up_blocks, gate_scale, up_scale, down_blocks, down_scale):
    gate_part = jnp.einsum(
        "skd,kdf->ksf", picked, gate_blocks[0], preferred_element_type=jnp.float32
    )
    up_part = jnp.einsum("skd,kdf->ksf", picked, up_blocks[0], preferred_element_type=jnp.float32)
    gate_sum = jnp.sum(gate_part * gate_scale[0][:, None, None], axis=0)
    up_sum = jnp.sum(up_part * up_scale[0][:, None, None], axis=0)
    hidden = (jax.nn.silu(gate_sum) * up_sum).astype(jnp.bfloat16)
    return (
        jnp.einsum("sf,kfe->ske", hidden, down_blocks[0], preferred_element_type=jnp.float32)
        * down_scale[0][None, :, None]
    ).astype(jnp.bfloat16)


def per_device(
    branch_query,
    key_new,
    value_new,
    pool_pages,
    page_table,
    tail_length,
    parent_row,
    residual,
    norm_gain,
    gate_blocks,
    up_blocks,
    gate_up_keep,
    gate_scale,
    up_scale,
    down_blocks,
    down_keep,
    down_scale,
):
    row_count = branch_query.shape[0]
    tail_size = page_table.shape[1] * pool_pages.shape[2]
    own_tails = pool_pages[:, page_table].reshape(2, row_count, tail_size, pool_pages.shape[3])
    own_length = tail_length.astype(jnp.bfloat16)
    prior_tails, prior_length = shifted((own_tails, own_length), "wide", 1)
    both_tails = jnp.concatenate([prior_tails, own_tails], axis=1)
    both_length = jnp.concatenate([prior_length, own_length]).astype(jnp.float32)
    local_parent = parent_row - (lax.axis_index("wide") - 1) * row_count
    child_tails = both_tails[:, local_parent]
    child_length = both_length[local_parent]
    attention = attend(branch_query, key_new, value_new, child_tails, child_length)
    half = residual.shape[0]
    here = lax.axis_index("head")
    mine = lax.dynamic_slice_in_dim(attention, here * half, half, axis=0)
    theirs = lax.dynamic_slice_in_dim(attention, (1 - here) * half, half, axis=0)
    arrived_half = lax.ppermute(theirs, "head", [(0, 1), (1, 0)])
    head_rows = jnp.where(
        here == 0,
        jnp.concatenate([mine, arrived_half], axis=1),
        jnp.concatenate([arrived_half, mine], axis=1),
    )
    middle = residual.astype(jnp.float32) + head_rows.astype(jnp.float32)
    normed = (
        middle * lax.rsqrt(jnp.mean(middle * middle, axis=-1, keepdims=True) + 1e-05) * norm_gain
    ).astype(jnp.bfloat16)
    peers = lax.axis_size("wide")
    own_lists = jnp.concatenate([gate_up_keep, down_keep], axis=1)
    keep_lists = lax.all_to_all(
        jnp.broadcast_to(own_lists, (peers, own_lists.shape[1])),
        "wide",
        split_axis=0,
        concat_axis=0,
        tiled=True,
    )
    keep = gate_up_keep.shape[1]
    in_keep, out_keep = keep_lists[:, :keep], keep_lists[:, keep:]
    feature_blocks = normed.shape[1] // BLK
    rows = normed.shape[0]
    blocks = jnp.arange(feature_blocks, dtype=jnp.int32)
    choose = (in_keep.reshape(peers * keep, 1) == blocks[None, :]).astype(jnp.bfloat16)
    by_block = jnp.swapaxes(normed.reshape(rows, feature_blocks, BLK), 0, 1)
    outgoing = jnp.dot(
        choose, by_block.reshape(feature_blocks, rows * BLK), preferred_element_type=jnp.float32
    ).astype(jnp.bfloat16)
    picked = exchange(outgoing.reshape(peers, keep, rows * BLK), gather_route, Z_LANES)
    terms = [
        ffn_terms(
            picked[:, :, r * BLK : (r + 1) * BLK],
            gate_blocks,
            up_blocks,
            gate_scale,
            up_scale,
            down_blocks,
            down_scale,
        )
        for r in range(rows)
    ]
    arrived = exchange(jnp.concatenate(terms, axis=2), return_route, Z_LANES)
    placement = (blocks[:, None] == out_keep.reshape(1, peers * keep)).astype(jnp.bfloat16)
    summed = jnp.dot(
        placement, arrived.reshape(peers * keep, rows * BLK), preferred_element_type=jnp.float32
    )
    ffn_share = jnp.swapaxes(summed.reshape(feature_blocks, rows, BLK), 0, 1).reshape(rows, -1)
    return (middle + ffn_share).astype(jnp.bfloat16)


def solution(mesh):
    placed = (
        P("wide", "head"),
        P("wide", "head"),
        P("wide", "head"),
        P(None, "wide", None, "head"),
        P("wide", None),
        P("wide"),
        P("wide"),
        P(("wide", "head"), None),
        P(),
        P("wide", None, None, None),
        P("wide", None, None, None),
        P("wide", None),
        P("wide", None),
        P("wide", None),
        P("wide", None, None, None),
        P("wide", None),
        P("wide", None),
    )
    return jax.shard_map(
        per_device, mesh=mesh, in_specs=placed, out_specs=P(("wide", "head"), None), check_vma=False
    )
```

```python
import functools
import math

import jax
import jax.numpy as jnp
from jax import lax
from jax.experimental import pallas as pl
from jax.experimental.pallas import tpu as pltpu
from jax.sharding import PartitionSpec as P

HD = 128
BLK = 128
Z_LANES = 4


def copy_head(source_z, target_lane, source_core, lanes):
    offset = (source_z - target_lane + 2 * lanes) % (2 * lanes)
    upper = ((offset + 1) % (2 * lanes)) // lanes
    tie = ((offset % lanes) // 2) * (1 - (offset % lanes) % 2)
    return upper + tie * source_core * (1 - 2 * upper)


def gather_route(me, here, peer, lanes):
    source_z = (me // 2) % lanes + lanes * here
    return copy_head(source_z, (peer // 2) % lanes, me % 2, lanes)


def return_route(me, here, peer, lanes):
    first = copy_head((peer // 2) % lanes, (me // 2) % lanes, peer % 2, lanes)
    return (first + here) % 2


def exchange_kernel(route, lanes, x_ref, y_ref, send_sem, recv_sem, local_sem):
    me = lax.axis_index("wide")
    here = lax.axis_index("head")
    n = x_ref.shape[0]
    local = pltpu.make_async_copy(x_ref.at[me], y_ref.at[me], local_sem)
    local.start()

    def send(j, carry):
        peer = lax.rem(me + j, n)
        pltpu.make_async_remote_copy(
            src_ref=x_ref.at[peer],
            dst_ref=y_ref.at[me],
            send_sem=send_sem,
            recv_sem=recv_sem,
            device_id=(peer, route(me, here, peer, lanes)),
            device_id_type=pl.DeviceIdType.MESH,
        ).start()
        return carry

    lax.fori_loop(1, n, send, 0)
    every = pltpu.make_async_remote_copy(
        src_ref=x_ref.at[pl.ds(0, n - 1)],
        dst_ref=y_ref.at[pl.ds(0, n - 1)],
        send_sem=send_sem,
        recv_sem=recv_sem,
        device_id=(me, here),
        device_id_type=pl.DeviceIdType.MESH,
    )
    every.wait_send()
    every.wait_recv()
    local.wait()


def exchange(x, route, lanes):
    return pl.pallas_call(
        functools.partial(exchange_kernel, route, lanes),
        out_shape=jax.ShapeDtypeStruct(x.shape, x.dtype),
        in_specs=[pl.BlockSpec(memory_space=pl.ANY)],
        out_specs=pl.BlockSpec(memory_space=pl.ANY),
        scratch_shapes=[pltpu.SemaphoreType.DMA, pltpu.SemaphoreType.DMA, pltpu.SemaphoreType.DMA],
        compiler_params=pltpu.CompilerParams(has_side_effects=True),
    )(x)


def shifted(block, axis, distance):
    devices = range(lax.axis_size(axis))
    route = [(i - distance, i) for i in devices if i - distance in devices]
    return lax.ppermute(block, axis, route)


def attend(branch_query, key_new, value_new, pools, tables, lengths, source, row):
    row_count = branch_query.shape[0]
    groups = key_new.shape[1] // HD
    per_group = branch_query.shape[1] // (groups * HD)
    pages, page_size = pools[0].shape[1], pools[0].shape[2]
    queries = branch_query.reshape(row_count, groups, per_group, HD)
    own_keys = key_new.reshape(row_count, groups, HD)
    own_values = value_new.reshape(row_count, groups, HD)
    factor = 1.0 / math.sqrt(HD)
    page_ids = jnp.arange(pages, dtype=jnp.int32)
    slots = jnp.arange(tables[0].shape[1], dtype=jnp.int32)
    offsets = jnp.arange(page_size, dtype=jnp.int32)
    scores, masks = [], []
    for which, (pool, table, length) in enumerate(zip(pools, tables, lengths)):
        parent_table = table[row]
        match = parent_table[:, None, :] == page_ids[None, :, None]
        slot = jnp.sum(jnp.where(match, slots[None, None, :], 0), axis=-1)
        found = jnp.any(match, axis=-1) & (source == which)[:, None]
        live = found[:, :, None] & (
            slot[:, :, None] * page_size + offsets[None, None, :] < length[row][:, None, None]
        )
        keys = pool[0].reshape(pages * page_size, groups, HD)
        part = (
            jnp.einsum("rgjd,tgd->rgjt", queries, keys, preferred_element_type=jnp.float32)
            * factor
        )
        scores.append(part)
        masks.append(live.reshape(row_count, 1, 1, pages * page_size))
    tail_scores = jnp.concatenate(scores, axis=-1)
    live_mask = jnp.concatenate(masks, axis=-1)
    own_scores = (
        jnp.einsum("rgjd,rgd->rgj", queries, own_keys, preferred_element_type=jnp.float32) * factor
    )
    top_score = jnp.maximum(jnp.max(jnp.where(live_mask, tail_scores, -1e30), axis=-1), own_scores)
    tail_exp = jnp.where(live_mask, jnp.exp(tail_scores - top_score[..., None]), 0.0)
    own_exp = jnp.exp(own_scores - top_score)
    totals = jnp.sum(tail_exp, axis=-1) + own_exp
    tail_weights = (tail_exp / totals[..., None]).astype(jnp.bfloat16)
    own_weights = (own_exp / totals).astype(jnp.bfloat16)
    span = pages * page_size
    mixture = own_weights[..., None].astype(jnp.float32) * own_values[:, :, None, :].astype(
        jnp.float32
    )
    for which, pool in enumerate(pools):
        values = pool[1].reshape(span, groups, HD)
        mixture = mixture + jnp.einsum(
            "rgjt,tgd->rgjd",
            tail_weights[..., which * span : (which + 1) * span],
            values,
            preferred_element_type=jnp.float32,
        )
    return mixture.reshape(row_count, -1).astype(jnp.bfloat16)


def ffn_terms(picked, gate_blocks, up_blocks, gate_scale, up_scale, down_blocks, down_scale):
    gate_part = jnp.einsum(
        "skd,kdf->ksf", picked, gate_blocks[0], preferred_element_type=jnp.float32
    )
    up_part = jnp.einsum("skd,kdf->ksf", picked, up_blocks[0], preferred_element_type=jnp.float32)
    gate_sum = jnp.sum(gate_part * gate_scale[0][:, None, None], axis=0)
    up_sum = jnp.sum(up_part * up_scale[0][:, None, None], axis=0)
    hidden = (jax.nn.silu(gate_sum) * up_sum).astype(jnp.bfloat16)
    return (
        jnp.einsum("sf,kfe->ske", hidden, down_blocks[0], preferred_element_type=jnp.float32)
        * down_scale[0][None, :, None]
    ).astype(jnp.bfloat16)


def per_device(
    branch_query,
    key_new,
    value_new,
    pool_pages,
    page_table,
    tail_length,
    parent_row,
    residual,
    norm_gain,
    gate_blocks,
    up_blocks,
    gate_up_keep,
    gate_scale,
    up_scale,
    down_blocks,
    down_keep,
    down_scale,
):
    row_count = branch_query.shape[0]
    prior = shifted((pool_pages, page_table, tail_length), "wide", 1)
    local_parent = parent_row - (lax.axis_index("wide") - 1) * row_count
    attention = attend(
        branch_query,
        key_new,
        value_new,
        (prior[0], pool_pages),
        (prior[1], page_table),
        (prior[2], tail_length),
        local_parent // row_count,
        local_parent % row_count,
    )
    half = residual.shape[0]
    here = lax.axis_index("head")
    mine = lax.dynamic_slice_in_dim(attention, here * half, half, axis=0)
    theirs = lax.dynamic_slice_in_dim(attention, (1 - here) * half, half, axis=0)
    arrived_half = lax.ppermute(theirs, "head", [(0, 1), (1, 0)])
    head_rows = jnp.where(
        here == 0,
        jnp.concatenate([mine, arrived_half], axis=1),
        jnp.concatenate([arrived_half, mine], axis=1),
    )
    middle = residual.astype(jnp.float32) + head_rows.astype(jnp.float32)
    normed = (
        middle * lax.rsqrt(jnp.mean(middle * middle, axis=-1, keepdims=True) + 1e-05) * norm_gain
    ).astype(jnp.bfloat16)
    peers = lax.axis_size("wide")
    own_lists = jnp.concatenate([gate_up_keep, down_keep], axis=1)
    keep_lists = lax.all_to_all(
        jnp.broadcast_to(own_lists, (peers, own_lists.shape[1])),
        "wide",
        split_axis=0,
        concat_axis=0,
        tiled=True,
    )
    keep = gate_up_keep.shape[1]
    in_keep, out_keep = keep_lists[:, :keep], keep_lists[:, keep:]
    feature_blocks = normed.shape[1] // BLK
    rows = normed.shape[0]
    blocks = jnp.arange(feature_blocks, dtype=jnp.int32)
    choose = (in_keep.reshape(peers * keep, 1) == blocks[None, :]).astype(jnp.bfloat16)
    by_block = jnp.swapaxes(normed.reshape(rows, feature_blocks, BLK), 0, 1)
    outgoing = jnp.dot(
        choose, by_block.reshape(feature_blocks, rows * BLK), preferred_element_type=jnp.float32
    ).astype(jnp.bfloat16)
    picked = exchange(outgoing.reshape(peers, keep, rows * BLK), gather_route, Z_LANES)
    terms = [
        ffn_terms(
            picked[:, :, r * BLK : (r + 1) * BLK],
            gate_blocks,
            up_blocks,
            gate_scale,
            up_scale,
            down_blocks,
            down_scale,
        )
        for r in range(rows)
    ]
    arrived = exchange(jnp.concatenate(terms, axis=2), return_route, Z_LANES)
    placement = (blocks[:, None] == out_keep.reshape(1, peers * keep)).astype(jnp.bfloat16)
    summed = jnp.dot(
        placement, arrived.reshape(peers * keep, rows * BLK), preferred_element_type=jnp.float32
    )
    ffn_share = jnp.swapaxes(summed.reshape(feature_blocks, rows, BLK), 0, 1).reshape(rows, -1)
    return (middle + ffn_share).astype(jnp.bfloat16)


def solution(mesh):
    placed = (
        P("wide", "head"),
        P("wide", "head"),
        P("wide", "head"),
        P(None, "wide", None, "head"),
        P("wide", None),
        P("wide"),
        P("wide"),
        P(("wide", "head"), None),
        P(),
        P("wide", None, None, None),
        P("wide", None, None, None),
        P("wide", None),
        P("wide", None),
        P("wide", None),
        P("wide", None, None, None),
        P("wide", None),
        P("wide", None),
    )
    return jax.shard_map(
        per_device, mesh=mesh, in_specs=placed, out_specs=P(("wide", "head"), None), check_vma=False
    )
```

```python
import functools
import math

import jax
import jax.numpy as jnp
from jax import lax
from jax.experimental import pallas as pl
from jax.experimental.pallas import tpu as pltpu
from jax.sharding import PartitionSpec as P

HD = 128
BLK = 128
Z_LANES = 4


def copy_head(source_z, target_lane, source_core, lanes):
    offset = (source_z - target_lane + 2 * lanes) % (2 * lanes)
    upper = ((offset + 1) % (2 * lanes)) // lanes
    tie = ((offset % lanes) // 2) * (1 - (offset % lanes) % 2)
    return upper + tie * source_core * (1 - 2 * upper)


def gather_route(me, here, peer, lanes):
    source_z = (me // 2) % lanes + lanes * here
    return copy_head(source_z, (peer // 2) % lanes, me % 2, lanes)


def return_route(me, here, peer, lanes):
    first = copy_head((peer // 2) % lanes, (me // 2) % lanes, peer % 2, lanes)
    return (first + here) % 2


def exchange_kernel(route, lanes, x_ref, y_ref, send_sem, recv_sem, local_sem):
    me = lax.axis_index("wide")
    here = lax.axis_index("head")
    n = x_ref.shape[0]
    local = pltpu.make_async_copy(x_ref.at[me], y_ref.at[me], local_sem)
    local.start()

    def send(j, carry):
        peer = lax.rem(me + j, n)
        pltpu.make_async_remote_copy(
            src_ref=x_ref.at[peer],
            dst_ref=y_ref.at[me],
            send_sem=send_sem,
            recv_sem=recv_sem,
            device_id=(peer, route(me, here, peer, lanes)),
            device_id_type=pl.DeviceIdType.MESH,
        ).start()
        return carry

    lax.fori_loop(1, n, send, 0)
    every = pltpu.make_async_remote_copy(
        src_ref=x_ref.at[pl.ds(0, n - 1)],
        dst_ref=y_ref.at[pl.ds(0, n - 1)],
        send_sem=send_sem,
        recv_sem=recv_sem,
        device_id=(me, here),
        device_id_type=pl.DeviceIdType.MESH,
    )
    every.wait_send()
    every.wait_recv()
    local.wait()


def exchange(x, route, lanes):
    return pl.pallas_call(
        functools.partial(exchange_kernel, route, lanes),
        out_shape=jax.ShapeDtypeStruct(x.shape, x.dtype),
        in_specs=[pl.BlockSpec(memory_space=pl.ANY)],
        out_specs=pl.BlockSpec(memory_space=pl.ANY),
        scratch_shapes=[pltpu.SemaphoreType.DMA, pltpu.SemaphoreType.DMA, pltpu.SemaphoreType.DMA],
        compiler_params=pltpu.CompilerParams(has_side_effects=True),
    )(x)


def shifted(block, axis, distance):
    devices = range(lax.axis_size(axis))
    route = [(i - distance, i) for i in devices if i - distance in devices]
    return lax.ppermute(block, axis, route)


def attend(branch_query, key_new, value_new, pools, tables, lengths, source, row):
    row_count = branch_query.shape[0]
    groups = key_new.shape[1] // HD
    per_group = branch_query.shape[1] // (groups * HD)
    pages, page_size = pools[0].shape[1], pools[0].shape[2]
    queries = branch_query.reshape(row_count, groups, per_group, HD)
    own_keys = key_new.reshape(row_count, groups, HD)
    own_values = value_new.reshape(row_count, groups, HD)
    factor = 1.0 / math.sqrt(HD)
    page_ids = jnp.arange(pages, dtype=jnp.int32)
    slots = jnp.arange(tables[0].shape[1], dtype=jnp.int32)
    offsets = jnp.arange(page_size, dtype=jnp.int32)
    scores, masks = [], []
    for which, (pool, table, length) in enumerate(zip(pools, tables, lengths)):
        parent_table = table[row]
        match = parent_table[:, None, :] == page_ids[None, :, None]
        slot = jnp.sum(jnp.where(match, slots[None, None, :], 0), axis=-1)
        found = jnp.any(match, axis=-1) & (source == which)[:, None]
        live = found[:, :, None] & (
            slot[:, :, None] * page_size + offsets[None, None, :] < length[row][:, None, None]
        )
        keys = pool[0].reshape(pages * page_size, groups * HD)
        part = jnp.stack(
            [
                jnp.einsum(
                    "rjd,td->rjt",
                    queries[:, g],
                    keys[:, g * HD : (g + 1) * HD],
                    preferred_element_type=jnp.float32,
                )
                for g in range(groups)
            ],
            axis=1,
        ) * factor
        scores.append(part)
        masks.append(live.reshape(row_count, 1, 1, pages * page_size))
    tail_scores = jnp.concatenate(scores, axis=-1)
    live_mask = jnp.concatenate(masks, axis=-1)
    own_scores = (
        jnp.einsum("rgjd,rgd->rgj", queries, own_keys, preferred_element_type=jnp.float32) * factor
    )
    top_score = jnp.maximum(jnp.max(jnp.where(live_mask, tail_scores, -1e30), axis=-1), own_scores)
    tail_exp = jnp.where(live_mask, jnp.exp(tail_scores - top_score[..., None]), 0.0)
    own_exp = jnp.exp(own_scores - top_score)
    totals = jnp.sum(tail_exp, axis=-1) + own_exp
    tail_weights = (tail_exp / totals[..., None]).astype(jnp.bfloat16)
    own_weights = (own_exp / totals).astype(jnp.bfloat16)
    span = pages * page_size
    mixture = own_weights[..., None].astype(jnp.float32) * own_values[:, :, None, :].astype(
        jnp.float32
    )
    for which, pool in enumerate(pools):
        values = pool[1].reshape(span, groups * HD)
        weights = tail_weights[..., which * span : (which + 1) * span]
        mixture = mixture + jnp.stack(
            [
                jnp.einsum(
                    "rjt,td->rjd",
                    weights[:, g],
                    values[:, g * HD : (g + 1) * HD],
                    preferred_element_type=jnp.float32,
                )
                for g in range(groups)
            ],
            axis=1,
        )
    return mixture.reshape(row_count, -1).astype(jnp.bfloat16)


def ffn_terms(picked, gate_blocks, up_blocks, gate_scale, up_scale, down_blocks, down_scale):
    gate_part = jnp.einsum(
        "skd,kdf->ksf", picked, gate_blocks[0], preferred_element_type=jnp.float32
    )
    up_part = jnp.einsum("skd,kdf->ksf", picked, up_blocks[0], preferred_element_type=jnp.float32)
    gate_sum = jnp.sum(gate_part * gate_scale[0][:, None, None], axis=0)
    up_sum = jnp.sum(up_part * up_scale[0][:, None, None], axis=0)
    hidden = (jax.nn.silu(gate_sum) * up_sum).astype(jnp.bfloat16)
    return (
        jnp.einsum("sf,kfe->ske", hidden, down_blocks[0], preferred_element_type=jnp.float32)
        * down_scale[0][None, :, None]
    ).astype(jnp.bfloat16)


def per_device(
    branch_query,
    key_new,
    value_new,
    pool_pages,
    page_table,
    tail_length,
    parent_row,
    residual,
    norm_gain,
    gate_blocks,
    up_blocks,
    gate_up_keep,
    gate_scale,
    up_scale,
    down_blocks,
    down_keep,
    down_scale,
):
    row_count = branch_query.shape[0]
    prior_pool, prior_meta = shifted(
        (pool_pages, jnp.concatenate([page_table, tail_length[:, None]], axis=1)), "wide", 1
    )
    prior = (prior_pool, prior_meta[:, :-1], prior_meta[:, -1])
    local_parent = parent_row - (lax.axis_index("wide") - 1) * row_count
    attention = attend(
        branch_query,
        key_new,
        value_new,
        (prior[0], pool_pages),
        (prior[1], page_table),
        (prior[2], tail_length),
        local_parent // row_count,
        local_parent % row_count,
    )
    half = residual.shape[0]
    here = lax.axis_index("head")
    mine = lax.dynamic_slice_in_dim(attention, here * half, half, axis=0)
    theirs = lax.dynamic_slice_in_dim(attention, (1 - here) * half, half, axis=0)
    arrived_half = lax.ppermute(theirs, "head", [(0, 1), (1, 0)])
    head_rows = jnp.where(
        here == 0,
        jnp.concatenate([mine, arrived_half], axis=1),
        jnp.concatenate([arrived_half, mine], axis=1),
    )
    middle = residual.astype(jnp.float32) + head_rows.astype(jnp.float32)
    normed = (
        middle * lax.rsqrt(jnp.mean(middle * middle, axis=-1, keepdims=True) + 1e-05) * norm_gain
    ).astype(jnp.bfloat16)
    peers = lax.axis_size("wide")
    own_lists = jnp.concatenate([gate_up_keep, down_keep], axis=1)
    keep_lists = lax.all_to_all(
        jnp.broadcast_to(own_lists, (peers, own_lists.shape[1])),
        "wide",
        split_axis=0,
        concat_axis=0,
        tiled=True,
    )
    keep = gate_up_keep.shape[1]
    in_keep, out_keep = keep_lists[:, :keep], keep_lists[:, keep:]
    feature_blocks = normed.shape[1] // BLK
    rows = normed.shape[0]
    blocks = jnp.arange(feature_blocks, dtype=jnp.int32)
    choose = (in_keep.reshape(peers * keep, 1) == blocks[None, :]).astype(jnp.bfloat16)
    by_block = jnp.swapaxes(normed.reshape(rows, feature_blocks, BLK), 0, 1)
    outgoing = jnp.dot(
        choose, by_block.reshape(feature_blocks, rows * BLK), preferred_element_type=jnp.float32
    ).astype(jnp.bfloat16)
    picked = exchange(outgoing.reshape(peers, keep, rows * BLK), gather_route, Z_LANES)
    terms = [
        ffn_terms(
            picked[:, :, r * BLK : (r + 1) * BLK],
            gate_blocks,
            up_blocks,
            gate_scale,
            up_scale,
            down_blocks,
            down_scale,
        )
        for r in range(rows)
    ]
    arrived = exchange(jnp.concatenate(terms, axis=2), return_route, Z_LANES)
    placement = (blocks[:, None] == out_keep.reshape(1, peers * keep)).astype(jnp.bfloat16)
    summed = jnp.dot(
        placement, arrived.reshape(peers * keep, rows * BLK), preferred_element_type=jnp.float32
    )
    ffn_share = jnp.swapaxes(summed.reshape(feature_blocks, rows, BLK), 0, 1).reshape(rows, -1)
    return (middle + ffn_share).astype(jnp.bfloat16)


def solution(mesh):
    placed = (
        P("wide", "head"),
        P("wide", "head"),
        P("wide", "head"),
        P(None, "wide", None, "head"),
        P("wide", None),
        P("wide"),
        P("wide"),
        P(("wide", "head"), None),
        P(),
        P("wide", None, None, None),
        P("wide", None, None, None),
        P("wide", None),
        P("wide", None),
        P("wide", None),
        P("wide", None, None, None),
        P("wide", None),
        P("wide", None),
    )
    return jax.shard_map(
        per_device, mesh=mesh, in_specs=placed, out_specs=P(("wide", "head"), None), check_vma=False
    )
```

```python
import functools
import math

import jax
import jax.numpy as jnp
from jax import lax
from jax.experimental import pallas as pl
from jax.experimental.pallas import tpu as pltpu
from jax.sharding import PartitionSpec as P

HD = 128
BLK = 128
Z_LANES = 4


def copy_head(source_z, target_lane, source_core, lanes):
    offset = (source_z - target_lane + 2 * lanes) % (2 * lanes)
    upper = ((offset + 1) % (2 * lanes)) // lanes
    tie = ((offset % lanes) // 2) * (1 - (offset % lanes) % 2)
    return upper + tie * source_core * (1 - 2 * upper)


def gather_route(me, here, peer, lanes):
    source_z = (me // 2) % lanes + lanes * here
    return copy_head(source_z, (peer // 2) % lanes, me % 2, lanes)


def return_route(me, here, peer, lanes):
    first = copy_head((peer // 2) % lanes, (me // 2) % lanes, peer % 2, lanes)
    return (first + here) % 2


def exchange_kernel(route, lanes, x_ref, y_ref, send_sem, recv_sem, local_sem):
    me = lax.axis_index("wide")
    here = lax.axis_index("head")
    n = x_ref.shape[0]
    local = pltpu.make_async_copy(x_ref.at[me], y_ref.at[me], local_sem)
    local.start()

    def send(j, carry):
        peer = lax.rem(me + j, n)
        pltpu.make_async_remote_copy(
            src_ref=x_ref.at[peer],
            dst_ref=y_ref.at[me],
            send_sem=send_sem,
            recv_sem=recv_sem,
            device_id=(peer, route(me, here, peer, lanes)),
            device_id_type=pl.DeviceIdType.MESH,
        ).start()
        return carry

    lax.fori_loop(1, n, send, 0)
    every = pltpu.make_async_remote_copy(
        src_ref=x_ref.at[pl.ds(0, n - 1)],
        dst_ref=y_ref.at[pl.ds(0, n - 1)],
        send_sem=send_sem,
        recv_sem=recv_sem,
        device_id=(me, here),
        device_id_type=pl.DeviceIdType.MESH,
    )
    every.wait_send()
    every.wait_recv()
    local.wait()


def exchange(x, route, lanes):
    return pl.pallas_call(
        functools.partial(exchange_kernel, route, lanes),
        out_shape=jax.ShapeDtypeStruct(x.shape, x.dtype),
        in_specs=[pl.BlockSpec(memory_space=pl.ANY)],
        out_specs=pl.BlockSpec(memory_space=pl.ANY),
        scratch_shapes=[pltpu.SemaphoreType.DMA, pltpu.SemaphoreType.DMA, pltpu.SemaphoreType.DMA],
        compiler_params=pltpu.CompilerParams(has_side_effects=True),
    )(x)


def shifted(block, axis, distance):
    devices = range(lax.axis_size(axis))
    route = [(i - distance, i) for i in devices if i - distance in devices]
    return lax.ppermute(block, axis, route)


def attend(branch_query, key_new, value_new, pools, tables, lengths, source, row):
    row_count = branch_query.shape[0]
    groups = key_new.shape[1] // HD
    per_group = branch_query.shape[1] // (groups * HD)
    pages, page_size = pools[0].shape[1], pools[0].shape[2]
    queries = branch_query.reshape(row_count, groups, per_group, HD)
    own_keys = key_new.reshape(row_count, groups, HD)
    own_values = value_new.reshape(row_count, groups, HD)
    factor = 1.0 / math.sqrt(HD)
    page_ids = jnp.arange(pages, dtype=jnp.int32)
    slots = jnp.arange(tables[0].shape[1], dtype=jnp.int32)
    offsets = jnp.arange(page_size, dtype=jnp.int32)
    scores, masks = [], []
    for which, (pool, table, length) in enumerate(zip(pools, tables, lengths)):
        parent_table = table[row]
        match = parent_table[:, None, :] == page_ids[None, :, None]
        slot = jnp.sum(jnp.where(match, slots[None, None, :], 0), axis=-1)
        found = jnp.any(match, axis=-1) & (source == which)[:, None]
        live = found[:, :, None] & (
            slot[:, :, None] * page_size + offsets[None, None, :] < length[row][:, None, None]
        )
        keys = pool[0].reshape(pages * page_size, groups * HD)
        part = jnp.stack(
            [
                jnp.einsum(
                    "rjd,td->rjt",
                    queries[:, g],
                    keys[:, g * HD : (g + 1) * HD],
                    preferred_element_type=jnp.float32,
                )
                for g in range(groups)
            ],
            axis=1,
        ) * factor
        scores.append(part)
        masks.append(live.reshape(row_count, 1, 1, pages * page_size))
    tail_scores = jnp.concatenate(scores, axis=-1)
    live_mask = jnp.concatenate(masks, axis=-1)
    own_scores = (
        jnp.einsum("rgjd,rgd->rgj", queries, own_keys, preferred_element_type=jnp.float32) * factor
    )
    top_score = jnp.maximum(jnp.max(jnp.where(live_mask, tail_scores, -1e30), axis=-1), own_scores)
    tail_exp = jnp.where(live_mask, jnp.exp(tail_scores - top_score[..., None]), 0.0)
    own_exp = jnp.exp(own_scores - top_score)
    totals = jnp.sum(tail_exp, axis=-1) + own_exp
    tail_weights = (tail_exp / totals[..., None]).astype(jnp.bfloat16)
    own_weights = (own_exp / totals).astype(jnp.bfloat16)
    span = pages * page_size
    mixture = own_weights[..., None].astype(jnp.float32) * own_values[:, :, None, :].astype(
        jnp.float32
    )
    for which, pool in enumerate(pools):
        values = pool[1].reshape(span, groups * HD)
        weights = tail_weights[..., which * span : (which + 1) * span]
        mixture = mixture + jnp.stack(
            [
                jnp.einsum(
                    "rjt,td->rjd",
                    weights[:, g],
                    values[:, g * HD : (g + 1) * HD],
                    preferred_element_type=jnp.float32,
                )
                for g in range(groups)
            ],
            axis=1,
        )
    return mixture.reshape(row_count, -1).astype(jnp.bfloat16)


def hidden_units(picked, gate_blocks, up_blocks, gate_scale, up_scale):
    gate_part = jnp.einsum(
        "skd,kdf->ksf", picked, gate_blocks[0], preferred_element_type=jnp.float32
    )
    up_part = jnp.einsum("skd,kdf->ksf", picked, up_blocks[0], preferred_element_type=jnp.float32)
    gate_sum = jnp.sum(gate_part * gate_scale[0][:, None, None], axis=0)
    up_sum = jnp.sum(up_part * up_scale[0][:, None, None], axis=0)
    return (jax.nn.silu(gate_sum) * up_sum).astype(jnp.bfloat16)


def per_device(
    branch_query,
    key_new,
    value_new,
    pool_pages,
    page_table,
    tail_length,
    parent_row,
    residual,
    norm_gain,
    gate_blocks,
    up_blocks,
    gate_up_keep,
    gate_scale,
    up_scale,
    down_blocks,
    down_keep,
    down_scale,
):
    row_count = branch_query.shape[0]
    prior_pool, prior_meta = shifted(
        (pool_pages, jnp.concatenate([page_table, tail_length[:, None]], axis=1)), "wide", 1
    )
    prior = (prior_pool, prior_meta[:, :-1], prior_meta[:, -1])
    local_parent = parent_row - (lax.axis_index("wide") - 1) * row_count
    attention = attend(
        branch_query,
        key_new,
        value_new,
        (prior[0], pool_pages),
        (prior[1], page_table),
        (prior[2], tail_length),
        local_parent // row_count,
        local_parent % row_count,
    )
    half = residual.shape[0]
    here = lax.axis_index("head")
    mine = lax.dynamic_slice_in_dim(attention, here * half, half, axis=0)
    theirs = lax.dynamic_slice_in_dim(attention, (1 - here) * half, half, axis=0)
    arrived_half = lax.ppermute(theirs, "head", [(0, 1), (1, 0)])
    head_rows = jnp.where(
        here == 0,
        jnp.concatenate([mine, arrived_half], axis=1),
        jnp.concatenate([arrived_half, mine], axis=1),
    )
    middle = residual.astype(jnp.float32) + head_rows.astype(jnp.float32)
    normed = (
        middle * lax.rsqrt(jnp.mean(middle * middle, axis=-1, keepdims=True) + 1e-05) * norm_gain
    ).astype(jnp.bfloat16)
    peers = lax.axis_size("wide")
    own_lists = jnp.concatenate([gate_up_keep, down_keep], axis=1)
    keep_lists = lax.all_to_all(
        jnp.broadcast_to(own_lists, (peers, own_lists.shape[1])),
        "wide",
        split_axis=0,
        concat_axis=0,
        tiled=True,
    )
    keep = gate_up_keep.shape[1]
    in_keep, out_keep = keep_lists[:, :keep], keep_lists[:, keep:]
    feature_blocks = normed.shape[1] // BLK
    rows = normed.shape[0]
    blocks = jnp.arange(feature_blocks, dtype=jnp.int32)
    choose = (in_keep.reshape(peers * keep, 1) == blocks[None, :]).astype(jnp.bfloat16)
    by_block = jnp.swapaxes(normed.reshape(rows, feature_blocks, BLK), 0, 1)
    outgoing = jnp.dot(
        choose, by_block.reshape(feature_blocks, rows * BLK), preferred_element_type=jnp.float32
    ).astype(jnp.bfloat16)
    picked = exchange(outgoing.reshape(peers, keep, rows * BLK), gather_route, Z_LANES)
    hidden = jnp.concatenate(
        [
            hidden_units(
                picked[:, :, r * BLK : (r + 1) * BLK], gate_blocks, up_blocks, gate_scale, up_scale
            )
            for r in range(rows)
        ],
        axis=0,
    )
    down_flat = jnp.swapaxes(down_blocks[0], 0, 1).reshape(BLK, keep * BLK)
    down_part = jnp.dot(hidden, down_flat, preferred_element_type=jnp.float32)
    column_scale = jnp.repeat(down_scale[0], BLK)
    contrib = lax.optimization_barrier((down_part * column_scale[None, :]).astype(jnp.bfloat16))
    contrib = contrib.reshape(rows, peers, keep, BLK)
    outgoing_sums = jnp.concatenate([contrib[r] for r in range(rows)], axis=-1)
    arrived = exchange(outgoing_sums, return_route, Z_LANES)
    placement = (blocks[:, None] == out_keep.reshape(1, peers * keep)).astype(jnp.bfloat16)
    summed = jnp.stack(
        [
            jnp.dot(
                placement,
                arrived[:, :, r * BLK : (r + 1) * BLK].reshape(peers * keep, BLK),
                preferred_element_type=jnp.float32,
            )
            for r in range(rows)
        ],
        axis=0,
    )
    ffn_share = summed.reshape(rows, -1)
    return (middle + ffn_share).astype(jnp.bfloat16)


def solution(mesh):
    placed = (
        P("wide", "head"),
        P("wide", "head"),
        P("wide", "head"),
        P(None, "wide", None, "head"),
        P("wide", None),
        P("wide"),
        P("wide"),
        P(("wide", "head"), None),
        P(),
        P("wide", None, None, None),
        P("wide", None, None, None),
        P("wide", None),
        P("wide", None),
        P("wide", None),
        P("wide", None, None, None),
        P("wide", None),
        P("wide", None),
    )
    return jax.shard_map(
        per_device, mesh=mesh, in_specs=placed, out_specs=P(("wide", "head"), None), check_vma=False
    )
```

```python
import functools
import math

import jax
import jax.numpy as jnp
from jax import lax
from jax.experimental import pallas as pl
from jax.experimental.pallas import tpu as pltpu
from jax.sharding import PartitionSpec as P

HD = 128
BLK = 128
Z_LANES = 4


def copy_head(source_z, target_lane, source_core, lanes):
    offset = (source_z - target_lane + 2 * lanes) % (2 * lanes)
    upper = ((offset + 1) % (2 * lanes)) // lanes
    tie = ((offset % lanes) // 2) * (1 - (offset % lanes) % 2)
    return upper + tie * source_core * (1 - 2 * upper)


def gather_route(me, here, peer, lanes):
    source_z = (me // 2) % lanes + lanes * here
    return copy_head(source_z, (peer // 2) % lanes, me % 2, lanes)


def return_route(me, here, peer, lanes):
    first = copy_head((peer // 2) % lanes, (me // 2) % lanes, peer % 2, lanes)
    return (first + here) % 2


def exchange_kernel(route, lanes, x_ref, y_ref, send_sem, recv_sem, local_sem):
    me = lax.axis_index("wide")
    here = lax.axis_index("head")
    n = x_ref.shape[0]
    local = pltpu.make_async_copy(x_ref.at[me], y_ref.at[me], local_sem)
    local.start()

    def send(j, carry):
        peer = lax.rem(me + j, n)
        pltpu.make_async_remote_copy(
            src_ref=x_ref.at[peer],
            dst_ref=y_ref.at[me],
            send_sem=send_sem,
            recv_sem=recv_sem,
            device_id=(peer, route(me, here, peer, lanes)),
            device_id_type=pl.DeviceIdType.MESH,
        ).start()
        return carry

    lax.fori_loop(1, n, send, 0)
    every = pltpu.make_async_remote_copy(
        src_ref=x_ref.at[pl.ds(0, n - 1)],
        dst_ref=y_ref.at[pl.ds(0, n - 1)],
        send_sem=send_sem,
        recv_sem=recv_sem,
        device_id=(me, here),
        device_id_type=pl.DeviceIdType.MESH,
    )
    every.wait_send()
    every.wait_recv()
    local.wait()


def exchange(x, route, lanes):
    return pl.pallas_call(
        functools.partial(exchange_kernel, route, lanes),
        out_shape=jax.ShapeDtypeStruct(x.shape, x.dtype),
        in_specs=[pl.BlockSpec(memory_space=pl.ANY)],
        out_specs=pl.BlockSpec(memory_space=pl.ANY),
        scratch_shapes=[pltpu.SemaphoreType.DMA, pltpu.SemaphoreType.DMA, pltpu.SemaphoreType.DMA],
        compiler_params=pltpu.CompilerParams(has_side_effects=True),
    )(x)


def swap_kernel(lanes, half_ref, lists_ref, half_out, lists_out, sems):
    me = lax.axis_index("wide")
    here = lax.axis_index("head")
    n = lists_ref.shape[0]
    partner = pltpu.make_async_remote_copy(
        src_ref=half_ref,
        dst_ref=half_out,
        send_sem=sems.at[0],
        recv_sem=sems.at[1],
        device_id=(me, 1 - here),
        device_id_type=pl.DeviceIdType.MESH,
    )
    partner.start()
    local = pltpu.make_async_copy(lists_ref.at[me], lists_out.at[me], sems.at[4])
    local.start()

    def send(j, carry):
        peer = lax.rem(me + j, n)
        pltpu.make_async_remote_copy(
            src_ref=lists_ref.at[peer],
            dst_ref=lists_out.at[me],
            send_sem=sems.at[2],
            recv_sem=sems.at[3],
            device_id=(peer, return_route(me, here, peer, lanes)),
            device_id_type=pl.DeviceIdType.MESH,
        ).start()
        return carry

    lax.fori_loop(1, n, send, 0)
    every = pltpu.make_async_remote_copy(
        src_ref=lists_ref.at[pl.ds(0, n - 1)],
        dst_ref=lists_out.at[pl.ds(0, n - 1)],
        send_sem=sems.at[2],
        recv_sem=sems.at[3],
        device_id=(me, here),
        device_id_type=pl.DeviceIdType.MESH,
    )
    every.wait_send()
    every.wait_recv()
    partner.wait()
    local.wait()


def swap(half, lists, lanes):
    return pl.pallas_call(
        functools.partial(swap_kernel, lanes),
        out_shape=(
            jax.ShapeDtypeStruct(half.shape, half.dtype),
            jax.ShapeDtypeStruct(lists.shape, lists.dtype),
        ),
        in_specs=[pl.BlockSpec(memory_space=pl.ANY)] * 2,
        out_specs=(pl.BlockSpec(memory_space=pl.ANY),) * 2,
        scratch_shapes=[pltpu.SemaphoreType.DMA((5,))],
        compiler_params=pltpu.CompilerParams(has_side_effects=True),
    )(half, lists)


def shifted(block, axis, distance):
    devices = range(lax.axis_size(axis))
    route = [(i - distance, i) for i in devices if i - distance in devices]
    return lax.ppermute(block, axis, route)


def attend(branch_query, key_new, value_new, pools, tables, lengths, source, row):
    row_count = branch_query.shape[0]
    groups = key_new.shape[1] // HD
    per_group = branch_query.shape[1] // (groups * HD)
    pages, page_size = pools[0].shape[1], pools[0].shape[2]
    queries = branch_query.reshape(row_count, groups, per_group, HD)
    own_keys = key_new.reshape(row_count, groups, HD)
    own_values = value_new.reshape(row_count, groups, HD)
    factor = 1.0 / math.sqrt(HD)
    page_ids = jnp.arange(pages, dtype=jnp.int32)
    slots = jnp.arange(tables[0].shape[1], dtype=jnp.int32)
    offsets = jnp.arange(page_size, dtype=jnp.int32)
    scores, masks = [], []
    for which, (pool, table, length) in enumerate(zip(pools, tables, lengths)):
        parent_table = table[row]
        match = parent_table[:, None, :] == page_ids[None, :, None]
        slot = jnp.sum(jnp.where(match, slots[None, None, :], 0), axis=-1)
        found = jnp.any(match, axis=-1) & (source == which)[:, None]
        live = found[:, :, None] & (
            slot[:, :, None] * page_size + offsets[None, None, :] < length[row][:, None, None]
        )
        keys = pool[0].reshape(pages * page_size, groups * HD)
        part = jnp.stack(
            [
                jnp.einsum(
                    "rjd,td->rjt",
                    queries[:, g],
                    keys[:, g * HD : (g + 1) * HD],
                    preferred_element_type=jnp.float32,
                )
                for g in range(groups)
            ],
            axis=1,
        ) * factor
        scores.append(part)
        masks.append(live.reshape(row_count, 1, 1, pages * page_size))
    tail_scores = jnp.concatenate(scores, axis=-1)
    live_mask = jnp.concatenate(masks, axis=-1)
    own_scores = (
        jnp.einsum("rgjd,rgd->rgj", queries, own_keys, preferred_element_type=jnp.float32) * factor
    )
    top_score = jnp.maximum(jnp.max(jnp.where(live_mask, tail_scores, -1e30), axis=-1), own_scores)
    tail_exp = jnp.where(live_mask, jnp.exp(tail_scores - top_score[..., None]), 0.0)
    own_exp = jnp.exp(own_scores - top_score)
    totals = jnp.sum(tail_exp, axis=-1) + own_exp
    tail_weights = (tail_exp / totals[..., None]).astype(jnp.bfloat16)
    own_weights = (own_exp / totals).astype(jnp.bfloat16)
    span = pages * page_size
    mixture = own_weights[..., None].astype(jnp.float32) * own_values[:, :, None, :].astype(
        jnp.float32
    )
    for which, pool in enumerate(pools):
        values = pool[1].reshape(span, groups * HD)
        weights = tail_weights[..., which * span : (which + 1) * span]
        mixture = mixture + jnp.stack(
            [
                jnp.einsum(
                    "rjt,td->rjd",
                    weights[:, g],
                    values[:, g * HD : (g + 1) * HD],
                    preferred_element_type=jnp.float32,
                )
                for g in range(groups)
            ],
            axis=1,
        )
    return mixture.reshape(row_count, -1).astype(jnp.bfloat16)


def hidden_units(picked, gate_blocks, up_blocks, gate_scale, up_scale):
    gate_part = jnp.einsum(
        "skd,kdf->ksf", picked, gate_blocks[0], preferred_element_type=jnp.float32
    )
    up_part = jnp.einsum("skd,kdf->ksf", picked, up_blocks[0], preferred_element_type=jnp.float32)
    gate_sum = jnp.sum(gate_part * gate_scale[0][:, None, None], axis=0)
    up_sum = jnp.sum(up_part * up_scale[0][:, None, None], axis=0)
    return (jax.nn.silu(gate_sum) * up_sum).astype(jnp.bfloat16)


def per_device(
    branch_query,
    key_new,
    value_new,
    pool_pages,
    page_table,
    tail_length,
    parent_row,
    residual,
    norm_gain,
    gate_blocks,
    up_blocks,
    gate_up_keep,
    gate_scale,
    up_scale,
    down_blocks,
    down_keep,
    down_scale,
):
    row_count = branch_query.shape[0]
    prior_pool, prior_meta = shifted(
        (pool_pages, jnp.concatenate([page_table, tail_length[:, None]], axis=1)), "wide", 1
    )
    prior = (prior_pool, prior_meta[:, :-1], prior_meta[:, -1])
    local_parent = parent_row - (lax.axis_index("wide") - 1) * row_count
    attention = attend(
        branch_query,
        key_new,
        value_new,
        (prior[0], pool_pages),
        (prior[1], page_table),
        (prior[2], tail_length),
        local_parent // row_count,
        local_parent % row_count,
    )
    half = residual.shape[0]
    here = lax.axis_index("head")
    mine = lax.dynamic_slice_in_dim(attention, here * half, half, axis=0)
    theirs = lax.dynamic_slice_in_dim(attention, (1 - here) * half, half, axis=0)
    peers = lax.axis_size("wide")
    own_lists = jnp.concatenate([gate_up_keep, down_keep], axis=1)
    list_width = own_lists.shape[1]
    padded = jnp.pad(own_lists, ((0, 7), (0, BLK - list_width)))
    arrived_half, keep_lists = swap(
        theirs, jnp.broadcast_to(padded, (peers,) + padded.shape), Z_LANES
    )
    keep_lists = keep_lists[:, 0, :list_width]
    head_rows = jnp.where(
        here == 0,
        jnp.concatenate([mine, arrived_half], axis=1),
        jnp.concatenate([arrived_half, mine], axis=1),
    )
    middle = residual.astype(jnp.float32) + head_rows.astype(jnp.float32)
    normed = (
        middle * lax.rsqrt(jnp.mean(middle * middle, axis=-1, keepdims=True) + 1e-05) * norm_gain
    ).astype(jnp.bfloat16)
    keep = gate_up_keep.shape[1]
    in_keep, out_keep = keep_lists[:, :keep], keep_lists[:, keep:]
    feature_blocks = normed.shape[1] // BLK
    rows = normed.shape[0]
    blocks = jnp.arange(feature_blocks, dtype=jnp.int32)
    choose = (in_keep.reshape(peers * keep, 1) == blocks[None, :]).astype(jnp.bfloat16)
    by_block = jnp.swapaxes(normed.reshape(rows, feature_blocks, BLK), 0, 1)
    outgoing = jnp.dot(
        choose, by_block.reshape(feature_blocks, rows * BLK), preferred_element_type=jnp.float32
    ).astype(jnp.bfloat16)
    picked = exchange(outgoing.reshape(peers, keep, rows * BLK), gather_route, Z_LANES)
    hidden = jnp.concatenate(
        [
            hidden_units(
                picked[:, :, r * BLK : (r + 1) * BLK], gate_blocks, up_blocks, gate_scale, up_scale
            )
            for r in range(rows)
        ],
        axis=0,
    )
    down_flat = jnp.swapaxes(down_blocks[0], 0, 1).reshape(BLK, keep * BLK)
    down_part = jnp.dot(hidden, down_flat, preferred_element_type=jnp.float32)
    column_scale = jnp.repeat(down_scale[0], BLK)
    contrib = lax.optimization_barrier((down_part * column_scale[None, :]).astype(jnp.bfloat16))
    contrib = contrib.reshape(rows, peers, keep, BLK)
    outgoing_sums = jnp.concatenate([contrib[r] for r in range(rows)], axis=-1)
    arrived = exchange(outgoing_sums, return_route, Z_LANES)
    placement = (blocks[:, None] == out_keep.reshape(1, peers * keep)).astype(jnp.bfloat16)
    summed = jnp.stack(
        [
            jnp.dot(
                placement,
                arrived[:, :, r * BLK : (r + 1) * BLK].reshape(peers * keep, BLK),
                preferred_element_type=jnp.float32,
            )
            for r in range(rows)
        ],
        axis=0,
    )
    ffn_share = summed.reshape(rows, -1)
    return (middle + ffn_share).astype(jnp.bfloat16)


def solution(mesh):
    placed = (
        P("wide", "head"),
        P("wide", "head"),
        P("wide", "head"),
        P(None, "wide", None, "head"),
        P("wide", None),
        P("wide"),
        P("wide"),
        P(("wide", "head"), None),
        P(),
        P("wide", None, None, None),
        P("wide", None, None, None),
        P("wide", None),
        P("wide", None),
        P("wide", None),
        P("wide", None, None, None),
        P("wide", None),
        P("wide", None),
    )
    return jax.shard_map(
        per_device, mesh=mesh, in_specs=placed, out_specs=P(("wide", "head"), None), check_vma=False
    )
```

```python
import functools
import math

import jax
import jax.numpy as jnp
from jax import lax
from jax.experimental import pallas as pl
from jax.experimental.pallas import tpu as pltpu
from jax.sharding import PartitionSpec as P

HD = 128
BLK = 128
Z_LANES = 4


def copy_head(source_z, target_lane, source_core, lanes):
    offset = (source_z - target_lane + 2 * lanes) % (2 * lanes)
    upper = ((offset + 1) % (2 * lanes)) // lanes
    tie = ((offset % lanes) // 2) * (1 - (offset % lanes) % 2)
    return upper + tie * source_core * (1 - 2 * upper)


def gather_route(me, here, peer, lanes):
    source_z = (me // 2) % lanes + lanes * here
    return copy_head(source_z, (peer // 2) % lanes, me % 2, lanes)


def return_route(me, here, peer, lanes):
    first = copy_head((peer // 2) % lanes, (me // 2) % lanes, peer % 2, lanes)
    return (first + here) % 2


def exchange_kernel(route, lanes, x_ref, y_ref, send_sem, recv_sem, local_sem):
    me = lax.axis_index("wide")
    here = lax.axis_index("head")
    n = x_ref.shape[0]
    local = pltpu.make_async_copy(x_ref.at[me], y_ref.at[me], local_sem)
    local.start()

    def send(j, carry):
        peer = lax.rem(me + j, n)
        pltpu.make_async_remote_copy(
            src_ref=x_ref.at[peer],
            dst_ref=y_ref.at[me],
            send_sem=send_sem,
            recv_sem=recv_sem,
            device_id=(peer, route(me, here, peer, lanes)),
            device_id_type=pl.DeviceIdType.MESH,
        ).start()
        return carry

    lax.fori_loop(1, n, send, 0)
    every = pltpu.make_async_remote_copy(
        src_ref=x_ref.at[pl.ds(0, n - 1)],
        dst_ref=y_ref.at[pl.ds(0, n - 1)],
        send_sem=send_sem,
        recv_sem=recv_sem,
        device_id=(me, here),
        device_id_type=pl.DeviceIdType.MESH,
    )
    every.wait_send()
    every.wait_recv()
    local.wait()


def exchange(x, route, lanes):
    return pl.pallas_call(
        functools.partial(exchange_kernel, route, lanes),
        out_shape=jax.ShapeDtypeStruct(x.shape, x.dtype),
        in_specs=[pl.BlockSpec(memory_space=pl.ANY)],
        out_specs=pl.BlockSpec(memory_space=pl.ANY),
        scratch_shapes=[pltpu.SemaphoreType.DMA, pltpu.SemaphoreType.DMA, pltpu.SemaphoreType.DMA],
        compiler_params=pltpu.CompilerParams(has_side_effects=True),
    )(x)


def staged_kernel(route, lanes, x_ref, y_ref, mid_ref, sems):
    me = lax.axis_index("wide")
    here = lax.axis_index("head")
    inner, outer = x_ref.shape[0], x_ref.shape[1]
    near, far = me % inner, me // inner
    first_local = pltpu.make_async_copy(x_ref.at[near], mid_ref.at[near], sems.at[0])
    first_local.start()

    def first(j, carry):
        part = lax.rem(near + j, inner)
        peer = far * inner + part
        pltpu.make_async_remote_copy(
            src_ref=x_ref.at[part],
            dst_ref=mid_ref.at[near],
            send_sem=sems.at[1],
            recv_sem=sems.at[2],
            device_id=(peer, route(me, here, peer, lanes)),
            device_id_type=pl.DeviceIdType.MESH,
        ).start()
        return carry

    lax.fori_loop(1, inner, first, 0)
    first_all = pltpu.make_async_remote_copy(
        src_ref=mid_ref.at[pl.ds(0, inner - 1)],
        dst_ref=mid_ref.at[pl.ds(0, inner - 1)],
        send_sem=sems.at[1],
        recv_sem=sems.at[2],
        device_id=(me, here),
        device_id_type=pl.DeviceIdType.MESH,
    )
    first_all.wait_recv()
    first_local.wait()
    second_local = pltpu.make_async_copy(mid_ref.at[:, far], y_ref.at[far], sems.at[3])
    second_local.start()

    def second(j, carry):
        part = lax.rem(far + j, outer)
        pltpu.make_async_remote_copy(
            src_ref=mid_ref.at[:, part],
            dst_ref=y_ref.at[far],
            send_sem=sems.at[4],
            recv_sem=sems.at[5],
            device_id=(part * inner + near, here),
            device_id_type=pl.DeviceIdType.MESH,
        ).start()
        return carry

    lax.fori_loop(1, outer, second, 0)
    second_all = pltpu.make_async_remote_copy(
        src_ref=y_ref.at[pl.ds(0, outer - 1)],
        dst_ref=y_ref.at[pl.ds(0, outer - 1)],
        send_sem=sems.at[4],
        recv_sem=sems.at[5],
        device_id=(me, here),
        device_id_type=pl.DeviceIdType.MESH,
    )
    second_all.wait_recv()
    second_all.wait_send()
    first_all.wait_send()
    second_local.wait()


def staged_exchange(x, route, lanes):
    peers, depth, width = x.shape
    inner = 2 * lanes
    outer = peers // inner
    by_part = jnp.swapaxes(x.reshape(outer, inner, depth, width), 0, 1)
    y, _ = pl.pallas_call(
        functools.partial(staged_kernel, route, lanes),
        out_shape=(
            jax.ShapeDtypeStruct((outer, inner, depth, width), x.dtype),
            jax.ShapeDtypeStruct((inner, outer, depth, width), x.dtype),
        ),
        in_specs=[pl.BlockSpec(memory_space=pl.ANY)],
        out_specs=(pl.BlockSpec(memory_space=pl.ANY),) * 2,
        scratch_shapes=[pltpu.SemaphoreType.DMA((6,))],
        compiler_params=pltpu.CompilerParams(has_side_effects=True),
    )(by_part)
    return y.reshape(peers, depth, width)


def shifted(block, axis, distance):
    devices = range(lax.axis_size(axis))
    route = [(i - distance, i) for i in devices if i - distance in devices]
    return lax.ppermute(block, axis, route)


def attend(branch_query, key_new, value_new, pools, tables, lengths, source, row):
    row_count = branch_query.shape[0]
    groups = key_new.shape[1] // HD
    per_group = branch_query.shape[1] // (groups * HD)
    pages, page_size = pools[0].shape[1], pools[0].shape[2]
    queries = branch_query.reshape(row_count, groups, per_group, HD)
    own_keys = key_new.reshape(row_count, groups, HD)
    own_values = value_new.reshape(row_count, groups, HD)
    factor = 1.0 / math.sqrt(HD)
    page_ids = jnp.arange(pages, dtype=jnp.int32)
    slots = jnp.arange(tables[0].shape[1], dtype=jnp.int32)
    offsets = jnp.arange(page_size, dtype=jnp.int32)
    scores, masks = [], []
    for which, (pool, table, length) in enumerate(zip(pools, tables, lengths)):
        parent_table = table[row]
        match = parent_table[:, None, :] == page_ids[None, :, None]
        slot = jnp.sum(jnp.where(match, slots[None, None, :], 0), axis=-1)
        found = jnp.any(match, axis=-1) & (source == which)[:, None]
        live = found[:, :, None] & (
            slot[:, :, None] * page_size + offsets[None, None, :] < length[row][:, None, None]
        )
        keys = pool[0].reshape(pages * page_size, groups * HD)
        part = jnp.stack(
            [
                jnp.einsum(
                    "rjd,td->rjt",
                    queries[:, g],
                    keys[:, g * HD : (g + 1) * HD],
                    preferred_element_type=jnp.float32,
                )
                for g in range(groups)
            ],
            axis=1,
        ) * factor
        scores.append(part)
        masks.append(live.reshape(row_count, 1, 1, pages * page_size))
    tail_scores = jnp.concatenate(scores, axis=-1)
    live_mask = jnp.concatenate(masks, axis=-1)
    own_scores = (
        jnp.einsum("rgjd,rgd->rgj", queries, own_keys, preferred_element_type=jnp.float32) * factor
    )
    top_score = jnp.maximum(jnp.max(jnp.where(live_mask, tail_scores, -1e30), axis=-1), own_scores)
    tail_exp = jnp.where(live_mask, jnp.exp(tail_scores - top_score[..., None]), 0.0)
    own_exp = jnp.exp(own_scores - top_score)
    totals = jnp.sum(tail_exp, axis=-1) + own_exp
    tail_weights = (tail_exp / totals[..., None]).astype(jnp.bfloat16)
    own_weights = (own_exp / totals).astype(jnp.bfloat16)
    span = pages * page_size
    mixture = own_weights[..., None].astype(jnp.float32) * own_values[:, :, None, :].astype(
        jnp.float32
    )
    for which, pool in enumerate(pools):
        values = pool[1].reshape(span, groups * HD)
        weights = tail_weights[..., which * span : (which + 1) * span]
        mixture = mixture + jnp.stack(
            [
                jnp.einsum(
                    "rjt,td->rjd",
                    weights[:, g],
                    values[:, g * HD : (g + 1) * HD],
                    preferred_element_type=jnp.float32,
                )
                for g in range(groups)
            ],
            axis=1,
        )
    return mixture.reshape(row_count, -1).astype(jnp.bfloat16)


def hidden_units(picked, gate_blocks, up_blocks, gate_scale, up_scale):
    gate_part = jnp.einsum(
        "skd,kdf->ksf", picked, gate_blocks[0], preferred_element_type=jnp.float32
    )
    up_part = jnp.einsum("skd,kdf->ksf", picked, up_blocks[0], preferred_element_type=jnp.float32)
    gate_sum = jnp.sum(gate_part * gate_scale[0][:, None, None], axis=0)
    up_sum = jnp.sum(up_part * up_scale[0][:, None, None], axis=0)
    return (jax.nn.silu(gate_sum) * up_sum).astype(jnp.bfloat16)


def per_device(
    branch_query,
    key_new,
    value_new,
    pool_pages,
    page_table,
    tail_length,
    parent_row,
    residual,
    norm_gain,
    gate_blocks,
    up_blocks,
    gate_up_keep,
    gate_scale,
    up_scale,
    down_blocks,
    down_keep,
    down_scale,
):
    row_count = branch_query.shape[0]
    prior_pool, prior_meta = shifted(
        (pool_pages, jnp.concatenate([page_table, tail_length[:, None]], axis=1)), "wide", 1
    )
    prior = (prior_pool, prior_meta[:, :-1], prior_meta[:, -1])
    local_parent = parent_row - (lax.axis_index("wide") - 1) * row_count
    attention = attend(
        branch_query,
        key_new,
        value_new,
        (prior[0], pool_pages),
        (prior[1], page_table),
        (prior[2], tail_length),
        local_parent // row_count,
        local_parent % row_count,
    )
    half = residual.shape[0]
    here = lax.axis_index("head")
    mine = lax.dynamic_slice_in_dim(attention, here * half, half, axis=0)
    theirs = lax.dynamic_slice_in_dim(attention, (1 - here) * half, half, axis=0)
    arrived_half = lax.ppermute(theirs, "head", [(0, 1), (1, 0)])
    head_rows = jnp.where(
        here == 0,
        jnp.concatenate([mine, arrived_half], axis=1),
        jnp.concatenate([arrived_half, mine], axis=1),
    )
    middle = residual.astype(jnp.float32) + head_rows.astype(jnp.float32)
    normed = (
        middle * lax.rsqrt(jnp.mean(middle * middle, axis=-1, keepdims=True) + 1e-05) * norm_gain
    ).astype(jnp.bfloat16)
    peers = lax.axis_size("wide")
    own_lists = jnp.concatenate([gate_up_keep, down_keep], axis=1)
    keep_lists = lax.all_to_all(
        jnp.broadcast_to(own_lists, (peers, own_lists.shape[1])),
        "wide",
        split_axis=0,
        concat_axis=0,
        tiled=True,
    )
    keep = gate_up_keep.shape[1]
    in_keep, out_keep = keep_lists[:, :keep], keep_lists[:, keep:]
    feature_blocks = normed.shape[1] // BLK
    rows = normed.shape[0]
    blocks = jnp.arange(feature_blocks, dtype=jnp.int32)
    choose = (in_keep.reshape(peers * keep, 1) == blocks[None, :]).astype(jnp.bfloat16)
    by_block = jnp.swapaxes(normed.reshape(rows, feature_blocks, BLK), 0, 1)
    outgoing = jnp.dot(
        choose, by_block.reshape(feature_blocks, rows * BLK), preferred_element_type=jnp.float32
    ).astype(jnp.bfloat16)
    picked = staged_exchange(outgoing.reshape(peers, keep, rows * BLK), gather_route, Z_LANES)
    hidden = jnp.concatenate(
        [
            hidden_units(
                picked[:, :, r * BLK : (r + 1) * BLK], gate_blocks, up_blocks, gate_scale, up_scale
            )
            for r in range(rows)
        ],
        axis=0,
    )
    down_flat = jnp.swapaxes(down_blocks[0], 0, 1).reshape(BLK, keep * BLK)
    down_part = jnp.dot(hidden, down_flat, preferred_element_type=jnp.float32)
    column_scale = jnp.repeat(down_scale[0], BLK)
    contrib = lax.optimization_barrier((down_part * column_scale[None, :]).astype(jnp.bfloat16))
    contrib = contrib.reshape(rows, peers, keep, BLK)
    outgoing_sums = jnp.concatenate([contrib[r] for r in range(rows)], axis=-1)
    arrived = staged_exchange(outgoing_sums, return_route, Z_LANES)
    placement = (blocks[:, None] == out_keep.reshape(1, peers * keep)).astype(jnp.bfloat16)
    summed = jnp.stack(
        [
            jnp.dot(
                placement,
                arrived[:, :, r * BLK : (r + 1) * BLK].reshape(peers * keep, BLK),
                preferred_element_type=jnp.float32,
            )
            for r in range(rows)
        ],
        axis=0,
    )
    ffn_share = summed.reshape(rows, -1)
    return (middle + ffn_share).astype(jnp.bfloat16)


def solution(mesh):
    placed = (
        P("wide", "head"),
        P("wide", "head"),
        P("wide", "head"),
        P(None, "wide", None, "head"),
        P("wide", None),
        P("wide"),
        P("wide"),
        P(("wide", "head"), None),
        P(),
        P("wide", None, None, None),
        P("wide", None, None, None),
        P("wide", None),
        P("wide", None),
        P("wide", None),
        P("wide", None, None, None),
        P("wide", None),
        P("wide", None),
    )
    return jax.shard_map(
        per_device, mesh=mesh, in_specs=placed, out_specs=P(("wide", "head"), None), check_vma=False
    )
```

```python
import functools
import math

import jax
import jax.numpy as jnp
from jax import lax
from jax.experimental import pallas as pl
from jax.experimental.pallas import tpu as pltpu
from jax.sharding import PartitionSpec as P

HD = 128
BLK = 128
Z_LANES = 4


def copy_head(source_z, target_lane, source_core, lanes):
    offset = (source_z - target_lane + 2 * lanes) % (2 * lanes)
    upper = ((offset + 1) % (2 * lanes)) // lanes
    tie = ((offset % lanes) // 2) * (1 - (offset % lanes) % 2)
    return upper + tie * source_core * (1 - 2 * upper)


def gather_route(me, here, peer, lanes):
    source_z = (me // 2) % lanes + lanes * here
    return copy_head(source_z, (peer // 2) % lanes, me % 2, lanes)


def return_route(me, here, peer, lanes):
    first = copy_head((peer // 2) % lanes, (me // 2) % lanes, peer % 2, lanes)
    return (first + here) % 2


def exchange_kernel(route, lanes, x_ref, y_ref, send_sem, recv_sem, local_sem):
    me = lax.axis_index("wide")
    here = lax.axis_index("head")
    n = x_ref.shape[0]
    ways = send_sem.shape[0]
    local = pltpu.make_async_copy(x_ref.at[me], y_ref.at[me], local_sem)
    local.start()
    for way in range(ways):

        def send(step, carry, way=way):
            peer = lax.rem(me + step * ways + way, n)
            pltpu.make_async_remote_copy(
                src_ref=x_ref.at[peer],
                dst_ref=y_ref.at[me],
                send_sem=send_sem.at[way],
                recv_sem=recv_sem.at[way],
                device_id=(peer, route(me, here, peer, lanes)),
                device_id_type=pl.DeviceIdType.MESH,
            ).start()
            return carry

        lax.fori_loop(1 if way == 0 else 0, (n - way + ways - 1) // ways, send, 0)
    for way in range(ways):
        count = (n - way + ways - 1) // ways - (1 if way == 0 else 0)
        every = pltpu.make_async_remote_copy(
            src_ref=x_ref.at[pl.ds(0, count)],
            dst_ref=y_ref.at[pl.ds(0, count)],
            send_sem=send_sem.at[way],
            recv_sem=recv_sem.at[way],
            device_id=(me, here),
            device_id_type=pl.DeviceIdType.MESH,
        )
        every.wait_send()
        every.wait_recv()
    local.wait()


def exchange(x, route, lanes, ways=8):
    return pl.pallas_call(
        functools.partial(exchange_kernel, route, lanes),
        out_shape=jax.ShapeDtypeStruct(x.shape, x.dtype),
        in_specs=[pl.BlockSpec(memory_space=pl.ANY)],
        out_specs=pl.BlockSpec(memory_space=pl.ANY),
        scratch_shapes=[
            pltpu.SemaphoreType.DMA((ways,)),
            pltpu.SemaphoreType.DMA((ways,)),
            pltpu.SemaphoreType.DMA,
        ],
        compiler_params=pltpu.CompilerParams(has_side_effects=True),
    )(x)


def shifted(block, axis, distance):
    devices = range(lax.axis_size(axis))
    route = [(i - distance, i) for i in devices if i - distance in devices]
    return lax.ppermute(block, axis, route)


def attend(branch_query, key_new, value_new, pools, tables, lengths, source, row):
    row_count = branch_query.shape[0]
    groups = key_new.shape[1] // HD
    per_group = branch_query.shape[1] // (groups * HD)
    pages, page_size = pools[0].shape[1], pools[0].shape[2]
    queries = branch_query.reshape(row_count, groups, per_group, HD)
    own_keys = key_new.reshape(row_count, groups, HD)
    own_values = value_new.reshape(row_count, groups, HD)
    factor = 1.0 / math.sqrt(HD)
    page_ids = jnp.arange(pages, dtype=jnp.int32)
    slots = jnp.arange(tables[0].shape[1], dtype=jnp.int32)
    offsets = jnp.arange(page_size, dtype=jnp.int32)
    scores, masks = [], []
    for which, (pool, table, length) in enumerate(zip(pools, tables, lengths)):
        parent_table = table[row]
        match = parent_table[:, None, :] == page_ids[None, :, None]
        slot = jnp.sum(jnp.where(match, slots[None, None, :], 0), axis=-1)
        found = jnp.any(match, axis=-1) & (source == which)[:, None]
        live = found[:, :, None] & (
            slot[:, :, None] * page_size + offsets[None, None, :] < length[row][:, None, None]
        )
        keys = pool[0].reshape(pages * page_size, groups * HD)
        part = jnp.stack(
            [
                jnp.einsum(
                    "rjd,td->rjt",
                    queries[:, g],
                    keys[:, g * HD : (g + 1) * HD],
                    preferred_element_type=jnp.float32,
                )
                for g in range(groups)
            ],
            axis=1,
        ) * factor
        scores.append(part)
        masks.append(live.reshape(row_count, 1, 1, pages * page_size))
    tail_scores = jnp.concatenate(scores, axis=-1)
    live_mask = jnp.concatenate(masks, axis=-1)
    own_scores = (
        jnp.einsum("rgjd,rgd->rgj", queries, own_keys, preferred_element_type=jnp.float32) * factor
    )
    top_score = jnp.maximum(jnp.max(jnp.where(live_mask, tail_scores, -1e30), axis=-1), own_scores)
    tail_exp = jnp.where(live_mask, jnp.exp(tail_scores - top_score[..., None]), 0.0)
    own_exp = jnp.exp(own_scores - top_score)
    totals = jnp.sum(tail_exp, axis=-1) + own_exp
    tail_weights = (tail_exp / totals[..., None]).astype(jnp.bfloat16)
    own_weights = (own_exp / totals).astype(jnp.bfloat16)
    span = pages * page_size
    mixture = own_weights[..., None].astype(jnp.float32) * own_values[:, :, None, :].astype(
        jnp.float32
    )
    for which, pool in enumerate(pools):
        values = pool[1].reshape(span, groups * HD)
        weights = tail_weights[..., which * span : (which + 1) * span]
        mixture = mixture + jnp.stack(
            [
                jnp.einsum(
                    "rjt,td->rjd",
                    weights[:, g],
                    values[:, g * HD : (g + 1) * HD],
                    preferred_element_type=jnp.float32,
                )
                for g in range(groups)
            ],
            axis=1,
        )
    return mixture.reshape(row_count, -1).astype(jnp.bfloat16)


def hidden_units(picked, gate_blocks, up_blocks, gate_scale, up_scale):
    gate_part = jnp.einsum(
        "skd,kdf->ksf", picked, gate_blocks[0], preferred_element_type=jnp.float32
    )
    up_part = jnp.einsum("skd,kdf->ksf", picked, up_blocks[0], preferred_element_type=jnp.float32)
    gate_sum = jnp.sum(gate_part * gate_scale[0][:, None, None], axis=0)
    up_sum = jnp.sum(up_part * up_scale[0][:, None, None], axis=0)
    return (jax.nn.silu(gate_sum) * up_sum).astype(jnp.bfloat16)


def per_device(
    branch_query,
    key_new,
    value_new,
    pool_pages,
    page_table,
    tail_length,
    parent_row,
    residual,
    norm_gain,
    gate_blocks,
    up_blocks,
    gate_up_keep,
    gate_scale,
    up_scale,
    down_blocks,
    down_keep,
    down_scale,
):
    row_count = branch_query.shape[0]
    prior_pool, prior_meta = shifted(
        (pool_pages, jnp.concatenate([page_table, tail_length[:, None]], axis=1)), "wide", 1
    )
    prior = (prior_pool, prior_meta[:, :-1], prior_meta[:, -1])
    local_parent = parent_row - (lax.axis_index("wide") - 1) * row_count
    attention = attend(
        branch_query,
        key_new,
        value_new,
        (prior[0], pool_pages),
        (prior[1], page_table),
        (prior[2], tail_length),
        local_parent // row_count,
        local_parent % row_count,
    )
    half = residual.shape[0]
    here = lax.axis_index("head")
    mine = lax.dynamic_slice_in_dim(attention, here * half, half, axis=0)
    theirs = lax.dynamic_slice_in_dim(attention, (1 - here) * half, half, axis=0)
    arrived_half = lax.ppermute(theirs, "head", [(0, 1), (1, 0)])
    head_rows = jnp.where(
        here == 0,
        jnp.concatenate([mine, arrived_half], axis=1),
        jnp.concatenate([arrived_half, mine], axis=1),
    )
    middle = residual.astype(jnp.float32) + head_rows.astype(jnp.float32)
    normed = (
        middle * lax.rsqrt(jnp.mean(middle * middle, axis=-1, keepdims=True) + 1e-05) * norm_gain
    ).astype(jnp.bfloat16)
    peers = lax.axis_size("wide")
    own_lists = jnp.concatenate([gate_up_keep, down_keep], axis=1)
    keep_lists = lax.all_to_all(
        jnp.broadcast_to(own_lists, (peers, own_lists.shape[1])),
        "wide",
        split_axis=0,
        concat_axis=0,
        tiled=True,
    )
    keep = gate_up_keep.shape[1]
    in_keep, out_keep = keep_lists[:, :keep], keep_lists[:, keep:]
    feature_blocks = normed.shape[1] // BLK
    rows = normed.shape[0]
    blocks = jnp.arange(feature_blocks, dtype=jnp.int32)
    choose = (in_keep.reshape(peers * keep, 1) == blocks[None, :]).astype(jnp.bfloat16)
    by_block = jnp.swapaxes(normed.reshape(rows, feature_blocks, BLK), 0, 1)
    outgoing = jnp.dot(
        choose, by_block.reshape(feature_blocks, rows * BLK), preferred_element_type=jnp.float32
    ).astype(jnp.bfloat16)
    picked = exchange(outgoing.reshape(peers, keep, rows * BLK), gather_route, Z_LANES)
    hidden = jnp.concatenate(
        [
            hidden_units(
                picked[:, :, r * BLK : (r + 1) * BLK], gate_blocks, up_blocks, gate_scale, up_scale
            )
            for r in range(rows)
        ],
        axis=0,
    )
    down_flat = jnp.swapaxes(down_blocks[0], 0, 1).reshape(BLK, keep * BLK)
    down_part = jnp.dot(hidden, down_flat, preferred_element_type=jnp.float32)
    column_scale = jnp.repeat(down_scale[0], BLK)
    contrib = lax.optimization_barrier((down_part * column_scale[None, :]).astype(jnp.bfloat16))
    contrib = contrib.reshape(rows, peers, keep, BLK)
    outgoing_sums = jnp.concatenate([contrib[r] for r in range(rows)], axis=-1)
    arrived = exchange(outgoing_sums, return_route, Z_LANES)
    placement = (blocks[:, None] == out_keep.reshape(1, peers * keep)).astype(jnp.bfloat16)
    summed = jnp.stack(
        [
            jnp.dot(
                placement,
                arrived[:, :, r * BLK : (r + 1) * BLK].reshape(peers * keep, BLK),
                preferred_element_type=jnp.float32,
            )
            for r in range(rows)
        ],
        axis=0,
    )
    ffn_share = summed.reshape(rows, -1)
    return (middle + ffn_share).astype(jnp.bfloat16)


def solution(mesh):
    placed = (
        P("wide", "head"),
        P("wide", "head"),
        P("wide", "head"),
        P(None, "wide", None, "head"),
        P("wide", None),
        P("wide"),
        P("wide"),
        P(("wide", "head"), None),
        P(),
        P("wide", None, None, None),
        P("wide", None, None, None),
        P("wide", None),
        P("wide", None),
        P("wide", None),
        P("wide", None, None, None),
        P("wide", None),
        P("wide", None),
    )
    return jax.shard_map(
        per_device, mesh=mesh, in_specs=placed, out_specs=P(("wide", "head"), None), check_vma=False
    )
```

```python
import functools
import math

import jax
import jax.numpy as jnp
from jax import lax
from jax.experimental import pallas as pl
from jax.experimental.pallas import tpu as pltpu
from jax.sharding import PartitionSpec as P

HD = 128
BLK = 128
Z_LANES = 4


def copy_head(source_z, target_lane, source_core, lanes):
    offset = (source_z - target_lane + 2 * lanes) % (2 * lanes)
    upper = ((offset + 1) % (2 * lanes)) // lanes
    tie = ((offset % lanes) // 2) * (1 - (offset % lanes) % 2)
    return upper + tie * source_core * (1 - 2 * upper)


def gather_route(me, here, peer, lanes):
    source_z = (me // 2) % lanes + lanes * here
    return copy_head(source_z, (peer // 2) % lanes, me % 2, lanes)


def return_route(me, here, peer, lanes):
    first = copy_head((peer // 2) % lanes, (me // 2) % lanes, peer % 2, lanes)
    return (first + here) % 2


def exchange_kernel(route, lanes, x_ref, y_ref, send_sem, recv_sem, local_sem):
    me = lax.axis_index("wide")
    here = lax.axis_index("head")
    n = x_ref.shape[0]
    ways = send_sem.shape[0]
    local = pltpu.make_async_copy(x_ref.at[me], y_ref.at[me], local_sem)
    local.start()
    for way in range(ways):

        def send(step, carry, way=way):
            peer = lax.rem(me + step * ways + way, n)
            pltpu.make_async_remote_copy(
                src_ref=x_ref.at[peer],
                dst_ref=y_ref.at[me],
                send_sem=send_sem.at[way],
                recv_sem=recv_sem.at[way],
                device_id=(peer, route(me, here, peer, lanes)),
                device_id_type=pl.DeviceIdType.MESH,
            ).start()
            return carry

        lax.fori_loop(1 if way == 0 else 0, (n - way + ways - 1) // ways, send, 0)
    for way in range(ways):
        count = (n - way + ways - 1) // ways - (1 if way == 0 else 0)
        every = pltpu.make_async_remote_copy(
            src_ref=x_ref.at[pl.ds(0, count)],
            dst_ref=y_ref.at[pl.ds(0, count)],
            send_sem=send_sem.at[way],
            recv_sem=recv_sem.at[way],
            device_id=(me, here),
            device_id_type=pl.DeviceIdType.MESH,
        )
        every.wait_send()
        every.wait_recv()
    local.wait()


def exchange(x, route, lanes, ways=32):
    return pl.pallas_call(
        functools.partial(exchange_kernel, route, lanes),
        out_shape=jax.ShapeDtypeStruct(x.shape, x.dtype),
        in_specs=[pl.BlockSpec(memory_space=pl.ANY)],
        out_specs=pl.BlockSpec(memory_space=pl.ANY),
        scratch_shapes=[
            pltpu.SemaphoreType.DMA((ways,)),
            pltpu.SemaphoreType.DMA((ways,)),
            pltpu.SemaphoreType.DMA,
        ],
        compiler_params=pltpu.CompilerParams(has_side_effects=True),
    )(x)


def shifted(block, axis, distance):
    devices = range(lax.axis_size(axis))
    route = [(i - distance, i) for i in devices if i - distance in devices]
    return lax.ppermute(block, axis, route)


def attend(branch_query, key_new, value_new, pools, tables, lengths, source, row):
    row_count = branch_query.shape[0]
    groups = key_new.shape[1] // HD
    per_group = branch_query.shape[1] // (groups * HD)
    pages, page_size = pools[0].shape[1], pools[0].shape[2]
    queries = branch_query.reshape(row_count, groups, per_group, HD)
    own_keys = key_new.reshape(row_count, groups, HD)
    own_values = value_new.reshape(row_count, groups, HD)
    factor = 1.0 / math.sqrt(HD)
    page_ids = jnp.arange(pages, dtype=jnp.int32)
    slots = jnp.arange(tables[0].shape[1], dtype=jnp.int32)
    offsets = jnp.arange(page_size, dtype=jnp.int32)
    scores, masks = [], []
    for which, (pool, table, length) in enumerate(zip(pools, tables, lengths)):
        parent_table = table[row]
        match = parent_table[:, None, :] == page_ids[None, :, None]
        slot = jnp.sum(jnp.where(match, slots[None, None, :], 0), axis=-1)
        found = jnp.any(match, axis=-1) & (source == which)[:, None]
        live = found[:, :, None] & (
            slot[:, :, None] * page_size + offsets[None, None, :] < length[row][:, None, None]
        )
        keys = pool[0].reshape(pages * page_size, groups * HD)
        part = jnp.stack(
            [
                jnp.einsum(
                    "rjd,td->rjt",
                    queries[:, g],
                    keys[:, g * HD : (g + 1) * HD],
                    preferred_element_type=jnp.float32,
                )
                for g in range(groups)
            ],
            axis=1,
        ) * factor
        scores.append(part)
        masks.append(live.reshape(row_count, 1, 1, pages * page_size))
    tail_scores = jnp.concatenate(scores, axis=-1)
    live_mask = jnp.concatenate(masks, axis=-1)
    own_scores = (
        jnp.einsum("rgjd,rgd->rgj", queries, own_keys, preferred_element_type=jnp.float32) * factor
    )
    top_score = jnp.maximum(jnp.max(jnp.where(live_mask, tail_scores, -1e30), axis=-1), own_scores)
    tail_exp = jnp.where(live_mask, jnp.exp(tail_scores - top_score[..., None]), 0.0)
    own_exp = jnp.exp(own_scores - top_score)
    totals = jnp.sum(tail_exp, axis=-1) + own_exp
    tail_weights = (tail_exp / totals[..., None]).astype(jnp.bfloat16)
    own_weights = (own_exp / totals).astype(jnp.bfloat16)
    span = pages * page_size
    mixture = own_weights[..., None].astype(jnp.float32) * own_values[:, :, None, :].astype(
        jnp.float32
    )
    for which, pool in enumerate(pools):
        values = pool[1].reshape(span, groups * HD)
        weights = tail_weights[..., which * span : (which + 1) * span]
        mixture = mixture + jnp.stack(
            [
                jnp.einsum(
                    "rjt,td->rjd",
                    weights[:, g],
                    values[:, g * HD : (g + 1) * HD],
                    preferred_element_type=jnp.float32,
                )
                for g in range(groups)
            ],
            axis=1,
        )
    return mixture.reshape(row_count, -1).astype(jnp.bfloat16)


def hidden_units(picked, gate_blocks, up_blocks, gate_scale, up_scale):
    gate_part = jnp.einsum(
        "skd,kdf->ksf", picked, gate_blocks[0], preferred_element_type=jnp.float32
    )
    up_part = jnp.einsum("skd,kdf->ksf", picked, up_blocks[0], preferred_element_type=jnp.float32)
    gate_sum = jnp.sum(gate_part * gate_scale[0][:, None, None], axis=0)
    up_sum = jnp.sum(up_part * up_scale[0][:, None, None], axis=0)
    return (jax.nn.silu(gate_sum) * up_sum).astype(jnp.bfloat16)


def per_device(
    branch_query,
    key_new,
    value_new,
    pool_pages,
    page_table,
    tail_length,
    parent_row,
    residual,
    norm_gain,
    gate_blocks,
    up_blocks,
    gate_up_keep,
    gate_scale,
    up_scale,
    down_blocks,
    down_keep,
    down_scale,
):
    row_count = branch_query.shape[0]
    prior_pool, prior_meta = shifted(
        (pool_pages, jnp.concatenate([page_table, tail_length[:, None]], axis=1)), "wide", 1
    )
    prior = (prior_pool, prior_meta[:, :-1], prior_meta[:, -1])
    local_parent = parent_row - (lax.axis_index("wide") - 1) * row_count
    attention = attend(
        branch_query,
        key_new,
        value_new,
        (prior[0], pool_pages),
        (prior[1], page_table),
        (prior[2], tail_length),
        local_parent // row_count,
        local_parent % row_count,
    )
    half = residual.shape[0]
    here = lax.axis_index("head")
    mine = lax.dynamic_slice_in_dim(attention, here * half, half, axis=0)
    theirs = lax.dynamic_slice_in_dim(attention, (1 - here) * half, half, axis=0)
    arrived_half = lax.ppermute(theirs, "head", [(0, 1), (1, 0)])
    head_rows = jnp.where(
        here == 0,
        jnp.concatenate([mine, arrived_half], axis=1),
        jnp.concatenate([arrived_half, mine], axis=1),
    )
    middle = residual.astype(jnp.float32) + head_rows.astype(jnp.float32)
    normed = (
        middle * lax.rsqrt(jnp.mean(middle * middle, axis=-1, keepdims=True) + 1e-05) * norm_gain
    ).astype(jnp.bfloat16)
    peers = lax.axis_size("wide")
    own_lists = jnp.concatenate([gate_up_keep, down_keep], axis=1)
    keep_lists = lax.all_to_all(
        jnp.broadcast_to(own_lists, (peers, own_lists.shape[1])),
        "wide",
        split_axis=0,
        concat_axis=0,
        tiled=True,
    )
    keep = gate_up_keep.shape[1]
    in_keep, out_keep = keep_lists[:, :keep], keep_lists[:, keep:]
    feature_blocks = normed.shape[1] // BLK
    rows = normed.shape[0]
    blocks = jnp.arange(feature_blocks, dtype=jnp.int32)
    choose = (in_keep.reshape(peers * keep, 1) == blocks[None, :]).astype(jnp.bfloat16)
    by_block = jnp.swapaxes(normed.reshape(rows, feature_blocks, BLK), 0, 1)
    outgoing = jnp.dot(
        choose, by_block.reshape(feature_blocks, rows * BLK), preferred_element_type=jnp.float32
    ).astype(jnp.bfloat16)
    picked = exchange(outgoing.reshape(peers, keep, rows * BLK), gather_route, Z_LANES)
    hidden = jnp.concatenate(
        [
            hidden_units(
                picked[:, :, r * BLK : (r + 1) * BLK], gate_blocks, up_blocks, gate_scale, up_scale
            )
            for r in range(rows)
        ],
        axis=0,
    )
    down_flat = jnp.swapaxes(down_blocks[0], 0, 1).reshape(BLK, keep * BLK)
    down_part = jnp.dot(hidden, down_flat, preferred_element_type=jnp.float32)
    column_scale = jnp.repeat(down_scale[0], BLK)
    contrib = lax.optimization_barrier((down_part * column_scale[None, :]).astype(jnp.bfloat16))
    contrib = contrib.reshape(rows, peers, keep, BLK)
    outgoing_sums = jnp.concatenate([contrib[r] for r in range(rows)], axis=-1)
    arrived = exchange(outgoing_sums, return_route, Z_LANES)
    placement = (blocks[:, None] == out_keep.reshape(1, peers * keep)).astype(jnp.bfloat16)
    summed = jnp.stack(
        [
            jnp.dot(
                placement,
                arrived[:, :, r * BLK : (r + 1) * BLK].reshape(peers * keep, BLK),
                preferred_element_type=jnp.float32,
            )
            for r in range(rows)
        ],
        axis=0,
    )
    ffn_share = summed.reshape(rows, -1)
    return (middle + ffn_share).astype(jnp.bfloat16)


def solution(mesh):
    placed = (
        P("wide", "head"),
        P("wide", "head"),
        P("wide", "head"),
        P(None, "wide", None, "head"),
        P("wide", None),
        P("wide"),
        P("wide"),
        P(("wide", "head"), None),
        P(),
        P("wide", None, None, None),
        P("wide", None, None, None),
        P("wide", None),
        P("wide", None),
        P("wide", None),
        P("wide", None, None, None),
        P("wide", None),
        P("wide", None),
    )
    return jax.shard_map(
        per_device, mesh=mesh, in_specs=placed, out_specs=P(("wide", "head"), None), check_vma=False
    )
```

```python
import functools
import math

import jax
import jax.numpy as jnp
from jax import lax
from jax.experimental import pallas as pl
from jax.experimental.pallas import tpu as pltpu
from jax.sharding import PartitionSpec as P

HD = 128
BLK = 128
Z_LANES = 4


def copy_head(source_z, target_lane, source_core, lanes):
    offset = (source_z - target_lane + 2 * lanes) % (2 * lanes)
    upper = ((offset + 1) % (2 * lanes)) // lanes
    tie = ((offset % lanes) // 2) * (1 - (offset % lanes) % 2)
    return upper + tie * source_core * (1 - 2 * upper)


def gather_route(me, here, peer, lanes):
    source_z = (me // 2) % lanes + lanes * here
    return copy_head(source_z, (peer // 2) % lanes, me % 2, lanes)


def return_route(me, here, peer, lanes):
    first = copy_head((peer // 2) % lanes, (me // 2) % lanes, peer % 2, lanes)
    return (first + here) % 2


def exchange_kernel(route, lanes, x_ref, y_ref, send_sem, recv_sem, local_sem):
    me = lax.axis_index("wide")
    here = lax.axis_index("head")
    n = x_ref.shape[0]
    ways = send_sem.shape[0]
    local = pltpu.make_async_copy(x_ref.at[me], y_ref.at[me], local_sem)
    local.start()
    for way in range(ways):

        def send(step, carry, way=way):
            peer = lax.rem(me + step * ways + way, n)
            pltpu.make_async_remote_copy(
                src_ref=x_ref.at[peer],
                dst_ref=y_ref.at[me],
                send_sem=send_sem.at[way],
                recv_sem=recv_sem.at[way],
                device_id=(peer, route(me, here, peer, lanes)),
                device_id_type=pl.DeviceIdType.MESH,
            ).start()
            return carry

        lax.fori_loop(1 if way == 0 else 0, (n - way + ways - 1) // ways, send, 0)
    for way in range(ways):
        count = (n - way + ways - 1) // ways - (1 if way == 0 else 0)
        every = pltpu.make_async_remote_copy(
            src_ref=x_ref.at[pl.ds(0, count)],
            dst_ref=y_ref.at[pl.ds(0, count)],
            send_sem=send_sem.at[way],
            recv_sem=recv_sem.at[way],
            device_id=(me, here),
            device_id_type=pl.DeviceIdType.MESH,
        )
        every.wait_send()
        every.wait_recv()
    local.wait()


def exchange(x, route, lanes, ways=4):
    return pl.pallas_call(
        functools.partial(exchange_kernel, route, lanes),
        out_shape=jax.ShapeDtypeStruct(x.shape, x.dtype),
        in_specs=[pl.BlockSpec(memory_space=pl.ANY)],
        out_specs=pl.BlockSpec(memory_space=pl.ANY),
        scratch_shapes=[
            pltpu.SemaphoreType.DMA((ways,)),
            pltpu.SemaphoreType.DMA((ways,)),
            pltpu.SemaphoreType.DMA,
        ],
        compiler_params=pltpu.CompilerParams(has_side_effects=True),
    )(x)


def shifted(block, axis, distance):
    devices = range(lax.axis_size(axis))
    route = [(i - distance, i) for i in devices if i - distance in devices]
    return lax.ppermute(block, axis, route)


def attend(branch_query, key_new, value_new, pools, tables, lengths, source, row):
    row_count = branch_query.shape[0]
    groups = key_new.shape[1] // HD
    per_group = branch_query.shape[1] // (groups * HD)
    pages, page_size = pools[0].shape[1], pools[0].shape[2]
    queries = branch_query.reshape(row_count, groups, per_group, HD)
    own_keys = key_new.reshape(row_count, groups, HD)
    own_values = value_new.reshape(row_count, groups, HD)
    factor = 1.0 / math.sqrt(HD)
    page_ids = jnp.arange(pages, dtype=jnp.int32)
    slots = jnp.arange(tables[0].shape[1], dtype=jnp.int32)
    offsets = jnp.arange(page_size, dtype=jnp.int32)
    scores, masks = [], []
    for which, (pool, table, length) in enumerate(zip(pools, tables, lengths)):
        parent_table = table[row]
        match = parent_table[:, None, :] == page_ids[None, :, None]
        slot = jnp.sum(jnp.where(match, slots[None, None, :], 0), axis=-1)
        found = jnp.any(match, axis=-1) & (source == which)[:, None]
        live = found[:, :, None] & (
            slot[:, :, None] * page_size + offsets[None, None, :] < length[row][:, None, None]
        )
        keys = pool[0].reshape(pages * page_size, groups * HD)
        part = jnp.stack(
            [
                jnp.einsum(
                    "rjd,td->rjt",
                    queries[:, g],
                    keys[:, g * HD : (g + 1) * HD],
                    preferred_element_type=jnp.float32,
                )
                for g in range(groups)
            ],
            axis=1,
        ) * factor
        scores.append(part)
        masks.append(live.reshape(row_count, 1, 1, pages * page_size))
    tail_scores = jnp.concatenate(scores, axis=-1)
    live_mask = jnp.concatenate(masks, axis=-1)
    own_scores = (
        jnp.einsum("rgjd,rgd->rgj", queries, own_keys, preferred_element_type=jnp.float32) * factor
    )
    top_score = jnp.maximum(jnp.max(jnp.where(live_mask, tail_scores, -1e30), axis=-1), own_scores)
    tail_exp = jnp.where(live_mask, jnp.exp(tail_scores - top_score[..., None]), 0.0)
    own_exp = jnp.exp(own_scores - top_score)
    totals = jnp.sum(tail_exp, axis=-1) + own_exp
    tail_weights = (tail_exp / totals[..., None]).astype(jnp.bfloat16)
    own_weights = (own_exp / totals).astype(jnp.bfloat16)
    span = pages * page_size
    mixture = own_weights[..., None].astype(jnp.float32) * own_values[:, :, None, :].astype(
        jnp.float32
    )
    for which, pool in enumerate(pools):
        values = pool[1].reshape(span, groups * HD)
        weights = tail_weights[..., which * span : (which + 1) * span]
        mixture = mixture + jnp.stack(
            [
                jnp.einsum(
                    "rjt,td->rjd",
                    weights[:, g],
                    values[:, g * HD : (g + 1) * HD],
                    preferred_element_type=jnp.float32,
                )
                for g in range(groups)
            ],
            axis=1,
        )
    return mixture.reshape(row_count, -1).astype(jnp.bfloat16)


def hidden_units(picked, gate_blocks, up_blocks, gate_scale, up_scale):
    gate_part = jnp.einsum(
        "skd,kdf->ksf", picked, gate_blocks[0], preferred_element_type=jnp.float32
    )
    up_part = jnp.einsum("skd,kdf->ksf", picked, up_blocks[0], preferred_element_type=jnp.float32)
    gate_sum = jnp.sum(gate_part * gate_scale[0][:, None, None], axis=0)
    up_sum = jnp.sum(up_part * up_scale[0][:, None, None], axis=0)
    return (jax.nn.silu(gate_sum) * up_sum).astype(jnp.bfloat16)


def per_device(
    branch_query,
    key_new,
    value_new,
    pool_pages,
    page_table,
    tail_length,
    parent_row,
    residual,
    norm_gain,
    gate_blocks,
    up_blocks,
    gate_up_keep,
    gate_scale,
    up_scale,
    down_blocks,
    down_keep,
    down_scale,
):
    row_count = branch_query.shape[0]
    prior_pool, prior_meta = shifted(
        (pool_pages, jnp.concatenate([page_table, tail_length[:, None]], axis=1)), "wide", 1
    )
    prior = (prior_pool, prior_meta[:, :-1], prior_meta[:, -1])
    local_parent = parent_row - (lax.axis_index("wide") - 1) * row_count
    attention = attend(
        branch_query,
        key_new,
        value_new,
        (prior[0], pool_pages),
        (prior[1], page_table),
        (prior[2], tail_length),
        local_parent // row_count,
        local_parent % row_count,
    )
    half = residual.shape[0]
    here = lax.axis_index("head")
    mine = lax.dynamic_slice_in_dim(attention, here * half, half, axis=0)
    theirs = lax.dynamic_slice_in_dim(attention, (1 - here) * half, half, axis=0)
    arrived_half = lax.ppermute(theirs, "head", [(0, 1), (1, 0)])
    head_rows = jnp.where(
        here == 0,
        jnp.concatenate([mine, arrived_half], axis=1),
        jnp.concatenate([arrived_half, mine], axis=1),
    )
    middle = residual.astype(jnp.float32) + head_rows.astype(jnp.float32)
    normed = (
        middle * lax.rsqrt(jnp.mean(middle * middle, axis=-1, keepdims=True) + 1e-05) * norm_gain
    ).astype(jnp.bfloat16)
    peers = lax.axis_size("wide")
    own_lists = jnp.concatenate([gate_up_keep, down_keep], axis=1)
    keep_lists = lax.all_to_all(
        jnp.broadcast_to(own_lists, (peers, own_lists.shape[1])),
        "wide",
        split_axis=0,
        concat_axis=0,
        tiled=True,
    )
    keep = gate_up_keep.shape[1]
    in_keep, out_keep = keep_lists[:, :keep], keep_lists[:, keep:]
    feature_blocks = normed.shape[1] // BLK
    rows = normed.shape[0]
    blocks = jnp.arange(feature_blocks, dtype=jnp.int32)
    choose = (in_keep.reshape(peers * keep, 1) == blocks[None, :]).astype(jnp.bfloat16)
    by_block = jnp.swapaxes(normed.reshape(rows, feature_blocks, BLK), 0, 1)
    outgoing = jnp.dot(
        choose, by_block.reshape(feature_blocks, rows * BLK), preferred_element_type=jnp.float32
    ).astype(jnp.bfloat16)
    picked = exchange(outgoing.reshape(peers, keep, rows * BLK), gather_route, Z_LANES)
    hidden = jnp.concatenate(
        [
            hidden_units(
                picked[:, :, r * BLK : (r + 1) * BLK], gate_blocks, up_blocks, gate_scale, up_scale
            )
            for r in range(rows)
        ],
        axis=0,
    )
    down_flat = jnp.swapaxes(down_blocks[0], 0, 1).reshape(BLK, keep * BLK)
    down_part = jnp.dot(hidden, down_flat, preferred_element_type=jnp.float32)
    column_scale = jnp.repeat(down_scale[0], BLK)
    contrib = lax.optimization_barrier((down_part * column_scale[None, :]).astype(jnp.bfloat16))
    contrib = contrib.reshape(rows, peers, keep, BLK)
    outgoing_sums = jnp.concatenate([contrib[r] for r in range(rows)], axis=-1)
    arrived = exchange(outgoing_sums, return_route, Z_LANES)
    placement = (blocks[:, None] == out_keep.reshape(1, peers * keep)).astype(jnp.bfloat16)
    summed = jnp.stack(
        [
            jnp.dot(
                placement,
                arrived[:, :, r * BLK : (r + 1) * BLK].reshape(peers * keep, BLK),
                preferred_element_type=jnp.float32,
            )
            for r in range(rows)
        ],
        axis=0,
    )
    ffn_share = summed.reshape(rows, -1)
    return (middle + ffn_share).astype(jnp.bfloat16)


def solution(mesh):
    placed = (
        P("wide", "head"),
        P("wide", "head"),
        P("wide", "head"),
        P(None, "wide", None, "head"),
        P("wide", None),
        P("wide"),
        P("wide"),
        P(("wide", "head"), None),
        P(),
        P("wide", None, None, None),
        P("wide", None, None, None),
        P("wide", None),
        P("wide", None),
        P("wide", None),
        P("wide", None, None, None),
        P("wide", None),
        P("wide", None),
    )
    return jax.shard_map(
        per_device, mesh=mesh, in_specs=placed, out_specs=P(("wide", "head"), None), check_vma=False
    )
```

```python
import functools
import math

import jax
import jax.numpy as jnp
from jax import lax
from jax.experimental import pallas as pl
from jax.experimental.pallas import tpu as pltpu
from jax.sharding import PartitionSpec as P

HD = 128
BLK = 128
Z_LANES = 4


def copy_head(source_z, target_lane, source_core, lanes):
    offset = (source_z - target_lane + 2 * lanes) % (2 * lanes)
    upper = ((offset + 1) % (2 * lanes)) // lanes
    tie = ((offset % lanes) // 2) * (1 - (offset % lanes) % 2)
    return upper + tie * source_core * (1 - 2 * upper)


def gather_route(me, here, peer, lanes):
    source_z = (me // 2) % lanes + lanes * here
    return copy_head(source_z, (peer // 2) % lanes, me % 2, lanes)


def return_route(me, here, peer, lanes):
    first = copy_head((peer // 2) % lanes, (me // 2) % lanes, peer % 2, lanes)
    return (first + here) % 2


def exchange_kernel(route, lanes, x_ref, y_ref, send_sem, recv_sem, local_sem):
    me = lax.axis_index("wide")
    here = lax.axis_index("head")
    n = x_ref.shape[0]
    ways = send_sem.shape[0]
    local = pltpu.make_async_copy(x_ref.at[me], y_ref.at[me], local_sem)
    local.start()
    for way in range(ways):

        def send(step, carry, way=way):
            peer = lax.rem(me + step * ways + way, n)
            pltpu.make_async_remote_copy(
                src_ref=x_ref.at[peer],
                dst_ref=y_ref.at[me],
                send_sem=send_sem.at[way],
                recv_sem=recv_sem.at[way],
                device_id=(peer, route(me, here, peer, lanes)),
                device_id_type=pl.DeviceIdType.MESH,
            ).start()
            return carry

        lax.fori_loop(1 if way == 0 else 0, (n - way + ways - 1) // ways, send, 0)
    for way in range(ways):
        count = (n - way + ways - 1) // ways - (1 if way == 0 else 0)
        every = pltpu.make_async_remote_copy(
            src_ref=x_ref.at[pl.ds(0, count)],
            dst_ref=y_ref.at[pl.ds(0, count)],
            send_sem=send_sem.at[way],
            recv_sem=recv_sem.at[way],
            device_id=(me, here),
            device_id_type=pl.DeviceIdType.MESH,
        )
        every.wait_send()
        every.wait_recv()
    local.wait()


def exchange(x, route, lanes, ways=8):
    return pl.pallas_call(
        functools.partial(exchange_kernel, route, lanes),
        out_shape=jax.ShapeDtypeStruct(x.shape, x.dtype),
        in_specs=[pl.BlockSpec(memory_space=pltpu.VMEM)],
        out_specs=pl.BlockSpec(memory_space=pltpu.VMEM),
        scratch_shapes=[
            pltpu.SemaphoreType.DMA((ways,)),
            pltpu.SemaphoreType.DMA((ways,)),
            pltpu.SemaphoreType.DMA,
        ],
        compiler_params=pltpu.CompilerParams(has_side_effects=True),
    )(x)


def shifted(block, axis, distance):
    devices = range(lax.axis_size(axis))
    route = [(i - distance, i) for i in devices if i - distance in devices]
    return lax.ppermute(block, axis, route)


def attend(branch_query, key_new, value_new, pools, tables, lengths, source, row):
    row_count = branch_query.shape[0]
    groups = key_new.shape[1] // HD
    per_group = branch_query.shape[1] // (groups * HD)
    pages, page_size = pools[0].shape[1], pools[0].shape[2]
    queries = branch_query.reshape(row_count, groups, per_group, HD)
    own_keys = key_new.reshape(row_count, groups, HD)
    own_values = value_new.reshape(row_count, groups, HD)
    factor = 1.0 / math.sqrt(HD)
    page_ids = jnp.arange(pages, dtype=jnp.int32)
    slots = jnp.arange(tables[0].shape[1], dtype=jnp.int32)
    offsets = jnp.arange(page_size, dtype=jnp.int32)
    scores, masks = [], []
    for which, (pool, table, length) in enumerate(zip(pools, tables, lengths)):
        parent_table = table[row]
        match = parent_table[:, None, :] == page_ids[None, :, None]
        slot = jnp.sum(jnp.where(match, slots[None, None, :], 0), axis=-1)
        found = jnp.any(match, axis=-1) & (source == which)[:, None]
        live = found[:, :, None] & (
            slot[:, :, None] * page_size + offsets[None, None, :] < length[row][:, None, None]
        )
        keys = pool[0].reshape(pages * page_size, groups * HD)
        part = jnp.stack(
            [
                jnp.einsum(
                    "rjd,td->rjt",
                    queries[:, g],
                    keys[:, g * HD : (g + 1) * HD],
                    preferred_element_type=jnp.float32,
                )
                for g in range(groups)
            ],
            axis=1,
        ) * factor
        scores.append(part)
        masks.append(live.reshape(row_count, 1, 1, pages * page_size))
    tail_scores = jnp.concatenate(scores, axis=-1)
    live_mask = jnp.concatenate(masks, axis=-1)
    own_scores = (
        jnp.einsum("rgjd,rgd->rgj", queries, own_keys, preferred_element_type=jnp.float32) * factor
    )
    top_score = jnp.maximum(jnp.max(jnp.where(live_mask, tail_scores, -1e30), axis=-1), own_scores)
    tail_exp = jnp.where(live_mask, jnp.exp(tail_scores - top_score[..., None]), 0.0)
    own_exp = jnp.exp(own_scores - top_score)
    totals = jnp.sum(tail_exp, axis=-1) + own_exp
    tail_weights = (tail_exp / totals[..., None]).astype(jnp.bfloat16)
    own_weights = (own_exp / totals).astype(jnp.bfloat16)
    span = pages * page_size
    mixture = own_weights[..., None].astype(jnp.float32) * own_values[:, :, None, :].astype(
        jnp.float32
    )
    for which, pool in enumerate(pools):
        values = pool[1].reshape(span, groups * HD)
        weights = tail_weights[..., which * span : (which + 1) * span]
        mixture = mixture + jnp.stack(
            [
                jnp.einsum(
                    "rjt,td->rjd",
                    weights[:, g],
                    values[:, g * HD : (g + 1) * HD],
                    preferred_element_type=jnp.float32,
                )
                for g in range(groups)
            ],
            axis=1,
        )
    return mixture.reshape(row_count, -1).astype(jnp.bfloat16)


def hidden_units(picked, gate_blocks, up_blocks, gate_scale, up_scale):
    gate_part = jnp.einsum(
        "skd,kdf->ksf", picked, gate_blocks[0], preferred_element_type=jnp.float32
    )
    up_part = jnp.einsum("skd,kdf->ksf", picked, up_blocks[0], preferred_element_type=jnp.float32)
    gate_sum = jnp.sum(gate_part * gate_scale[0][:, None, None], axis=0)
    up_sum = jnp.sum(up_part * up_scale[0][:, None, None], axis=0)
    return (jax.nn.silu(gate_sum) * up_sum).astype(jnp.bfloat16)


def per_device(
    branch_query,
    key_new,
    value_new,
    pool_pages,
    page_table,
    tail_length,
    parent_row,
    residual,
    norm_gain,
    gate_blocks,
    up_blocks,
    gate_up_keep,
    gate_scale,
    up_scale,
    down_blocks,
    down_keep,
    down_scale,
):
    row_count = branch_query.shape[0]
    prior_pool, prior_meta = shifted(
        (pool_pages, jnp.concatenate([page_table, tail_length[:, None]], axis=1)), "wide", 1
    )
    prior = (prior_pool, prior_meta[:, :-1], prior_meta[:, -1])
    local_parent = parent_row - (lax.axis_index("wide") - 1) * row_count
    attention = attend(
        branch_query,
        key_new,
        value_new,
        (prior[0], pool_pages),
        (prior[1], page_table),
        (prior[2], tail_length),
        local_parent // row_count,
        local_parent % row_count,
    )
    half = residual.shape[0]
    here = lax.axis_index("head")
    mine = lax.dynamic_slice_in_dim(attention, here * half, half, axis=0)
    theirs = lax.dynamic_slice_in_dim(attention, (1 - here) * half, half, axis=0)
    arrived_half = lax.ppermute(theirs, "head", [(0, 1), (1, 0)])
    head_rows = jnp.where(
        here == 0,
        jnp.concatenate([mine, arrived_half], axis=1),
        jnp.concatenate([arrived_half, mine], axis=1),
    )
    middle = residual.astype(jnp.float32) + head_rows.astype(jnp.float32)
    normed = (
        middle * lax.rsqrt(jnp.mean(middle * middle, axis=-1, keepdims=True) + 1e-05) * norm_gain
    ).astype(jnp.bfloat16)
    peers = lax.axis_size("wide")
    own_lists = jnp.concatenate([gate_up_keep, down_keep], axis=1)
    keep_lists = lax.all_to_all(
        jnp.broadcast_to(own_lists, (peers, own_lists.shape[1])),
        "wide",
        split_axis=0,
        concat_axis=0,
        tiled=True,
    )
    keep = gate_up_keep.shape[1]
    in_keep, out_keep = keep_lists[:, :keep], keep_lists[:, keep:]
    feature_blocks = normed.shape[1] // BLK
    rows = normed.shape[0]
    blocks = jnp.arange(feature_blocks, dtype=jnp.int32)
    choose = (in_keep.reshape(peers * keep, 1) == blocks[None, :]).astype(jnp.bfloat16)
    by_block = jnp.swapaxes(normed.reshape(rows, feature_blocks, BLK), 0, 1)
    outgoing = jnp.dot(
        choose, by_block.reshape(feature_blocks, rows * BLK), preferred_element_type=jnp.float32
    ).astype(jnp.bfloat16)
    picked = exchange(outgoing.reshape(peers, keep, rows * BLK), gather_route, Z_LANES)
    hidden = jnp.concatenate(
        [
            hidden_units(
                picked[:, :, r * BLK : (r + 1) * BLK], gate_blocks, up_blocks, gate_scale, up_scale
            )
            for r in range(rows)
        ],
        axis=0,
    )
    down_flat = jnp.swapaxes(down_blocks[0], 0, 1).reshape(BLK, keep * BLK)
    down_part = jnp.dot(hidden, down_flat, preferred_element_type=jnp.float32)
    column_scale = jnp.repeat(down_scale[0], BLK)
    contrib = lax.optimization_barrier((down_part * column_scale[None, :]).astype(jnp.bfloat16))
    contrib = contrib.reshape(rows, peers, keep, BLK)
    outgoing_sums = jnp.concatenate([contrib[r] for r in range(rows)], axis=-1)
    arrived = exchange(outgoing_sums, return_route, Z_LANES)
    placement = (blocks[:, None] == out_keep.reshape(1, peers * keep)).astype(jnp.bfloat16)
    summed = jnp.stack(
        [
            jnp.dot(
                placement,
                arrived[:, :, r * BLK : (r + 1) * BLK].reshape(peers * keep, BLK),
                preferred_element_type=jnp.float32,
            )
            for r in range(rows)
        ],
        axis=0,
    )
    ffn_share = summed.reshape(rows, -1)
    return (middle + ffn_share).astype(jnp.bfloat16)


def solution(mesh):
    placed = (
        P("wide", "head"),
        P("wide", "head"),
        P("wide", "head"),
        P(None, "wide", None, "head"),
        P("wide", None),
        P("wide"),
        P("wide"),
        P(("wide", "head"), None),
        P(),
        P("wide", None, None, None),
        P("wide", None, None, None),
        P("wide", None),
        P("wide", None),
        P("wide", None),
        P("wide", None, None, None),
        P("wide", None),
        P("wide", None),
    )
    return jax.shard_map(
        per_device, mesh=mesh, in_specs=placed, out_specs=P(("wide", "head"), None), check_vma=False
    )
```

```python
import functools
import math

import jax
import jax.numpy as jnp
from jax import lax
from jax.experimental import pallas as pl
from jax.experimental.pallas import tpu as pltpu
from jax.sharding import PartitionSpec as P

HD = 128
BLK = 128
Z_LANES = 4


def copy_head(source_z, target_lane, source_core, lanes):
    offset = (source_z - target_lane + 2 * lanes) % (2 * lanes)
    upper = ((offset + 1) % (2 * lanes)) // lanes
    tie = ((offset % lanes) // 2) * (1 - (offset % lanes) % 2)
    return upper + tie * source_core * (1 - 2 * upper)


def gather_route(me, here, peer, lanes):
    source_z = (me // 2) % lanes + lanes * here
    return copy_head(source_z, (peer // 2) % lanes, me % 2, lanes)


def return_route(me, here, peer, lanes):
    first = copy_head((peer // 2) % lanes, (me // 2) % lanes, peer % 2, lanes)
    return (first + here) % 2


def exchange_kernel(route, lanes, x_ref, y_ref, send_sem, recv_sem, local_sem):
    me = lax.axis_index("wide")
    here = lax.axis_index("head")
    n = x_ref.shape[0]
    ways = send_sem.shape[0]
    local = pltpu.make_async_copy(x_ref.at[me], y_ref.at[me], local_sem)
    local.start()
    for way in range(ways):

        def send(step, carry, way=way):
            peer = lax.rem(me + step * ways + way, n)
            pltpu.make_async_remote_copy(
                src_ref=x_ref.at[peer],
                dst_ref=y_ref.at[me],
                send_sem=send_sem.at[way],
                recv_sem=recv_sem.at[way],
                device_id=(peer, route(me, here, peer, lanes)),
                device_id_type=pl.DeviceIdType.MESH,
            ).start()
            return carry

        lax.fori_loop(1 if way == 0 else 0, (n - way + ways - 1) // ways, send, 0)
    for way in range(ways):
        count = (n - way + ways - 1) // ways - (1 if way == 0 else 0)
        every = pltpu.make_async_remote_copy(
            src_ref=x_ref.at[pl.ds(0, count)],
            dst_ref=y_ref.at[pl.ds(0, count)],
            send_sem=send_sem.at[way],
            recv_sem=recv_sem.at[way],
            device_id=(me, here),
            device_id_type=pl.DeviceIdType.MESH,
        )
        every.wait_send()
        every.wait_recv()
    local.wait()


def exchange(x, route, lanes, ways=8):
    return pl.pallas_call(
        functools.partial(exchange_kernel, route, lanes),
        out_shape=jax.ShapeDtypeStruct(x.shape, x.dtype),
        in_specs=[pl.BlockSpec(memory_space=pl.ANY)],
        out_specs=pl.BlockSpec(memory_space=pl.ANY),
        scratch_shapes=[
            pltpu.SemaphoreType.DMA((ways,)),
            pltpu.SemaphoreType.DMA((ways,)),
            pltpu.SemaphoreType.DMA,
        ],
        compiler_params=pltpu.CompilerParams(has_side_effects=True),
    )(x)


def shifted(block, axis, distance):
    devices = range(lax.axis_size(axis))
    route = [(i - distance, i) for i in devices if i - distance in devices]
    return lax.ppermute(block, axis, route)


def attend(branch_query, key_new, value_new, pools, tables, lengths, source, row):
    row_count = branch_query.shape[0]
    groups = key_new.shape[1] // HD
    per_group = branch_query.shape[1] // (groups * HD)
    pages, page_size = pools[0].shape[1], pools[0].shape[2]
    queries = branch_query.reshape(row_count, groups, per_group, HD)
    own_keys = key_new.reshape(row_count, groups, HD)
    own_values = value_new.reshape(row_count, groups, HD)
    factor = 1.0 / math.sqrt(HD)
    page_ids = jnp.arange(pages, dtype=jnp.int32)
    slots = jnp.arange(tables[0].shape[1], dtype=jnp.int32)
    offsets = jnp.arange(page_size, dtype=jnp.int32)
    scores, masks = [], []
    for which, (pool, table, length) in enumerate(zip(pools, tables, lengths)):
        parent_table = table[row]
        match = parent_table[:, None, :] == page_ids[None, :, None]
        slot = jnp.sum(jnp.where(match, slots[None, None, :], 0), axis=-1)
        found = jnp.any(match, axis=-1) & (source == which)[:, None]
        live = found[:, :, None] & (
            slot[:, :, None] * page_size + offsets[None, None, :] < length[row][:, None, None]
        )
        keys = pool[0].reshape(pages * page_size, groups * HD)
        part = jnp.stack(
            [
                jnp.einsum(
                    "rjd,td->rjt",
                    queries[:, g],
                    keys[:, g * HD : (g + 1) * HD],
                    preferred_element_type=jnp.float32,
                )
                for g in range(groups)
            ],
            axis=1,
        ) * factor
        scores.append(part)
        masks.append(live.reshape(row_count, 1, 1, pages * page_size))
    tail_scores = jnp.concatenate(scores, axis=-1)
    live_mask = jnp.concatenate(masks, axis=-1)
    own_scores = (
        jnp.einsum("rgjd,rgd->rgj", queries, own_keys, preferred_element_type=jnp.float32) * factor
    )
    top_score = jnp.maximum(jnp.max(jnp.where(live_mask, tail_scores, -1e30), axis=-1), own_scores)
    tail_exp = jnp.where(live_mask, jnp.exp(tail_scores - top_score[..., None]), 0.0)
    own_exp = jnp.exp(own_scores - top_score)
    totals = jnp.sum(tail_exp, axis=-1) + own_exp
    tail_weights = (tail_exp / totals[..., None]).astype(jnp.bfloat16)
    own_weights = (own_exp / totals).astype(jnp.bfloat16)
    span = pages * page_size
    mixture = own_weights[..., None].astype(jnp.float32) * own_values[:, :, None, :].astype(
        jnp.float32
    )
    for which, pool in enumerate(pools):
        values = pool[1].reshape(span, groups * HD)
        weights = tail_weights[..., which * span : (which + 1) * span]
        mixture = mixture + jnp.stack(
            [
                jnp.einsum(
                    "rjt,td->rjd",
                    weights[:, g],
                    values[:, g * HD : (g + 1) * HD],
                    preferred_element_type=jnp.float32,
                )
                for g in range(groups)
            ],
            axis=1,
        )
    return mixture.reshape(row_count, -1).astype(jnp.bfloat16)


def hidden_units(picked, gate_blocks, up_blocks, gate_scale, up_scale):
    gate_part = jnp.einsum(
        "skd,kdf->ksf", picked, gate_blocks[0], preferred_element_type=jnp.float32
    )
    up_part = jnp.einsum("skd,kdf->ksf", picked, up_blocks[0], preferred_element_type=jnp.float32)
    gate_sum = jnp.sum(gate_part * gate_scale[0][:, None, None], axis=0)
    up_sum = jnp.sum(up_part * up_scale[0][:, None, None], axis=0)
    return (jax.nn.silu(gate_sum) * up_sum).astype(jnp.bfloat16)


def per_device(
    branch_query,
    key_new,
    value_new,
    pool_pages,
    page_table,
    tail_length,
    parent_row,
    residual,
    norm_gain,
    gate_blocks,
    up_blocks,
    gate_up_keep,
    gate_scale,
    up_scale,
    down_blocks,
    down_keep,
    down_scale,
):
    row_count = branch_query.shape[0]
    prior_pool, prior_meta = shifted(
        (pool_pages, jnp.concatenate([page_table, tail_length[:, None]], axis=1)), "wide", 1
    )
    prior = (prior_pool, prior_meta[:, :-1], prior_meta[:, -1])
    local_parent = parent_row - (lax.axis_index("wide") - 1) * row_count
    attention = attend(
        branch_query,
        key_new,
        value_new,
        (prior[0], pool_pages),
        (prior[1], page_table),
        (prior[2], tail_length),
        local_parent // row_count,
        local_parent % row_count,
    )
    half = residual.shape[0]
    here = lax.axis_index("head")
    mine = lax.dynamic_slice_in_dim(attention, here * half, half, axis=0)
    theirs = lax.dynamic_slice_in_dim(attention, (1 - here) * half, half, axis=0)
    arrived_half = lax.ppermute(theirs, "head", [(0, 1), (1, 0)])
    head_rows = jnp.where(
        here == 0,
        jnp.concatenate([mine, arrived_half], axis=1),
        jnp.concatenate([arrived_half, mine], axis=1),
    )
    middle = residual.astype(jnp.float32) + head_rows.astype(jnp.float32)
    normed = (
        middle * lax.rsqrt(jnp.mean(middle * middle, axis=-1, keepdims=True) + 1e-05) * norm_gain
    ).astype(jnp.bfloat16)
    peers = lax.axis_size("wide")
    own_lists, normed = lax.optimization_barrier(
        (jnp.concatenate([gate_up_keep, down_keep], axis=1), normed)
    )
    keep_lists = lax.all_to_all(
        jnp.broadcast_to(own_lists, (peers, own_lists.shape[1])),
        "wide",
        split_axis=0,
        concat_axis=0,
        tiled=True,
    )
    keep = gate_up_keep.shape[1]
    in_keep, out_keep = keep_lists[:, :keep], keep_lists[:, keep:]
    feature_blocks = normed.shape[1] // BLK
    rows = normed.shape[0]
    blocks = jnp.arange(feature_blocks, dtype=jnp.int32)
    choose = (in_keep.reshape(peers * keep, 1) == blocks[None, :]).astype(jnp.bfloat16)
    by_block = jnp.swapaxes(normed.reshape(rows, feature_blocks, BLK), 0, 1)
    outgoing = jnp.dot(
        choose, by_block.reshape(feature_blocks, rows * BLK), preferred_element_type=jnp.float32
    ).astype(jnp.bfloat16)
    picked = exchange(outgoing.reshape(peers, keep, rows * BLK), gather_route, Z_LANES)
    hidden = jnp.concatenate(
        [
            hidden_units(
                picked[:, :, r * BLK : (r + 1) * BLK], gate_blocks, up_blocks, gate_scale, up_scale
            )
            for r in range(rows)
        ],
        axis=0,
    )
    down_flat = jnp.swapaxes(down_blocks[0], 0, 1).reshape(BLK, keep * BLK)
    down_part = jnp.dot(hidden, down_flat, preferred_element_type=jnp.float32)
    column_scale = jnp.repeat(down_scale[0], BLK)
    contrib = lax.optimization_barrier((down_part * column_scale[None, :]).astype(jnp.bfloat16))
    contrib = contrib.reshape(rows, peers, keep, BLK)
    outgoing_sums = jnp.concatenate([contrib[r] for r in range(rows)], axis=-1)
    arrived = exchange(outgoing_sums, return_route, Z_LANES)
    placement = (blocks[:, None] == out_keep.reshape(1, peers * keep)).astype(jnp.bfloat16)
    summed = jnp.stack(
        [
            jnp.dot(
                placement,
                arrived[:, :, r * BLK : (r + 1) * BLK].reshape(peers * keep, BLK),
                preferred_element_type=jnp.float32,
            )
            for r in range(rows)
        ],
        axis=0,
    )
    ffn_share = summed.reshape(rows, -1)
    return (middle + ffn_share).astype(jnp.bfloat16)


def solution(mesh):
    placed = (
        P("wide", "head"),
        P("wide", "head"),
        P("wide", "head"),
        P(None, "wide", None, "head"),
        P("wide", None),
        P("wide"),
        P("wide"),
        P(("wide", "head"), None),
        P(),
        P("wide", None, None, None),
        P("wide", None, None, None),
        P("wide", None),
        P("wide", None),
        P("wide", None),
        P("wide", None, None, None),
        P("wide", None),
        P("wide", None),
    )
    return jax.shard_map(
        per_device, mesh=mesh, in_specs=placed, out_specs=P(("wide", "head"), None), check_vma=False
    )
```

```python
import functools
import math

import jax
import jax.numpy as jnp
from jax import lax
from jax.experimental import pallas as pl
from jax.experimental.pallas import tpu as pltpu
from jax.sharding import PartitionSpec as P

HD = 128
BLK = 128
Z_LANES = 4


def copy_head(source_z, target_lane, source_core, lanes):
    offset = (source_z - target_lane + 2 * lanes) % (2 * lanes)
    upper = ((offset + 1) % (2 * lanes)) // lanes
    tie = ((offset % lanes) // 2) * (1 - (offset % lanes) % 2)
    return upper + tie * source_core * (1 - 2 * upper)


def gather_route(me, here, peer, lanes):
    source_z = (me // 2) % lanes + lanes * here
    return copy_head(source_z, (peer // 2) % lanes, me % 2, lanes)


def return_route(me, here, peer, lanes):
    first = copy_head((peer // 2) % lanes, (me // 2) % lanes, peer % 2, lanes)
    return (first + here) % 2


def exchange_kernel(route, lanes, x_ref, y_ref, send_sem, recv_sem, local_sem):
    me = lax.axis_index("wide")
    here = lax.axis_index("head")
    n = x_ref.shape[0]
    ways = send_sem.shape[0]
    local = pltpu.make_async_copy(x_ref.at[me], y_ref.at[me], local_sem)
    local.start()
    for way in range(ways):

        def send(step, carry, way=way):
            turn = step * ways + way
            hop = (turn % 2) * ((turn + 1) // 2) + (1 - turn % 2) * (n - turn // 2)
            peer = lax.rem(me + hop, n)
            pltpu.make_async_remote_copy(
                src_ref=x_ref.at[peer],
                dst_ref=y_ref.at[me],
                send_sem=send_sem.at[way],
                recv_sem=recv_sem.at[way],
                device_id=(peer, route(me, here, peer, lanes)),
                device_id_type=pl.DeviceIdType.MESH,
            ).start()
            return carry

        lax.fori_loop(1 if way == 0 else 0, (n - way + ways - 1) // ways, send, 0)
    for way in range(ways):
        count = (n - way + ways - 1) // ways - (1 if way == 0 else 0)
        every = pltpu.make_async_remote_copy(
            src_ref=x_ref.at[pl.ds(0, count)],
            dst_ref=y_ref.at[pl.ds(0, count)],
            send_sem=send_sem.at[way],
            recv_sem=recv_sem.at[way],
            device_id=(me, here),
            device_id_type=pl.DeviceIdType.MESH,
        )
        every.wait_send()
        every.wait_recv()
    local.wait()


def exchange(x, route, lanes, ways=8):
    return pl.pallas_call(
        functools.partial(exchange_kernel, route, lanes),
        out_shape=jax.ShapeDtypeStruct(x.shape, x.dtype),
        in_specs=[pl.BlockSpec(memory_space=pl.ANY)],
        out_specs=pl.BlockSpec(memory_space=pl.ANY),
        scratch_shapes=[
            pltpu.SemaphoreType.DMA((ways,)),
            pltpu.SemaphoreType.DMA((ways,)),
            pltpu.SemaphoreType.DMA,
        ],
        compiler_params=pltpu.CompilerParams(has_side_effects=True),
    )(x)


def shifted(block, axis, distance):
    devices = range(lax.axis_size(axis))
    route = [(i - distance, i) for i in devices if i - distance in devices]
    return lax.ppermute(block, axis, route)


def attend(branch_query, key_new, value_new, pools, tables, lengths, source, row):
    row_count = branch_query.shape[0]
    groups = key_new.shape[1] // HD
    per_group = branch_query.shape[1] // (groups * HD)
    pages, page_size = pools[0].shape[1], pools[0].shape[2]
    queries = branch_query.reshape(row_count, groups, per_group, HD)
    own_keys = key_new.reshape(row_count, groups, HD)
    own_values = value_new.reshape(row_count, groups, HD)
    factor = 1.0 / math.sqrt(HD)
    page_ids = jnp.arange(pages, dtype=jnp.int32)
    slots = jnp.arange(tables[0].shape[1], dtype=jnp.int32)
    offsets = jnp.arange(page_size, dtype=jnp.int32)
    scores, masks = [], []
    for which, (pool, table, length) in enumerate(zip(pools, tables, lengths)):
        parent_table = table[row]
        match = parent_table[:, None, :] == page_ids[None, :, None]
        slot = jnp.sum(jnp.where(match, slots[None, None, :], 0), axis=-1)
        found = jnp.any(match, axis=-1) & (source == which)[:, None]
        live = found[:, :, None] & (
            slot[:, :, None] * page_size + offsets[None, None, :] < length[row][:, None, None]
        )
        keys = pool[0].reshape(pages * page_size, groups * HD)
        part = jnp.stack(
            [
                jnp.einsum(
                    "rjd,td->rjt",
                    queries[:, g],
                    keys[:, g * HD : (g + 1) * HD],
                    preferred_element_type=jnp.float32,
                )
                for g in range(groups)
            ],
            axis=1,
        ) * factor
        scores.append(part)
        masks.append(live.reshape(row_count, 1, 1, pages * page_size))
    tail_scores = jnp.concatenate(scores, axis=-1)
    live_mask = jnp.concatenate(masks, axis=-1)
    own_scores = (
        jnp.einsum("rgjd,rgd->rgj", queries, own_keys, preferred_element_type=jnp.float32) * factor
    )
    top_score = jnp.maximum(jnp.max(jnp.where(live_mask, tail_scores, -1e30), axis=-1), own_scores)
    tail_exp = jnp.where(live_mask, jnp.exp(tail_scores - top_score[..., None]), 0.0)
    own_exp = jnp.exp(own_scores - top_score)
    totals = jnp.sum(tail_exp, axis=-1) + own_exp
    tail_weights = (tail_exp / totals[..., None]).astype(jnp.bfloat16)
    own_weights = (own_exp / totals).astype(jnp.bfloat16)
    span = pages * page_size
    mixture = own_weights[..., None].astype(jnp.float32) * own_values[:, :, None, :].astype(
        jnp.float32
    )
    for which, pool in enumerate(pools):
        values = pool[1].reshape(span, groups * HD)
        weights = tail_weights[..., which * span : (which + 1) * span]
        mixture = mixture + jnp.stack(
            [
                jnp.einsum(
                    "rjt,td->rjd",
                    weights[:, g],
                    values[:, g * HD : (g + 1) * HD],
                    preferred_element_type=jnp.float32,
                )
                for g in range(groups)
            ],
            axis=1,
        )
    return mixture.reshape(row_count, -1).astype(jnp.bfloat16)


def hidden_units(picked, gate_blocks, up_blocks, gate_scale, up_scale):
    gate_part = jnp.einsum(
        "skd,kdf->ksf", picked, gate_blocks[0], preferred_element_type=jnp.float32
    )
    up_part = jnp.einsum("skd,kdf->ksf", picked, up_blocks[0], preferred_element_type=jnp.float32)
    gate_sum = jnp.sum(gate_part * gate_scale[0][:, None, None], axis=0)
    up_sum = jnp.sum(up_part * up_scale[0][:, None, None], axis=0)
    return (jax.nn.silu(gate_sum) * up_sum).astype(jnp.bfloat16)


def per_device(
    branch_query,
    key_new,
    value_new,
    pool_pages,
    page_table,
    tail_length,
    parent_row,
    residual,
    norm_gain,
    gate_blocks,
    up_blocks,
    gate_up_keep,
    gate_scale,
    up_scale,
    down_blocks,
    down_keep,
    down_scale,
):
    row_count = branch_query.shape[0]
    prior_pool, prior_meta = shifted(
        (pool_pages, jnp.concatenate([page_table, tail_length[:, None]], axis=1)), "wide", 1
    )
    prior = (prior_pool, prior_meta[:, :-1], prior_meta[:, -1])
    local_parent = parent_row - (lax.axis_index("wide") - 1) * row_count
    attention = attend(
        branch_query,
        key_new,
        value_new,
        (prior[0], pool_pages),
        (prior[1], page_table),
        (prior[2], tail_length),
        local_parent // row_count,
        local_parent % row_count,
    )
    half = residual.shape[0]
    here = lax.axis_index("head")
    mine = lax.dynamic_slice_in_dim(attention, here * half, half, axis=0)
    theirs = lax.dynamic_slice_in_dim(attention, (1 - here) * half, half, axis=0)
    arrived_half = lax.ppermute(theirs, "head", [(0, 1), (1, 0)])
    head_rows = jnp.where(
        here == 0,
        jnp.concatenate([mine, arrived_half], axis=1),
        jnp.concatenate([arrived_half, mine], axis=1),
    )
    middle = residual.astype(jnp.float32) + head_rows.astype(jnp.float32)
    normed = (
        middle * lax.rsqrt(jnp.mean(middle * middle, axis=-1, keepdims=True) + 1e-05) * norm_gain
    ).astype(jnp.bfloat16)
    peers = lax.axis_size("wide")
    own_lists = jnp.concatenate([gate_up_keep, down_keep], axis=1)
    keep_lists = lax.all_to_all(
        jnp.broadcast_to(own_lists, (peers, own_lists.shape[1])),
        "wide",
        split_axis=0,
        concat_axis=0,
        tiled=True,
    )
    keep = gate_up_keep.shape[1]
    in_keep, out_keep = keep_lists[:, :keep], keep_lists[:, keep:]
    feature_blocks = normed.shape[1] // BLK
    rows = normed.shape[0]
    blocks = jnp.arange(feature_blocks, dtype=jnp.int32)
    choose = (in_keep.reshape(peers * keep, 1) == blocks[None, :]).astype(jnp.bfloat16)
    by_block = jnp.swapaxes(normed.reshape(rows, feature_blocks, BLK), 0, 1)
    outgoing = jnp.dot(
        choose, by_block.reshape(feature_blocks, rows * BLK), preferred_element_type=jnp.float32
    ).astype(jnp.bfloat16)
    picked = exchange(outgoing.reshape(peers, keep, rows * BLK), gather_route, Z_LANES)
    hidden = jnp.concatenate(
        [
            hidden_units(
                picked[:, :, r * BLK : (r + 1) * BLK], gate_blocks, up_blocks, gate_scale, up_scale
            )
            for r in range(rows)
        ],
        axis=0,
    )
    down_flat = jnp.swapaxes(down_blocks[0], 0, 1).reshape(BLK, keep * BLK)
    down_part = jnp.dot(hidden, down_flat, preferred_element_type=jnp.float32)
    column_scale = jnp.repeat(down_scale[0], BLK)
    contrib = lax.optimization_barrier((down_part * column_scale[None, :]).astype(jnp.bfloat16))
    contrib = contrib.reshape(rows, peers, keep, BLK)
    outgoing_sums = jnp.concatenate([contrib[r] for r in range(rows)], axis=-1)
    arrived = exchange(outgoing_sums, return_route, Z_LANES)
    placement = (blocks[:, None] == out_keep.reshape(1, peers * keep)).astype(jnp.bfloat16)
    summed = jnp.stack(
        [
            jnp.dot(
                placement,
                arrived[:, :, r * BLK : (r + 1) * BLK].reshape(peers * keep, BLK),
                preferred_element_type=jnp.float32,
            )
            for r in range(rows)
        ],
        axis=0,
    )
    ffn_share = summed.reshape(rows, -1)
    return (middle + ffn_share).astype(jnp.bfloat16)


def solution(mesh):
    placed = (
        P("wide", "head"),
        P("wide", "head"),
        P("wide", "head"),
        P(None, "wide", None, "head"),
        P("wide", None),
        P("wide"),
        P("wide"),
        P(("wide", "head"), None),
        P(),
        P("wide", None, None, None),
        P("wide", None, None, None),
        P("wide", None),
        P("wide", None),
        P("wide", None),
        P("wide", None, None, None),
        P("wide", None),
        P("wide", None),
    )
    return jax.shard_map(
        per_device, mesh=mesh, in_specs=placed, out_specs=P(("wide", "head"), None), check_vma=False
    )
```

```python
import functools
import math

import jax
import jax.numpy as jnp
from jax import lax
from jax.experimental import pallas as pl
from jax.experimental.pallas import tpu as pltpu
from jax.sharding import PartitionSpec as P

HD = 128
BLK = 128
Z_LANES = 4


def copy_head(source_z, target_lane, source_core, lanes):
    offset = (source_z - target_lane + 2 * lanes) % (2 * lanes)
    upper = ((offset + 1) % (2 * lanes)) // lanes
    tie = ((offset % lanes) // 2) * (1 - (offset % lanes) % 2)
    return upper + tie * source_core * (1 - 2 * upper)


def gather_route(me, here, peer, lanes):
    source_z = (me // 2) % lanes + lanes * here
    return copy_head(source_z, (peer // 2) % lanes, me % 2, lanes)


def return_route(me, here, peer, lanes):
    first = copy_head((peer // 2) % lanes, (me // 2) % lanes, peer % 2, lanes)
    return (first + here) % 2


def exchange_kernel(route, lanes, x_ref, y_ref, send_sem, recv_sem, local_sem):
    me = lax.axis_index("wide")
    here = lax.axis_index("head")
    n = x_ref.shape[0]
    ways = send_sem.shape[0]
    local = pltpu.make_async_copy(x_ref.at[me], y_ref.at[me], local_sem)
    local.start()
    for way in range(ways):

        def send(step, carry, way=way):
            turn = step * ways + way
            hop = (turn % 2) * ((turn + 1) // 2) + (1 - turn % 2) * (n - turn // 2)
            peer = lax.rem(me + hop, n)
            pltpu.make_async_remote_copy(
                src_ref=x_ref.at[peer],
                dst_ref=y_ref.at[me],
                send_sem=send_sem.at[way],
                recv_sem=recv_sem.at[way],
                device_id=(peer, route(me, here, peer, lanes)),
                device_id_type=pl.DeviceIdType.MESH,
            ).start()
            return carry

        lax.fori_loop(1 if way == 0 else 0, (n - way + ways - 1) // ways, send, 0)
    for way in range(ways):
        count = (n - way + ways - 1) // ways - (1 if way == 0 else 0)
        every = pltpu.make_async_remote_copy(
            src_ref=x_ref.at[pl.ds(0, count)],
            dst_ref=y_ref.at[pl.ds(0, count)],
            send_sem=send_sem.at[way],
            recv_sem=recv_sem.at[way],
            device_id=(me, here),
            device_id_type=pl.DeviceIdType.MESH,
        )
        every.wait_send()
        every.wait_recv()
    local.wait()


def exchange(x, route, lanes, ways=16):
    return pl.pallas_call(
        functools.partial(exchange_kernel, route, lanes),
        out_shape=jax.ShapeDtypeStruct(x.shape, x.dtype),
        in_specs=[pl.BlockSpec(memory_space=pl.ANY)],
        out_specs=pl.BlockSpec(memory_space=pl.ANY),
        scratch_shapes=[
            pltpu.SemaphoreType.DMA((ways,)),
            pltpu.SemaphoreType.DMA((ways,)),
            pltpu.SemaphoreType.DMA,
        ],
        compiler_params=pltpu.CompilerParams(has_side_effects=True),
    )(x)


def shifted(block, axis, distance):
    devices = range(lax.axis_size(axis))
    route = [(i - distance, i) for i in devices if i - distance in devices]
    return lax.ppermute(block, axis, route)


def attend(branch_query, key_new, value_new, pools, tables, lengths, source, row):
    row_count = branch_query.shape[0]
    groups = key_new.shape[1] // HD
    per_group = branch_query.shape[1] // (groups * HD)
    pages, page_size = pools[0].shape[1], pools[0].shape[2]
    queries = branch_query.reshape(row_count, groups, per_group, HD)
    own_keys = key_new.reshape(row_count, groups, HD)
    own_values = value_new.reshape(row_count, groups, HD)
    factor = 1.0 / math.sqrt(HD)
    page_ids = jnp.arange(pages, dtype=jnp.int32)
    slots = jnp.arange(tables[0].shape[1], dtype=jnp.int32)
    offsets = jnp.arange(page_size, dtype=jnp.int32)
    scores, masks = [], []
    for which, (pool, table, length) in enumerate(zip(pools, tables, lengths)):
        parent_table = table[row]
        match = parent_table[:, None, :] == page_ids[None, :, None]
        slot = jnp.sum(jnp.where(match, slots[None, None, :], 0), axis=-1)
        found = jnp.any(match, axis=-1) & (source == which)[:, None]
        live = found[:, :, None] & (
            slot[:, :, None] * page_size + offsets[None, None, :] < length[row][:, None, None]
        )
        keys = pool[0].reshape(pages * page_size, groups * HD)
        part = jnp.stack(
            [
                jnp.einsum(
                    "rjd,td->rjt",
                    queries[:, g],
                    keys[:, g * HD : (g + 1) * HD],
                    preferred_element_type=jnp.float32,
                )
                for g in range(groups)
            ],
            axis=1,
        ) * factor
        scores.append(part)
        masks.append(live.reshape(row_count, 1, 1, pages * page_size))
    tail_scores = jnp.concatenate(scores, axis=-1)
    live_mask = jnp.concatenate(masks, axis=-1)
    own_scores = (
        jnp.einsum("rgjd,rgd->rgj", queries, own_keys, preferred_element_type=jnp.float32) * factor
    )
    top_score = jnp.maximum(jnp.max(jnp.where(live_mask, tail_scores, -1e30), axis=-1), own_scores)
    tail_exp = jnp.where(live_mask, jnp.exp(tail_scores - top_score[..., None]), 0.0)
    own_exp = jnp.exp(own_scores - top_score)
    totals = jnp.sum(tail_exp, axis=-1) + own_exp
    tail_weights = (tail_exp / totals[..., None]).astype(jnp.bfloat16)
    own_weights = (own_exp / totals).astype(jnp.bfloat16)
    span = pages * page_size
    mixture = own_weights[..., None].astype(jnp.float32) * own_values[:, :, None, :].astype(
        jnp.float32
    )
    for which, pool in enumerate(pools):
        values = pool[1].reshape(span, groups * HD)
        weights = tail_weights[..., which * span : (which + 1) * span]
        mixture = mixture + jnp.stack(
            [
                jnp.einsum(
                    "rjt,td->rjd",
                    weights[:, g],
                    values[:, g * HD : (g + 1) * HD],
                    preferred_element_type=jnp.float32,
                )
                for g in range(groups)
            ],
            axis=1,
        )
    return mixture.reshape(row_count, -1).astype(jnp.bfloat16)


def hidden_units(picked, gate_blocks, up_blocks, gate_scale, up_scale):
    gate_part = jnp.einsum(
        "skd,kdf->ksf", picked, gate_blocks[0], preferred_element_type=jnp.float32
    )
    up_part = jnp.einsum("skd,kdf->ksf", picked, up_blocks[0], preferred_element_type=jnp.float32)
    gate_sum = jnp.sum(gate_part * gate_scale[0][:, None, None], axis=0)
    up_sum = jnp.sum(up_part * up_scale[0][:, None, None], axis=0)
    return (jax.nn.silu(gate_sum) * up_sum).astype(jnp.bfloat16)


def per_device(
    branch_query,
    key_new,
    value_new,
    pool_pages,
    page_table,
    tail_length,
    parent_row,
    residual,
    norm_gain,
    gate_blocks,
    up_blocks,
    gate_up_keep,
    gate_scale,
    up_scale,
    down_blocks,
    down_keep,
    down_scale,
):
    row_count = branch_query.shape[0]
    prior_pool, prior_meta = shifted(
        (pool_pages, jnp.concatenate([page_table, tail_length[:, None]], axis=1)), "wide", 1
    )
    prior = (prior_pool, prior_meta[:, :-1], prior_meta[:, -1])
    local_parent = parent_row - (lax.axis_index("wide") - 1) * row_count
    attention = attend(
        branch_query,
        key_new,
        value_new,
        (prior[0], pool_pages),
        (prior[1], page_table),
        (prior[2], tail_length),
        local_parent // row_count,
        local_parent % row_count,
    )
    half = residual.shape[0]
    here = lax.axis_index("head")
    mine = lax.dynamic_slice_in_dim(attention, here * half, half, axis=0)
    theirs = lax.dynamic_slice_in_dim(attention, (1 - here) * half, half, axis=0)
    arrived_half = lax.ppermute(theirs, "head", [(0, 1), (1, 0)])
    head_rows = jnp.where(
        here == 0,
        jnp.concatenate([mine, arrived_half], axis=1),
        jnp.concatenate([arrived_half, mine], axis=1),
    )
    middle = residual.astype(jnp.float32) + head_rows.astype(jnp.float32)
    normed = (
        middle * lax.rsqrt(jnp.mean(middle * middle, axis=-1, keepdims=True) + 1e-05) * norm_gain
    ).astype(jnp.bfloat16)
    peers = lax.axis_size("wide")
    own_lists = jnp.concatenate([gate_up_keep, down_keep], axis=1)
    keep_lists = lax.all_to_all(
        jnp.broadcast_to(own_lists, (peers, own_lists.shape[1])),
        "wide",
        split_axis=0,
        concat_axis=0,
        tiled=True,
    )
    keep = gate_up_keep.shape[1]
    in_keep, out_keep = keep_lists[:, :keep], keep_lists[:, keep:]
    feature_blocks = normed.shape[1] // BLK
    rows = normed.shape[0]
    blocks = jnp.arange(feature_blocks, dtype=jnp.int32)
    choose = (in_keep.reshape(peers * keep, 1) == blocks[None, :]).astype(jnp.bfloat16)
    by_block = jnp.swapaxes(normed.reshape(rows, feature_blocks, BLK), 0, 1)
    outgoing = jnp.dot(
        choose, by_block.reshape(feature_blocks, rows * BLK), preferred_element_type=jnp.float32
    ).astype(jnp.bfloat16)
    picked = exchange(outgoing.reshape(peers, keep, rows * BLK), gather_route, Z_LANES)
    hidden = jnp.concatenate(
        [
            hidden_units(
                picked[:, :, r * BLK : (r + 1) * BLK], gate_blocks, up_blocks, gate_scale, up_scale
            )
            for r in range(rows)
        ],
        axis=0,
    )
    down_flat = jnp.swapaxes(down_blocks[0], 0, 1).reshape(BLK, keep * BLK)
    down_part = jnp.dot(hidden, down_flat, preferred_element_type=jnp.float32)
    column_scale = jnp.repeat(down_scale[0], BLK)
    contrib = lax.optimization_barrier((down_part * column_scale[None, :]).astype(jnp.bfloat16))
    contrib = contrib.reshape(rows, peers, keep, BLK)
    outgoing_sums = jnp.concatenate([contrib[r] for r in range(rows)], axis=-1)
    arrived = exchange(outgoing_sums, return_route, Z_LANES)
    placement = (blocks[:, None] == out_keep.reshape(1, peers * keep)).astype(jnp.bfloat16)
    summed = jnp.stack(
        [
            jnp.dot(
                placement,
                arrived[:, :, r * BLK : (r + 1) * BLK].reshape(peers * keep, BLK),
                preferred_element_type=jnp.float32,
            )
            for r in range(rows)
        ],
        axis=0,
    )
    ffn_share = summed.reshape(rows, -1)
    return (middle + ffn_share).astype(jnp.bfloat16)


def solution(mesh):
    placed = (
        P("wide", "head"),
        P("wide", "head"),
        P("wide", "head"),
        P(None, "wide", None, "head"),
        P("wide", None),
        P("wide"),
        P("wide"),
        P(("wide", "head"), None),
        P(),
        P("wide", None, None, None),
        P("wide", None, None, None),
        P("wide", None),
        P("wide", None),
        P("wide", None),
        P("wide", None, None, None),
        P("wide", None),
        P("wide", None),
    )
    return jax.shard_map(
        per_device, mesh=mesh, in_specs=placed, out_specs=P(("wide", "head"), None), check_vma=False
    )
```

```python
import functools
import math

import jax
import jax.numpy as jnp
from jax import lax
from jax.experimental import pallas as pl
from jax.experimental.pallas import tpu as pltpu
from jax.sharding import PartitionSpec as P

HD = 128
BLK = 128
Z_LANES = 4


def copy_head(source_z, target_lane, source_core, lanes):
    offset = (source_z - target_lane + 2 * lanes) % (2 * lanes)
    upper = ((offset + 1) % (2 * lanes)) // lanes
    tie = ((offset % lanes) // 2) * (1 - (offset % lanes) % 2)
    return upper + tie * source_core * (1 - 2 * upper)


def gather_route(me, here, peer, lanes):
    source_z = (me // 2) % lanes + lanes * here
    return copy_head(source_z, (peer // 2) % lanes, me % 2, lanes)


def return_route(me, here, peer, lanes):
    first = copy_head((peer // 2) % lanes, (me // 2) % lanes, peer % 2, lanes)
    return (first + here) % 2


def exchange_kernel(route, lanes, x_ref, y_ref, send_sem, recv_sem, local_sem):
    me = lax.axis_index("wide")
    here = lax.axis_index("head")
    n = x_ref.shape[0]
    ways = send_sem.shape[0]
    local = pltpu.make_async_copy(x_ref.at[me], y_ref.at[me], local_sem)
    local.start()
    for way in range(ways):

        def send(step, carry, way=way):
            turn = step * ways + way
            hop = (turn % 2) * ((turn + 1) // 2) + (1 - turn % 2) * (n - turn // 2)
            peer = lax.rem(me + hop, n)
            pltpu.make_async_remote_copy(
                src_ref=x_ref.at[peer],
                dst_ref=y_ref.at[me],
                send_sem=send_sem.at[way],
                recv_sem=recv_sem.at[way],
                device_id=(peer, route(me, here, peer, lanes)),
                device_id_type=pl.DeviceIdType.MESH,
            ).start()
            return carry

        lax.fori_loop(1 if way == 0 else 0, (n - way + ways - 1) // ways, send, 0)
    for way in range(ways):
        count = (n - way + ways - 1) // ways - (1 if way == 0 else 0)
        every = pltpu.make_async_remote_copy(
            src_ref=x_ref.at[pl.ds(0, count)],
            dst_ref=y_ref.at[pl.ds(0, count)],
            send_sem=send_sem.at[way],
            recv_sem=recv_sem.at[way],
            device_id=(me, here),
            device_id_type=pl.DeviceIdType.MESH,
        )
        every.wait_send()
        every.wait_recv()
    local.wait()


def exchange(x, route, lanes, ways=8):
    return pl.pallas_call(
        functools.partial(exchange_kernel, route, lanes),
        out_shape=jax.ShapeDtypeStruct(x.shape, x.dtype),
        in_specs=[pl.BlockSpec(memory_space=pl.ANY)],
        out_specs=pl.BlockSpec(memory_space=pl.ANY),
        scratch_shapes=[
            pltpu.SemaphoreType.DMA((ways,)),
            pltpu.SemaphoreType.DMA((ways,)),
            pltpu.SemaphoreType.DMA,
        ],
        compiler_params=pltpu.CompilerParams(has_side_effects=True),
    )(x)


def shifted(block, axis, distance):
    devices = range(lax.axis_size(axis))
    route = [(i - distance, i) for i in devices if i - distance in devices]
    return lax.ppermute(block, axis, route)


def attend(branch_query, key_new, value_new, pools, tables, lengths, source, row):
    row_count = branch_query.shape[0]
    groups = key_new.shape[1] // HD
    per_group = branch_query.shape[1] // (groups * HD)
    pages, page_size = pools[0].shape[1], pools[0].shape[2]
    queries = branch_query.reshape(row_count, groups, per_group, HD)
    own_keys = key_new.reshape(row_count, groups, HD)
    own_values = value_new.reshape(row_count, groups, HD)
    factor = 1.0 / math.sqrt(HD)
    page_ids = jnp.arange(pages, dtype=jnp.int32)
    slots = jnp.arange(tables[0].shape[1], dtype=jnp.int32)
    offsets = jnp.arange(page_size, dtype=jnp.int32)
    scores, masks = [], []
    for which, (pool, table, length) in enumerate(zip(pools, tables, lengths)):
        parent_table = table[row]
        match = parent_table[:, None, :] == page_ids[None, :, None]
        slot = jnp.sum(jnp.where(match, slots[None, None, :], 0), axis=-1)
        found = jnp.any(match, axis=-1) & (source == which)[:, None]
        live = found[:, :, None] & (
            slot[:, :, None] * page_size + offsets[None, None, :] < length[row][:, None, None]
        )
        keys = pool[0].reshape(pages * page_size, groups * HD)
        part = jnp.stack(
            [
                jnp.einsum(
                    "rjd,td->rjt",
                    queries[:, g],
                    keys[:, g * HD : (g + 1) * HD],
                    preferred_element_type=jnp.float32,
                )
                for g in range(groups)
            ],
            axis=1,
        ) * factor
        scores.append(part)
        masks.append(live.reshape(row_count, 1, 1, pages * page_size))
    tail_scores = jnp.concatenate(scores, axis=-1)
    live_mask = jnp.concatenate(masks, axis=-1)
    own_scores = (
        jnp.einsum("rgjd,rgd->rgj", queries, own_keys, preferred_element_type=jnp.float32) * factor
    )
    top_score = jnp.maximum(jnp.max(jnp.where(live_mask, tail_scores, -1e30), axis=-1), own_scores)
    tail_exp = jnp.where(live_mask, jnp.exp(tail_scores - top_score[..., None]), 0.0)
    own_exp = jnp.exp(own_scores - top_score)
    totals = jnp.sum(tail_exp, axis=-1) + own_exp
    tail_weights = (tail_exp / totals[..., None]).astype(jnp.bfloat16)
    own_weights = (own_exp / totals).astype(jnp.bfloat16)
    span = pages * page_size
    mixture = own_weights[..., None].astype(jnp.float32) * own_values[:, :, None, :].astype(
        jnp.float32
    )
    for which, pool in enumerate(pools):
        values = pool[1].reshape(span, groups * HD)
        weights = tail_weights[..., which * span : (which + 1) * span]
        mixture = mixture + jnp.stack(
            [
                jnp.einsum(
                    "rjt,td->rjd",
                    weights[:, g],
                    values[:, g * HD : (g + 1) * HD],
                    preferred_element_type=jnp.float32,
                )
                for g in range(groups)
            ],
            axis=1,
        )
    return mixture.reshape(row_count, -1).astype(jnp.bfloat16)


def hidden_units(picked, gate_blocks, up_blocks, gate_scale, up_scale):
    gate_part = jnp.einsum(
        "skd,kdf->ksf", picked, gate_blocks[0], preferred_element_type=jnp.float32
    )
    up_part = jnp.einsum("skd,kdf->ksf", picked, up_blocks[0], preferred_element_type=jnp.float32)
    gate_sum = jnp.sum(gate_part * gate_scale[0][:, None, None], axis=0)
    up_sum = jnp.sum(up_part * up_scale[0][:, None, None], axis=0)
    return (jax.nn.silu(gate_sum) * up_sum).astype(jnp.bfloat16)


def per_device(
    branch_query,
    key_new,
    value_new,
    pool_pages,
    page_table,
    tail_length,
    parent_row,
    residual,
    norm_gain,
    gate_blocks,
    up_blocks,
    gate_up_keep,
    gate_scale,
    up_scale,
    down_blocks,
    down_keep,
    down_scale,
):
    row_count = branch_query.shape[0]
    prior_pool, prior_meta = shifted(
        (pool_pages, jnp.concatenate([page_table, tail_length[:, None]], axis=1)), "wide", 1
    )
    prior = (prior_pool, prior_meta[:, :-1], prior_meta[:, -1])
    local_parent = parent_row - (lax.axis_index("wide") - 1) * row_count
    attention = attend(
        branch_query,
        key_new,
        value_new,
        (prior[0], pool_pages),
        (prior[1], page_table),
        (prior[2], tail_length),
        local_parent // row_count,
        local_parent % row_count,
    )
    half = residual.shape[0]
    here = lax.axis_index("head")
    mine = lax.dynamic_slice_in_dim(attention, here * half, half, axis=0)
    theirs = lax.dynamic_slice_in_dim(attention, (1 - here) * half, half, axis=0)
    arrived_half = lax.ppermute(theirs, "head", [(0, 1), (1, 0)])
    head_rows = jnp.where(
        here == 0,
        jnp.concatenate([mine, arrived_half], axis=1),
        jnp.concatenate([arrived_half, mine], axis=1),
    )
    middle = residual.astype(jnp.float32) + head_rows.astype(jnp.float32)
    normed = (
        middle * lax.rsqrt(jnp.mean(middle * middle, axis=-1, keepdims=True) + 1e-05) * norm_gain
    ).astype(jnp.bfloat16)
    peers = lax.axis_size("wide")
    own_lists = jnp.concatenate([gate_up_keep, down_keep], axis=1)
    keep_lists = lax.all_to_all(
        jnp.broadcast_to(own_lists, (peers, own_lists.shape[1])),
        "wide",
        split_axis=0,
        concat_axis=0,
        tiled=True,
    )
    keep = gate_up_keep.shape[1]
    in_keep, out_keep = keep_lists[:, :keep], keep_lists[:, keep:]
    feature_blocks = normed.shape[1] // BLK
    rows = normed.shape[0]
    blocks = jnp.arange(feature_blocks, dtype=jnp.int32)
    choose = (in_keep.reshape(peers * keep, 1) == blocks[None, :]).astype(jnp.bfloat16)
    normed_blocks = normed.reshape(rows, feature_blocks, BLK)
    outgoing = jnp.stack(
        [
            jnp.dot(choose, normed_blocks[r], preferred_element_type=jnp.float32)
            .astype(jnp.bfloat16)
            .reshape(peers, keep, BLK)
            for r in range(rows)
        ],
        axis=1,
    ).reshape(peers, rows * keep, BLK)
    picked = exchange(outgoing, gather_route, Z_LANES)
    hidden = hidden_units(
        picked.reshape(peers * rows, keep, BLK), gate_blocks, up_blocks, gate_scale, up_scale
    )
    hidden = jnp.swapaxes(hidden.reshape(peers, rows, BLK), 0, 1).reshape(peers * rows, BLK)
    down_flat = jnp.swapaxes(down_blocks[0], 0, 1).reshape(BLK, keep * BLK)
    down_part = jnp.dot(hidden, down_flat, preferred_element_type=jnp.float32)
    column_scale = jnp.repeat(down_scale[0], BLK)
    contrib = lax.optimization_barrier((down_part * column_scale[None, :]).astype(jnp.bfloat16))
    contrib = contrib.reshape(rows, peers, keep, BLK)
    outgoing_sums = jnp.concatenate([contrib[r] for r in range(rows)], axis=-1)
    arrived = exchange(outgoing_sums, return_route, Z_LANES)
    placement = (blocks[:, None] == out_keep.reshape(1, peers * keep)).astype(jnp.bfloat16)
    summed = jnp.stack(
        [
            jnp.dot(
                placement,
                arrived[:, :, r * BLK : (r + 1) * BLK].reshape(peers * keep, BLK),
                preferred_element_type=jnp.float32,
            )
            for r in range(rows)
        ],
        axis=0,
    )
    ffn_share = summed.reshape(rows, -1)
    return (middle + ffn_share).astype(jnp.bfloat16)


def solution(mesh):
    placed = (
        P("wide", "head"),
        P("wide", "head"),
        P("wide", "head"),
        P(None, "wide", None, "head"),
        P("wide", None),
        P("wide"),
        P("wide"),
        P(("wide", "head"), None),
        P(),
        P("wide", None, None, None),
        P("wide", None, None, None),
        P("wide", None),
        P("wide", None),
        P("wide", None),
        P("wide", None, None, None),
        P("wide", None),
        P("wide", None),
    )
    return jax.shard_map(
        per_device, mesh=mesh, in_specs=placed, out_specs=P(("wide", "head"), None), check_vma=False
    )
```
